32 devices in a mesh: ctx: 8 (over y, x, core), fsdp: 4 (over z).
Axes of the slice: x: 2, y: 2, z: 4, core: 2. Of those that a mesh axis runs over, the one named last changes fastest.
Arguments:
- hidden_in: bfloat16 [8192, 1024], P(('fsdp', 'ctx')), may hold values from -6 to 6
- seq_ids: int32 [4, 2048], P('fsdp'), may hold values from 0 to 1, never falling along the last dimension, each value on 1 to 1536 neighbouring positions
- ln1_gain: bfloat16 [1024], P('fsdp'), may hold values from 0.5 to 1.5
- ln1_bias: bfloat16 [1024], P('fsdp'), may hold values from -3 to 3
- w_qkv: bfloat16 [1024, 3072], P('fsdp'), may hold values from -0.1875 to 0.1875
- b_qv: bfloat16 [2048], P('fsdp'), may hold values from -3 to 3
- w_dense: bfloat16 [1024, 1024], P('fsdp'), may hold values from -0.75 to 0.75
- b_dense: bfloat16 [1024], P('fsdp'), may hold values from -5 to 5
- ln2_gain: bfloat16 [1024], P('fsdp'), may hold values from 0.099609375 to 1.8984375
- ln2_bias: bfloat16 [1024], P('fsdp'), may hold values from -3 to 3
- w_up: bfloat16 [1024, 4096], P('fsdp'), may hold values from -0.1875 to 0.1875
- b_up: bfloat16 [4096], P('fsdp'), may hold values from -4 to 4
- w_down: bfloat16 [4096, 1024], P('fsdp'), may hold values from -0.09375 to 0.09375
- b_down: bfloat16 [1024], P('fsdp'), may hold values from -5 to 5
- cotangent: bfloat16 [8192, 1024], P(('fsdp', 'ctx')), may hold values from -6 to 6
Outputs:
- block_out: float32 [8192, 1024], P(('fsdp', 'ctx'))
- grad_input: float32 [8192, 1024], P(('fsdp', 'ctx'))
- grad_ln1_gain: float32 [1024], P('fsdp')
- grad_ln1_bias: float32 [1024], P('fsdp')
- grad_w_qkv: float32 [1024, 3072], P('fsdp')
- grad_b_qv: float32 [2048], P('fsdp')
- grad_w_dense: float32 [1024, 1024], P('fsdp')
- grad_b_dense: float32 [1024], P('fsdp')
- grad_ln2_gain: float32 [1024], P('fsdp')
- grad_ln2_bias: float32 [1024], P('fsdp')
- grad_w_up: float32 [1024, 4096], P('fsdp')
- grad_b_up: float32 [4096], P('fsdp')
- grad_w_down: float32 [4096, 1024], P('fsdp')
- grad_b_down: float32 [1024], P('fsdp')
The draws below stay inside these ranges and needn't reach their ends.
Inputs may be any that keep to these rules, and one draw needn't show every extreme that they name: `seq_ids`: ids never fall along a row; each row holds two documents of neighbouring positions.
All inputs are finite; a program needn't handle non-finite values.
Results may differ from the reference program's by a relative error of at most 0.025.
Values may be sent and summed in bfloat16 or wider, within the bound.
No kernel may reach another device: no remote copies, remote signals or barrier semaphores. Data moves between devices by JAX's collectives and lax.ppermute only.
A program may use at most 256 MiB of HBM per device.

```python
import math
import jax
import jax.numpy as jnp
import numpy as np
from jax import lax

D = 1024
HEADS = 16
FF = 4096
SEQ_LEN = 2048
TOKENS = 8192
N_FSDP = 4


def steps_of(own_key, shape, cuts, smallest, top_value):
    def one(dim, shards_of):
        draws = jax.random.uniform(jax.random.fold_in(jax.random.fold_in(own_key, 6), dim), (shards_of,), jnp.float32, smallest / len(cuts), top_value / len(cuts))
        return jnp.repeat(jnp.exp(draws), shape[dim] // shards_of).reshape((-1,) + (1,) * (len(shape) - dim - 1))

    level = one(*cuts[0])
    for cut in cuts[1:]:
        level = level * one(*cut)
    return level


def profile(amount, total, most, lean):
    weights = [(1 << 20) // math.isqrt(grade ** lean) + 1 for grade in range(2, amount + 1)]
    spare, counts = total - most - (amount - 1), [1] * (amount - 1)
    while spare > 0:
        candidates = [i for i in range(amount - 1) if counts[i] < most]
        pool, budget = sum([weights[i] for i in candidates]), spare
        for i in candidates:
            addition = min(most - counts[i], max(1, budget * weights[i] // pool), spare)
            counts[i] = counts[i] + addition
            spare = spare - addition
    return np.array([most] + counts)


def uneven(stream_key, amount, total, bound, lean):
    if amount == 2:
        one = jax.random.randint(stream_key, (), max(1, total - bound), min(bound, total - 1) + 1)
        return jnp.stack([one, total - one])
    tallies = jnp.asarray(profile(amount, total, bound, lean), jnp.int32)
    twos = (amount - 1) // 2
    source_of, taker = tallies[1:1 + 2 * twos:2], tallies[2:2 + 2 * twos:2]
    margin = jnp.minimum(source_of - 1, bound - taker)
    shifted = jax.random.randint(jax.random.fold_in(stream_key, 1), (twos,), 0, 1 << 20) % (margin + 1)
    tallies = tallies.at[1:1 + 2 * twos:2].set(source_of - shifted).at[2:2 + 2 * twos:2].set(taker + shifted)
    return tallies[jax.random.permutation(jax.random.fold_in(stream_key, 2), amount)]


def gaussian(own_key, shape, spread, most, shards=(), dtype=jnp.bfloat16):
    loudness = steps_of(own_key, shape, shards, -0.22, 0.18) if shards else 1.0
    result = jax.random.normal(own_key, shape, jnp.float32) * spread * loudness
    return jnp.minimum(jnp.maximum(result, -most), most).astype(dtype)


def setup_inputs(seed: int = 0) -> dict:
    key_list = jax.random.split(jax.random.key(seed), 16)
    hidden_in = gaussian(key_list[0], (TOKENS, D), 1.0, 6.0, ((0, 32),))
    seq_ids = jax.vmap(lambda own: jnp.searchsorted(jnp.cumsum(uneven(own, 2, SEQ_LEN, 3 * SEQ_LEN // 4, 0)), jnp.arange(SEQ_LEN), side="right"))(jax.random.split(key_list[1], N_FSDP)).reshape((N_FSDP, SEQ_LEN)).astype(jnp.int32)
    ln1_gain = jnp.clip(1.0 + 0.1 * jax.random.normal(key_list[2], (D,), jnp.float32), 0.5, 1.5).astype(jnp.bfloat16)
    ln1_bias = gaussian(key_list[3], (D,), 0.3, 3.0, ((0, 4),))
    w_qkv = gaussian(key_list[4], (D, 3 * D), D ** -0.5, 0.1875, ((0, 4),))
    b_qv = gaussian(key_list[5], (2 * D,), 0.3, 3.0, ((0, 4),))
    w_dense = gaussian(key_list[6], (D, D), (max(D // 16, 4)) ** -0.5, 0.75, ((0, 4),))
    b_dense = gaussian(key_list[7], (D,), 1.0, 5.0, ((0, 4),))
    ln2_gain = jnp.clip(1.0 + 0.18 * jax.random.normal(key_list[8], (D,), jnp.float32), 0.099609375, 1.8984375).astype(jnp.bfloat16)
    ln2_bias = gaussian(key_list[9], (D,), 0.3, 3.0, ((0, 4),))
    w_up = gaussian(key_list[10], (D, FF), D ** -0.5, 0.1875, ((0, 4),))
    b_up = gaussian(key_list[11], (FF,), 0.5, 4.0, ((0, 4),))
    w_down = gaussian(key_list[12], (FF, D), FF ** -0.5, 0.09375, ((0, 4),))
    b_down = gaussian(key_list[13], (D,), 1.0, 5.0, ((0, 4),))
    cotangent = gaussian(key_list[14], (TOKENS, D), 1.0, 6.0, ((0, 32),))
    return dict(hidden_in=hidden_in, seq_ids=seq_ids, ln1_gain=ln1_gain, ln1_bias=ln1_bias, w_qkv=w_qkv, b_qv=b_qv, w_dense=w_dense, b_dense=b_dense, ln2_gain=ln2_gain, ln2_bias=ln2_bias, w_up=w_up, b_up=b_up, w_down=w_down, b_down=b_down, cotangent=cotangent)


NORM_EPSILON = 1e-05
MASKED_SCORE = -1e+30
GELU_SCALE = math.sqrt(2.0 / math.pi)

def layer_norm(values, gain, shift):
    centre = values - lax.optimization_barrier(jnp.mean(values, axis=-1, keepdims=True))
    inv_std = lax.rsqrt(lax.optimization_barrier(jnp.mean(centre * centre, axis=-1, keepdims=True)) + NORM_EPSILON)
    normed = centre * inv_std
    return (normed * gain + shift, normed, inv_std)

def norm_backward(grad_out, normed, inv_std, gain):
    scaled = grad_out * gain
    return inv_std * (scaled - lax.optimization_barrier(jnp.mean(scaled, axis=-1, keepdims=True)) - normed * lax.optimization_barrier(jnp.mean(scaled * normed, axis=-1, keepdims=True)))

def gelu_pair(pre_act):
    inner = jnp.tanh(GELU_SCALE * (pre_act + 0.044715 * pre_act * pre_act * pre_act))
    value = 0.5 * pre_act * (1.0 + inner)
    deriv = 0.5 * (1.0 + inner) + 0.5 * pre_act * (1.0 - inner * inner) * GELU_SCALE * (1.0 + 3.0 * 0.044715 * pre_act * pre_act)
    return (value, deriv)

def alibi_slopes(head_count, row_length):
    order = jnp.arange(1, head_count + 1).astype(jnp.float32)
    return jnp.exp2(-8.0 * order / head_count) * (8.0 / row_length)

def masked_scores(query_blk, key_heads, query_pos, key_pos, query_seg, key_seg, slopes, inv_root):
    scores = jnp.einsum('qhd,khd->hqk', query_blk.astype(jnp.float32), key_heads.astype(jnp.float32)) * inv_root
    distance = (query_pos[:, None] - key_pos[None, :]).astype(jnp.float32)
    scores = scores - slopes[:, None, None] * distance[None]
    allowed = ((query_seg[:, None] == key_seg[None, :]) & (key_pos[None, :] <= query_pos[:, None]))[None]
    return (scores, allowed)

def sequence_pass(params, hidden_row, seg_row, cot_row):
    gain_one, shift_one, weight_qkv, bias_qv, weight_dense, bias_dense, gain_two, shift_two, weight_up, bias_up, weight_down, bias_down = params
    seq_len, model_width = hidden_row.shape
    head_count = HEADS
    head_size = model_width // head_count
    inv_root = 1.0 / math.sqrt(head_size)
    slopes = alibi_slopes(head_count, seq_len)
    block = min(512, seq_len)
    block_count = seq_len // block
    positions = jnp.arange(seq_len).astype(jnp.int32)
    inputs = hidden_row.astype(jnp.float32)
    normed_in, normed_one, inv_std_one = layer_norm(inputs, gain_one, shift_one)
    hidden_one = normed_in.astype(jnp.bfloat16)
    projected = jnp.dot(hidden_one, weight_qkv, preferred_element_type=jnp.float32)
    queries = (projected[:, :model_width] + bias_qv[:model_width]).astype(jnp.bfloat16)
    keys = projected[:, model_width:2 * model_width].astype(jnp.bfloat16)
    values = (projected[:, 2 * model_width:] + bias_qv[model_width:]).astype(jnp.bfloat16)
    query_heads = queries.reshape(seq_len, head_count, head_size)
    key_heads = keys.reshape(seq_len, head_count, head_size)
    value_heads = values.reshape(seq_len, head_count, head_size)
    query_blocks = query_heads.reshape(block_count, block, head_count, head_size)
    pos_blocks = positions.reshape(block_count, block)
    seg_blocks = seg_row.reshape(block_count, block)

    def attend(record):
        query_blk, query_pos, query_seg = record
        scores, allowed = masked_scores(query_blk, key_heads, query_pos, positions, query_seg, seg_row, slopes, inv_root)
        row_max = lax.optimization_barrier(jnp.max(jnp.where(allowed, scores, MASKED_SCORE), axis=-1))
        row_sum = lax.optimization_barrier(jnp.sum(jnp.where(allowed, jnp.exp(scores - row_max[..., None]), 0.0), axis=-1))
        log_total = row_max + jnp.log(row_sum)
        weights = jnp.where(allowed, jnp.exp(scores - log_total[..., None]), 0.0).astype(jnp.bfloat16)
        attended = jnp.einsum('hqk,khd->qhd', weights.astype(jnp.float32), value_heads.astype(jnp.float32))
        return (attended.astype(jnp.bfloat16), log_total)
    attn_blocks, lse_blocks = lax.map(attend, (query_blocks, pos_blocks, seg_blocks))
    attended = attn_blocks.reshape(seq_len, model_width)
    resid = inputs + (jnp.dot(attended, weight_dense, preferred_element_type=jnp.float32) + bias_dense)
    normed_mid, normed_two, inv_std_two = layer_norm(resid, gain_two, shift_two)
    hidden_two = normed_mid.astype(jnp.bfloat16)
    pre_act = jnp.dot(hidden_two, weight_up, preferred_element_type=jnp.float32) + bias_up
    act_value, act_deriv = gelu_pair(pre_act)
    activ = act_value.astype(jnp.bfloat16)
    block_out = resid + (jnp.dot(activ, weight_down, preferred_element_type=jnp.float32) + bias_down)
    grad_top = cot_row.astype(jnp.float32)
    g_b_down = lax.optimization_barrier(jnp.sum(grad_top, axis=0))
    g_w_down = jnp.dot(activ.T, cot_row, preferred_element_type=jnp.float32)
    grad_pre = jnp.dot(cot_row, weight_down.T, preferred_element_type=jnp.float32) * act_deriv
    g_b_up = lax.optimization_barrier(jnp.sum(grad_pre, axis=0))
    grad_pre_bf = grad_pre.astype(jnp.bfloat16)
    g_w_up = jnp.dot(hidden_two.T, grad_pre_bf, preferred_element_type=jnp.float32)
    grad_hidden_two = jnp.dot(grad_pre_bf, weight_up.T, preferred_element_type=jnp.float32)
    g_gain_two = lax.optimization_barrier(jnp.sum(grad_hidden_two * normed_two, axis=0))
    g_shift_two = lax.optimization_barrier(jnp.sum(grad_hidden_two, axis=0))
    grad_resid = grad_top + norm_backward(grad_hidden_two, normed_two, inv_std_two, gain_two)
    g_b_dense = lax.optimization_barrier(jnp.sum(grad_resid, axis=0))
    grad_resid_bf = grad_resid.astype(jnp.bfloat16)
    g_w_dense = jnp.dot(attended.T, grad_resid_bf, preferred_element_type=jnp.float32)
    grad_attended = jnp.dot(grad_resid_bf, weight_dense.T, preferred_element_type=jnp.float32).astype(jnp.bfloat16)
    grad_heads = grad_attended.reshape(seq_len, head_count, head_size)
    delta = lax.optimization_barrier(jnp.sum(grad_heads.astype(jnp.float32) * attn_blocks.reshape(seq_len, head_count, head_size).astype(jnp.float32), axis=-1))
    delta_blocks = delta.reshape(block_count, block, head_count).transpose(0, 2, 1)
    grad_blocks = grad_heads.reshape(block_count, block, head_count, head_size)

    def back_step(state, record):
        query_blk, grad_blk, lse_blk, delta_blk, query_pos, query_seg = record
        scores, allowed = masked_scores(query_blk, key_heads, query_pos, positions, query_seg, seg_row, slopes, inv_root)
        prob = jnp.where(allowed, jnp.exp(scores - lse_blk[..., None]), 0.0)
        dprob = jnp.einsum('qhd,khd->hqk', grad_blk.astype(jnp.float32), value_heads.astype(jnp.float32))
        dscore = (prob * (dprob - delta_blk[..., None]) * inv_root).astype(jnp.bfloat16)
        prob_bf = prob.astype(jnp.bfloat16)
        grad_q = jnp.einsum('hqk,khd->qhd', dscore.astype(jnp.float32), key_heads.astype(jnp.float32))
        grad_k = state[0] + jnp.einsum('hqk,qhd->khd', dscore.astype(jnp.float32), query_blk.astype(jnp.float32))
        grad_v = state[1] + jnp.einsum('hqk,qhd->khd', prob_bf.astype(jnp.float32), grad_blk.astype(jnp.float32))
        return ((grad_k, grad_v), grad_q)
    empty_kv = jnp.zeros((seq_len, head_count, head_size), jnp.float32)
    (grad_k, grad_v), grad_q = lax.scan(back_step, (empty_kv, empty_kv), (query_blocks, grad_blocks, lse_blocks, delta_blocks, pos_blocks, seg_blocks))
    grad_query = grad_q.reshape(seq_len, model_width)
    grad_key = grad_k.reshape(seq_len, model_width)
    grad_value = grad_v.reshape(seq_len, model_width)
    g_b_qv = jnp.concatenate([lax.optimization_barrier(jnp.sum(grad_query, axis=0)), lax.optimization_barrier(jnp.sum(grad_value, axis=0))])
    grad_qkv = jnp.concatenate([grad_query.astype(jnp.bfloat16), grad_key.astype(jnp.bfloat16), grad_value.astype(jnp.bfloat16)], axis=1)
    g_w_qkv = jnp.dot(hidden_one.T, grad_qkv, preferred_element_type=jnp.float32)
    grad_hidden_one = jnp.dot(grad_qkv, weight_qkv.T, preferred_element_type=jnp.float32)
    g_gain_one = lax.optimization_barrier(jnp.sum(grad_hidden_one * normed_one, axis=0))
    g_shift_one = lax.optimization_barrier(jnp.sum(grad_hidden_one, axis=0))
    grad_input = grad_resid + norm_backward(grad_hidden_one, normed_one, inv_std_one, gain_one)
    grads = (g_gain_one, g_shift_one, g_w_qkv, g_b_qv, g_w_dense, g_b_dense, g_gain_two, g_shift_two, g_w_up, g_b_up, g_w_down, g_b_down)
    return (block_out, grad_input, grads)

def zeros_like_float(array):
    return jnp.zeros(array.shape, jnp.float32)

def reference(hidden_in, seq_ids, ln1_gain, ln1_bias, w_qkv, b_qv, w_dense, b_dense, ln2_gain, ln2_bias, w_up, b_up, w_down, b_down, cotangent):
    params = (ln1_gain.astype(jnp.float32), ln1_bias.astype(jnp.float32), w_qkv, b_qv.astype(jnp.float32), w_dense, b_dense.astype(jnp.float32), ln2_gain.astype(jnp.float32), ln2_bias.astype(jnp.float32), w_up, b_up.astype(jnp.float32), w_down, b_down.astype(jnp.float32))
    hidden_rows = hidden_in.reshape(N_FSDP, SEQ_LEN, D)
    cot_rows = cotangent.reshape(N_FSDP, SEQ_LEN, D)
    init = jax.tree.map(zeros_like_float, params)

    def step(grad_sums, record):
        out_row, input_row, grads = sequence_pass(params, record[0], record[1], record[2])
        return (jax.tree.map(jnp.add, grad_sums, grads), (out_row, input_row))
    totals, (out_rows, input_rows) = lax.scan(step, init, (hidden_rows, seq_ids, cot_rows))
    return (out_rows.reshape(TOKENS, D), input_rows.reshape(TOKENS, D), totals[0], totals[1], totals[2], totals[3], totals[4], totals[5], totals[6], totals[7], totals[8], totals[9], totals[10], totals[11])
```

```python
import functools
import math

import jax
import jax.numpy as jnp
from jax import lax
from jax.experimental import pallas as pl
from jax.experimental.pallas import tpu as pltpu
from jax.sharding import PartitionSpec as P

HEADS = 16
HEAD = 64
NORM_EPSILON = 1e-05
MASKED_SCORE = -1e30
GELU_SCALE = math.sqrt(2.0 / math.pi)
NT = (((1,), (1,)), ((), ()))
TN = (((0,), (0,)), ((), ()))
f32 = jnp.float32
bf16 = jnp.bfloat16
MIB = 1 << 20


def head_masks(hp, w):
    lane = lax.broadcasted_iota(jnp.int32, (1, w), 1)
    return [(lane // HEAD) == h for h in range(hp)]


def normalize(x):
    centre = x - jnp.mean(x, axis=-1, keepdims=True)
    inv_std = lax.rsqrt(jnp.mean(centre * centre, axis=-1, keepdims=True) + NORM_EPSILON)
    return centre * inv_std, inv_std


def norm_backward(grad_out, normed, inv_std, gain):
    scaled = grad_out * gain
    return inv_std * (
        scaled
        - jnp.mean(scaled, axis=-1, keepdims=True)
        - normed * jnp.mean(scaled * normed, axis=-1, keepdims=True)
    )


def gelu_pair(u):
    inner = jnp.tanh(GELU_SCALE * (u + 0.044715 * u * u * u))
    value = 0.5 * u * (1.0 + inner)
    deriv = 0.5 * (1.0 + inner) + 0.5 * u * (1.0 - inner * inner) * GELU_SCALE * (
        1.0 + 3.0 * 0.044715 * u * u
    )
    return value, deriv


def dot(a, b):
    return jnp.dot(a, b, preferred_element_type=f32)


def dot_nt(a, b):
    return lax.dot_general(a, b, NT, preferred_element_type=f32)


def dot_tn(a, b):
    return lax.dot_general(a, b, TN, preferred_element_type=f32)


def ln_qkv_kernel(x_ref, g_ref, s_ref, w_ref, b_ref, h_ref, q_ref, k_ref, v_ref):
    width = q_ref.shape[1]
    normed, _ = normalize(x_ref[...].astype(f32))
    h = (normed * g_ref[...] + s_ref[...]).astype(bf16)
    h_ref[...] = h
    p = dot(h, w_ref[...])
    q_ref[...] = (p[:, :width] + b_ref[0:1, :]).astype(bf16)
    k_ref[...] = p[:, width : 2 * width].astype(bf16)
    v_ref[...] = (p[:, 2 * width :] + b_ref[1:2, :]).astype(bf16)


def ln_qkv(x, gain, shift, weight, bias, blk):
    rows, dim = x.shape
    width = weight.shape[1] // 3
    full = lambda a: pl.BlockSpec(a.shape, lambda i: (0, 0))
    tok = lambda cols: pl.BlockSpec((blk, cols), lambda i: (i, 0))
    out = lambda cols: jax.ShapeDtypeStruct((rows, cols), bf16)
    return pl.pallas_call(
        ln_qkv_kernel,
        name="ln_qkv",
        grid=(rows // blk,),
        in_specs=[tok(dim), full(gain), full(shift), full(weight), full(bias)],
        out_specs=[tok(dim), tok(width), tok(width), tok(width)],
        out_shape=[out(dim), out(width), out(width), out(width)],
        compiler_params=pltpu.CompilerParams(vmem_limit_bytes=32 * MIB),
        cost_estimate=pl.CostEstimate(
            flops=6 * rows * dim * width, bytes_accessed=4 * rows * dim, transcendentals=0
        ),
    )(x, gain, shift, weight, bias)


def attn_fwd_kernel(hp, blk, sc_ref, sl_ref, q_ref, k_ref, v_ref, o_ref, lse_ref):
    i = pl.program_id(0)
    c, b = sc_ref[0], sc_ref[1]
    w = q_ref.shape[1]
    masks = head_masks(hp, w)
    q = q_ref[...] * jnp.asarray(0.125, bf16)
    zero = jnp.zeros_like(q)
    q2 = jnp.concatenate([jnp.where(m, q, zero) for m in masks], axis=0)
    rows = hp * blk

    def tile(j, carry, masked):
        m, l, acc = carry
        at = pl.multiple_of((j ^ c) * blk, blk)
        k = k_ref[pl.ds(at, blk), :]
        v = v_ref[pl.ds(at, blk), :]
        s = lax.dot_general(q2, k, NT, preferred_element_type=f32)
        kpos = j * blk + lax.broadcasted_iota(jnp.int32, (1, blk), 1)
        kf = kpos.astype(f32)
        parts = []
        if masked:
            qpos = i * blk + lax.broadcasted_iota(jnp.int32, (blk, 1), 0)
            allowed = (kpos <= qpos) & ((kpos >= b) | (qpos < b))
        for h in range(hp):
            t = s[h * blk:(h + 1) * blk] + sl_ref[h] * kf
            if masked:
                t = jnp.where(allowed, t, MASKED_SCORE)
            parts.append(t)
        s = jnp.concatenate(parts, axis=0)
        mn = jnp.maximum(m, jnp.max(s, axis=1, keepdims=True))
        p = jnp.exp(s - mn)
        alpha = jnp.exp(m - mn)
        l = l * alpha + jnp.sum(p, axis=1, keepdims=True)
        acc = acc * alpha + jnp.dot(p.astype(bf16), v, preferred_element_type=f32)
        return mn, l, acc

    init = (jnp.full((rows, 1), MASKED_SCORE, f32), jnp.zeros((rows, 1), f32), jnp.zeros((rows, w), f32))
    carry = tile(i, init, True)
    own_first = i * blk < b
    lo = jnp.where(own_first, 0, b // blk)
    mixed = (i + 1) * blk > b
    split = jnp.where(mixed, jnp.minimum((b + blk - 1) // blk, i), lo)
    split = jnp.maximum(split, lo)
    carry = lax.fori_loop(lo, split, lambda j, cy: tile(j, cy, True), carry)
    m, l, acc = lax.fori_loop(split, i, lambda j, cy: tile(j, cy, False), carry)
    out = acc / l
    o = out[:blk]
    for h in range(1, hp):
        o = jnp.where(masks[h], out[h * blk:(h + 1) * blk], o)
    o_ref[...] = o.astype(bf16)
    lse = m + jnp.log(l)
    lse_ref[0] = jnp.transpose(jnp.broadcast_to(lse, (rows, 128)))[0:1, :]

def attn_fwd(sc, sl, q, k, v, blk, hp):
    S, w = q.shape
    nb = S // blk
    return pl.pallas_call(
        functools.partial(attn_fwd_kernel, hp, blk),
        name="attn_fwd",
        grid_spec=pltpu.PrefetchScalarGridSpec(
            num_scalar_prefetch=2, grid=(nb,),
            in_specs=[pl.BlockSpec((blk, w), lambda i, sc, sl: (i ^ sc[0], 0)),
                      pl.BlockSpec((S, w), lambda i, sc, sl: (0, 0)),
                      pl.BlockSpec((S, w), lambda i, sc, sl: (0, 0))],
            out_specs=[pl.BlockSpec((blk, w), lambda i, sc, sl: (i, 0)),
                       pl.BlockSpec((1, 1, hp * blk), lambda i, sc, sl: (i, 0, 0))]),
        out_shape=[jax.ShapeDtypeStruct((S, w), bf16), jax.ShapeDtypeStruct((nb, 1, hp * blk), f32)],
        compiler_params=pltpu.CompilerParams(vmem_limit_bytes=48 * MIB),
        cost_estimate=pl.CostEstimate(flops=4 * S * S * w, bytes_accessed=8 * S * w, transcendentals=S * S * hp // 2),
    )(sc, sl, q, k, v)

def attn_bwd_kernel(hp, blk, sc_ref, sl_ref, q_ref, k_ref, v_ref, do_ref, o_ref, lse_ref, g_ref, gb_ref,
                    q2_ref, do2_ref, delta_ref, dq_ref, bias_ref, dk_ref, dv_ref):
    j = pl.program_id(0)
    nb = pl.num_programs(0)
    c, b = sc_ref[0], sc_ref[1]
    w = k_ref.shape[1]
    rows = hp * blk
    masks = head_masks(hp, w)

    @pl.when(j == 0)
    def _():
        pick = (lax.broadcasted_iota(jnp.int32, (8, w), 1) // HEAD == lax.broadcasted_iota(jnp.int32, (8, w), 0)).astype(f32)
        gb_ref[...] = jnp.zeros_like(gb_ref)
        def prep(i, _):
            at = pl.multiple_of((i ^ c) * blk, blk)
            ai = pl.multiple_of(i * blk, blk)
            q = q_ref[pl.ds(at, blk), :] * jnp.asarray(0.125, bf16)
            do = do_ref[pl.ds(ai, blk), :]
            o = o_ref[pl.ds(ai, blk), :]
            zero = jnp.zeros_like(q)
            for h in range(hp):
                q2_ref[i, h * blk:(h + 1) * blk, :] = jnp.where(masks[h], q, zero)
                do2_ref[i, h * blk:(h + 1) * blk, :] = jnp.where(masks[h], do, zero)
            prod = do.astype(f32) * o.astype(f32)
            d = lax.dot_general(pick, prod, NT, preferred_element_type=f32, precision=lax.Precision.HIGHEST)
            for h in range(hp):
                delta_ref[i, :, h * blk:(h + 1) * blk] = d[h:h + 1, :]
            dq_ref[i] = jnp.zeros((blk, w), f32)
            return 0
        lax.fori_loop(0, nb, prep, 0)

    k = k_ref[...]
    v = v_ref[...]
    kcol = j * blk + lax.broadcasted_iota(jnp.int32, (blk, 1), 0)
    kf = kcol.astype(f32)
    for h in range(hp):
        bias_ref[:, h * blk:(h + 1) * blk] = jnp.broadcast_to(kf * sl_ref[h], (blk, blk))
    dk_ref[...] = jnp.zeros_like(dk_ref)
    dv_ref[...] = jnp.zeros_like(dv_ref)

    def tile(i, masked):
        q2 = q2_ref[i]
        do2 = do2_ref[i]
        s = lax.dot_general(k, q2, NT, preferred_element_type=f32)
        p = jnp.exp(s + bias_ref[...] - lse_ref[i])
        if masked:
            r = lax.broadcasted_iota(jnp.int32, (1, rows), 1)
            qpos = i * blk + (r & (blk - 1))
            allowed = (kcol <= qpos) & ((kcol >= b) | (qpos < b))
            p = jnp.where(allowed, p, 0.0)
        dp = lax.dot_general(v, do2, NT, preferred_element_type=f32)
        ds = (p * (dp - delta_ref[i])).astype(bf16)
        dv_ref[...] += jnp.dot(p.astype(bf16), do2, preferred_element_type=f32)
        dk_ref[...] += jnp.dot(ds, q2, preferred_element_type=f32)
        dq2 = lax.dot_general(ds, k, TN, preferred_element_type=f32)
        d = dq2[:blk]
        for h in range(1, hp):
            d = jnp.where(masks[h], dq2[h * blk:(h + 1) * blk], d)
        dq_ref[i] += d

    tile(j, True)
    hi = jnp.where((j + 1) * blk <= b, (b + blk - 1) // blk, nb)
    split = jnp.where(j * blk < b, jnp.maximum(b // blk, j + 1), hi)
    split = jnp.minimum(split, hi)
    lax.fori_loop(j + 1, split, lambda i, _: (tile(i, False), 0)[1], 0)
    lax.fori_loop(jnp.maximum(split, j + 1), hi, lambda i, _: (tile(i, True), 0)[1], 0)
    dq = dq_ref[j] * 0.125
    dv = dv_ref[...]
    g_ref[:, 0:w] = dq.astype(bf16)
    g_ref[:, w:2 * w] = dk_ref[...].astype(bf16)
    g_ref[:, 2 * w:3 * w] = dv.astype(bf16)
    gb_ref[0:1, :] += jnp.sum(dq, axis=0, keepdims=True)
    gb_ref[1:2, :] += jnp.sum(dv, axis=0, keepdims=True)

def attn_bwd(sc, sl, q, k, v, do, o, lse, blk, hp):
    S, w = q.shape
    nb = S // blk
    full = lambda shape: pl.BlockSpec(shape, lambda j, sc, sl: (0,) * len(shape))
    slot = lambda width: pl.BlockSpec((blk, width), lambda j, sc, sl: (j ^ sc[0], 0))
    return pl.pallas_call(
        functools.partial(attn_bwd_kernel, hp, blk),
        name="attn_bwd",
        grid_spec=pltpu.PrefetchScalarGridSpec(
            num_scalar_prefetch=2, grid=(nb,),
            in_specs=[full((S, w)), slot(w), slot(w), full((S, w)), full((S, w)), full((nb, 1, hp * blk))],
            out_specs=[slot(3 * w), full((8, w))],
            scratch_shapes=[pltpu.VMEM((nb, hp * blk, w), bf16), pltpu.VMEM((nb, hp * blk, w), bf16),
                            pltpu.VMEM((nb, 1, hp * blk), f32), pltpu.VMEM((nb, blk, w), f32),
                            pltpu.VMEM((blk, hp * blk), f32), pltpu.VMEM((blk, w), f32), pltpu.VMEM((blk, w), f32)]),
        out_shape=[jax.ShapeDtypeStruct((S, 3 * w), bf16), jax.ShapeDtypeStruct((8, w), f32)],
        compiler_params=pltpu.CompilerParams(vmem_limit_bytes=48 * MIB),
        cost_estimate=pl.CostEstimate(flops=10 * S * S * w, bytes_accessed=16 * S * w, transcendentals=S * S * hp // 2),
    )(sc, sl, q, k, v, do, o, lse)


def dense_ln_kernel(x_ref, o_ref, w_ref, v_ref, y_ref, h_ref):
    y = x_ref[...].astype(f32) + (dot(o_ref[...], w_ref[...]) + v_ref[0:1, :])
    y_ref[...] = y
    normed, _ = normalize(y)
    h_ref[...] = (normed * v_ref[1:2, :] + v_ref[2:3, :]).astype(bf16)


def dense_ln(x, o, weight, vectors):
    rows, dim = x.shape
    return pl.pallas_call(
        dense_ln_kernel,
        name="dense_ln",
        out_shape=[jax.ShapeDtypeStruct((rows, dim), f32), jax.ShapeDtypeStruct((rows, dim), bf16)],
        compiler_params=pltpu.CompilerParams(vmem_limit_bytes=32 * MIB),
        cost_estimate=pl.CostEstimate(
            flops=2 * rows * dim * dim, bytes_accessed=2 * dim * dim + 12 * rows * dim, transcendentals=0
        ),
    )(x, o, weight, vectors)


def mlp_kernel(h_ref, dz_ref, u_ref, b_ref, z_ref, du_ref, dh_ref, gb_ref):
    pre = dot(h_ref[...], u_ref[...]) + b_ref[...]
    value, deriv = gelu_pair(pre)
    z_ref[...] = value.astype(bf16)
    du = dz_ref[...] * deriv

    @pl.when(pl.program_id(0) == 0)
    def _():
        gb_ref[...] = jnp.zeros_like(gb_ref)

    gb_ref[...] += jnp.sum(du, axis=0, keepdims=True)
    du = du.astype(bf16)
    du_ref[...] = du
    dh_ref[...] = dot_nt(du, u_ref[...]).astype(bf16)


def mlp(h, dz, up, bias, blk):
    rows, dim = h.shape
    width = up.shape[1]
    full = lambda a: pl.BlockSpec(a.shape, lambda i: (0, 0))
    tok = lambda cols: pl.BlockSpec((blk, cols), lambda i: (i, 0))
    out = lambda cols: jax.ShapeDtypeStruct((rows, cols), bf16)
    return pl.pallas_call(
        mlp_kernel,
        name="mlp",
        grid=(rows // blk,),
        in_specs=[tok(dim), tok(width), full(up), full(bias)],
        out_specs=[tok(width), tok(width), tok(dim), pl.BlockSpec((1, width), lambda i: (0, 0))],
        out_shape=[out(width), out(width), out(dim), jax.ShapeDtypeStruct((1, width), f32)],
        compiler_params=pltpu.CompilerParams(vmem_limit_bytes=32 * MIB),
        cost_estimate=pl.CostEstimate(
            flops=4 * rows * dim * width, bytes_accessed=4 * rows * dim + 8 * rows * width, transcendentals=rows * width
        ),
    )(h, dz, up, bias)


def ln2_back_kernel(y_ref, dh_ref, cot_ref, w_ref, v_ref, dy_ref, dyb_ref, do_ref, gs_ref):
    normed, inv_std = normalize(y_ref[...])
    dh = dh_ref[...]
    dy = cot_ref[...].astype(f32) + norm_backward(dh, normed, inv_std, v_ref[1:2, :])
    dy_ref[...] = dy
    dyb = dy.astype(bf16)
    dyb_ref[...] = dyb
    do_ref[...] = dot_nt(dyb, w_ref[...]).astype(bf16)
    gs_ref[0:1, :] = jnp.sum(dy, axis=0, keepdims=True)
    gs_ref[1:2, :] = jnp.sum(dh * normed, axis=0, keepdims=True)
    gs_ref[2:3, :] = jnp.sum(dh, axis=0, keepdims=True)
    gs_ref[3:4, :] = jnp.sum(cot_ref[...].astype(f32), axis=0, keepdims=True)


def ln2_back(y, dh, cot, weight, vectors):
    rows, dim = y.shape
    return pl.pallas_call(
        ln2_back_kernel,
        name="ln2_back",
        out_shape=[
            jax.ShapeDtypeStruct((rows, dim), f32),
            jax.ShapeDtypeStruct((rows, dim), bf16),
            jax.ShapeDtypeStruct((rows, dim), bf16),
            jax.ShapeDtypeStruct((4, dim), f32),
        ],
        compiler_params=pltpu.CompilerParams(vmem_limit_bytes=32 * MIB),
        cost_estimate=pl.CostEstimate(
            flops=2 * rows * dim * dim, bytes_accessed=2 * dim * dim + 20 * rows * dim, transcendentals=0
        ),
    )(y, dh, cot, weight, vectors)


def dh1_kernel(g_ref, w_ref, x_ref, dh_ref, gs_ref):
    dh = dot_nt(g_ref[...], w_ref[...])
    dh_ref[...] = dh.astype(bf16)
    normed, _ = normalize(x_ref[...].astype(f32))

    @pl.when(pl.program_id(0) == 0)
    def _():
        gs_ref[...] = jnp.zeros_like(gs_ref)

    gs_ref[0:1, :] += jnp.sum(dh * normed, axis=0, keepdims=True)
    gs_ref[1:2, :] += jnp.sum(dh, axis=0, keepdims=True)


def dh1_part(g, weight, x, blk):
    rows, dim = x.shape
    full = lambda a: pl.BlockSpec(a.shape, lambda i: (0, 0))
    tok = lambda cols: pl.BlockSpec((blk, cols), lambda i: (i, 0))
    return pl.pallas_call(
        dh1_kernel,
        name="dh1_part",
        grid=(rows // blk,),
        in_specs=[tok(g.shape[1]), full(weight), tok(dim)],
        out_specs=[tok(dim), pl.BlockSpec((2, dim), lambda i: (0, 0))],
        out_shape=[jax.ShapeDtypeStruct((rows, dim), bf16), jax.ShapeDtypeStruct((2, dim), f32)],
        compiler_params=pltpu.CompilerParams(vmem_limit_bytes=32 * MIB),
        cost_estimate=pl.CostEstimate(
            flops=2 * rows * dim * g.shape[1], bytes_accessed=4 * rows * dim, transcendentals=0
        ),
    )(g, weight, x)


def swap(x, n, bit):
    return lax.ppermute(x, "ctx", [(i, i ^ bit) for i in range(n)])


def gather_slots(x, n):
    if n != 8:
        slots = {0: x}
        bit = n >> 1
        while bit:
            for s in list(slots):
                slots[s ^ bit] = swap(slots[s], n, bit)
            bit >>= 1
        return [slots[s] for s in range(n)]
    half = x.shape[0] // 2
    a, b = swap(x, n, 2), swap(x, n, 4)
    c = jnp.concatenate([swap(a[:half], n, 4), swap(b[half:], n, 2)], axis=0)
    slots = [x, None, a, None, b, None, c, None]
    for s in range(0, n, 2):
        slots[s + 1] = swap(slots[s], n, 1)
    return slots


def add16(a, b):
    return (a.astype(f32) + b.astype(f32)).astype(bf16)


def scatter_slots(parts, n):
    if n != 8:
        parts = dict(enumerate(parts))
        bit = 1
        while bit < n:
            for s in [s for s in parts if not s & bit]:
                parts[s] = add16(parts[s], swap(parts.pop(s | bit), n, bit))
            bit <<= 1
        return parts[0].astype(f32)
    half = parts[0].shape[0] // 2
    q6, q2, q4, q0 = [add16(parts[s], swap(parts[s + 1], n, 1)) for s in (6, 2, 4, 0)]
    far2, far4 = swap(q6[:half], n, 4), swap(q6[half:], n, 2)
    near2 = swap(q2[half:], n, 2)
    near4 = swap(q4[:half], n, 4)
    last2 = swap(add16(q2[:half], far2), n, 2)
    last4 = swap(add16(q4[half:], far4), n, 4)
    return q0.astype(f32) + jnp.concatenate(
        [last2.astype(f32) + near4.astype(f32), near2.astype(f32) + last4.astype(f32)], axis=0
    )


def on_device(
    hidden_in,
    seq_ids,
    ln1_gain,
    ln1_bias,
    w_qkv,
    b_qv,
    w_dense,
    b_dense,
    ln2_gain,
    ln2_bias,
    w_up,
    b_up,
    w_down,
    b_down,
    cotangent,
    n,
    nz,
):
    c = lax.axis_index("ctx")
    z = lax.axis_index("fsdp")
    rows, dim = hidden_in.shape
    seq_len = seq_ids.shape[1]
    shard = dim // nz
    hp = HEADS // n
    w = hp * HEAD
    fb = w_down.shape[0] // n
    fl = nz * fb
    both = ("fsdp", "ctx")

    small = jnp.concatenate([ln1_gain, ln1_bias, b_dense, ln2_gain, ln2_bias, b_down, b_qv, b_up])
    small = lax.all_gather(small, "fsdp", axis=0, tiled=False).astype(f32)
    vec = lambda i: small[:, i * shard : (i + 1) * shard].reshape(1, dim)
    gain1, shift1 = vec(0), vec(1)
    mid = jnp.concatenate([vec(2), vec(3), vec(4)], axis=0)
    bias_down = vec(5)
    bias_qv = small[:, 6 * shard : 8 * shard].reshape(2, n, w)
    bias_qv = lax.dynamic_index_in_dim(bias_qv, c, 1, keepdims=False)
    bias_up = small[:, 8 * shard :].reshape(nz, n, fb)
    bias_up = lax.dynamic_index_in_dim(bias_up, c, 1, keepdims=False).reshape(1, fl)

    wq = lax.dynamic_index_in_dim(w_qkv.reshape(shard, 3, n, w), c, 2, keepdims=False).reshape(shard, 3 * w)
    wq = lax.all_gather(wq, "fsdp", axis=0, tiled=True)
    wd = lax.dynamic_slice_in_dim(w_dense, c * (shard // n), shard // n, 0)
    wd = lax.all_gather(wd, both, axis=0, tiled=True)
    wu = lax.dynamic_index_in_dim(w_up.reshape(shard, nz, n, fb), c, 2, keepdims=False).reshape(shard, fl)
    wn = lax.dynamic_slice_in_dim(w_down, c * fb, fb, 0).reshape(shard, fl)
    ff = lax.all_gather(jnp.concatenate([wu, wn], axis=1), "fsdp", axis=0, tiled=True)
    wu = ff[:, :fl]
    wn = ff[:, fl:].reshape(fl, dim)

    seg = seq_ids[0]
    boundary = jnp.sum((seg == seg[0]).astype(jnp.int32))
    sc = jnp.stack([c.astype(jnp.int32), boundary])
    order = (c * hp + 1 + jnp.arange(hp)).astype(f32)
    slopes = jnp.exp2(-8.0 * order / HEADS) * (8.0 / seq_len)

    x_slots = gather_slots(hidden_in, n)
    x_all = jnp.concatenate(x_slots, axis=0)
    h1, q, k, v = ln_qkv(x_all, gain1, shift1, wq, bias_qv, rows)
    o, lse = attn_fwd(sc, slopes, q, k, v, rows, hp)
    cot_gate, _ = lax.optimization_barrier((cotangent, x_slots[n - 2]))
    cot_all = jnp.concatenate(gather_slots(cot_gate, n), axis=0)
    o_own = lax.all_to_all(o, "ctx", split_axis=0, concat_axis=1, tiled=True)
    y1, h2 = dense_ln(hidden_in, o_own, wd, mid)

    h2_all = jnp.concatenate(gather_slots(h2, n), axis=0)
    dz = dot_nt(cot_all, wn)
    act, du, dh2, gb_up = mlp(h2_all, dz, wu, bias_up, rows)
    blocks = lambda a: [a[s * rows : (s + 1) * rows] for s in range(n)]
    dh2_own = scatter_slots(blocks(dh2), n)
    dy, dyb, do, sums = ln2_back(y1, dh2_own, cotangent, wd, mid)
    do_heads = lax.all_to_all(do, "ctx", split_axis=1, concat_axis=0, tiled=True)

    out_part = dot(act, wn).astype(bf16)
    block_out = y1 + (scatter_slots(blocks(out_part), n) + bias_down)
    g_down = dot_tn(act, cot_all).astype(bf16)
    g_up = dot_tn(h2_all, du).astype(bf16)
    g_dense = dot_tn(o_own, dyb).astype(bf16)

    g, gb_qv = attn_bwd(sc, slopes, q, k, v, do_heads, o, lse, rows, hp)
    dh1, sums1 = dh1_part(g, wq, x_all, rows)
    dh1_own = scatter_slots(blocks(dh1), n)
    normed1, inv1 = normalize(hidden_in.astype(f32))
    grad_input = dy + norm_backward(dh1_own, normed1, inv1, gain1)
    g_qkv = dot_tn(h1, g).astype(bf16)

    rs = lambda a: lax.psum_scatter(a, "fsdp", scatter_dimension=0, tiled=True)
    g_down = lax.all_gather(rs(g_down), "ctx", axis=0, tiled=True).astype(f32)
    g_up = lax.all_gather(rs(g_up).reshape(shard, nz, fb), "ctx", axis=2, tiled=True).reshape(shard, nz * n * fb).astype(f32)
    g_dense = lax.psum_scatter(g_dense, both, scatter_dimension=0, tiled=True)
    g_dense = lax.all_gather(g_dense, "ctx", axis=0, tiled=True).astype(f32)
    g_qkv = lax.all_gather(rs(g_qkv).reshape(shard, 3, w), "ctx", axis=2, tiled=True).reshape(shard, 3 * dim).astype(f32)

    own = lambda a, lead: lax.dynamic_update_index_in_dim(
        jnp.zeros((lead, n, a.shape[-1]), f32), a, c, 1
    )
    flat = jnp.concatenate(
        [
            sums1.reshape(2, nz, shard).transpose(1, 0, 2).reshape(nz, -1),
            sums.reshape(4, nz, shard).transpose(1, 0, 2).reshape(nz, -1),
            own(gb_qv[:2], 2).reshape(nz, 2 * shard),
            own(gb_up.reshape(nz, fb), nz).reshape(nz, n * fb),
        ],
        axis=1,
    )
    total = lax.psum(flat, both)
    total = lax.dynamic_index_in_dim(total, z, 0, keepdims=False)
    piece = lambda i, k=1: total[i * shard : (i + k) * shard]
    return (
        block_out,
        grad_input,
        piece(0),
        piece(1),
        g_qkv,
        piece(6, 2),
        g_dense,
        piece(2),
        piece(3),
        piece(4),
        g_up,
        total[8 * shard :],
        g_down,
        piece(5),
    )


def solution(mesh):
    n, nz = mesh.shape["ctx"], mesh.shape["fsdp"]
    shard = P("fsdp")
    mat = P("fsdp", None)
    tokens = P(("fsdp", "ctx"), None)
    return jax.shard_map(
        functools.partial(on_device, n=n, nz=nz),
        mesh=mesh,
        in_specs=(tokens, mat, shard, shard, mat, shard, mat, shard, shard, shard, mat, shard, mat, shard, tokens),
        out_specs=(tokens, tokens, shard, shard, mat, shard, mat, shard, shard, shard, mat, shard, mat, shard),
        check_vma=False,
    )
```

```python
import functools
import math

import jax
import jax.numpy as jnp
from jax import lax
from jax.experimental import pallas as pl
from jax.experimental.pallas import tpu as pltpu
from jax.sharding import PartitionSpec as P

HEADS = 16
HEAD = 64
LANES = 128
NORM_EPSILON = 1e-05
MASKED_SCORE = -1e30
GELU_SCALE = math.sqrt(2.0 / math.pi)
NT = (((1,), (1,)), ((), ()))
TN = (((0,), (0,)), ((), ()))
f32 = jnp.float32
bf16 = jnp.bfloat16
MIB = 1 << 20
EVEN_FIRST = (0, 2, 4, 6, 1, 3, 5, 7)
ANY = pl.BlockSpec(memory_space=pl.ANY)
SMEM = pl.BlockSpec(memory_space=pltpu.SMEM)


def params(limit=40):
    return pltpu.CompilerParams(vmem_limit_bytes=limit * MIB)


def cost(flops, moved, hard=0):
    return pl.CostEstimate(flops=flops, bytes_accessed=moved, transcendentals=hard)


def head_masks(hp, w):
    lane = lax.broadcasted_iota(jnp.int32, (1, w), 1)
    return [(lane // HEAD) == h for h in range(hp)]


def normalize(x):
    centre = x - jnp.mean(x, axis=-1, keepdims=True)
    inv_std = lax.rsqrt(jnp.mean(centre * centre, axis=-1, keepdims=True) + NORM_EPSILON)
    return centre * inv_std, inv_std


def norm_backward(grad_out, normed, inv_std, gain):
    scaled = grad_out * gain
    return inv_std * (
        scaled
        - jnp.mean(scaled, axis=-1, keepdims=True)
        - normed * jnp.mean(scaled * normed, axis=-1, keepdims=True)
    )


def gelu_pair(u):
    inner = jnp.tanh(GELU_SCALE * (u + 0.044715 * u * u * u))
    value = 0.5 * u * (1.0 + inner)
    deriv = 0.5 * (1.0 + inner) + 0.5 * u * (1.0 - inner * inner) * GELU_SCALE * (
        1.0 + 3.0 * 0.044715 * u * u
    )
    return value, deriv


def dot(a, b):
    return jnp.dot(a, b, preferred_element_type=f32)


def dot_nt(a, b):
    return lax.dot_general(a, b, NT, preferred_element_type=f32)


def dot_tn(a, b):
    return lax.dot_general(a, b, TN, preferred_element_type=f32)


def rowsum(x):
    return jnp.sum(x, axis=0, keepdims=True)


def pieces_of(slots):
    flat, where = [], []
    for slot in slots:
        slot = slot if isinstance(slot, tuple) else (slot,)
        where.append((len(flat), [a.shape[0] for a in slot]))
        flat += slot
    return flat, where


def slot_copies(refs, where, s, buf, sem):
    first, sizes = where[s]
    row, out = 0, []
    for k, size in enumerate(sizes):
        out.append(
            pltpu.make_async_copy(
                refs[first + k], buf.at[s % 2, pl.ds(row, size), :], sem.at[s % 2, k]
            )
        )
        row += size
    return out


def take_slot(step, refs, where, buf, sem):
    count = len(where)

    @pl.when(step == 0)
    def _():
        for copy in slot_copies(refs, where, 0, buf, sem):
            copy.start()

    for s in range(count):

        @pl.when(step == s)
        def _(s=s):
            if s + 1 < count:
                for copy in slot_copies(refs, where, s + 1, buf, sem):
                    copy.start()
            for copy in slot_copies(refs, where, s, buf, sem):
                copy.wait()


def give_slot(step, value, refs, buf, sem):
    count = len(refs)
    copies = [pltpu.make_async_copy(buf.at[s % 2], refs[s], sem.at[s % 2]) for s in range(count)]
    for s in range(2, count):

        @pl.when(step == s)
        def _(s=s):
            copies[s - 2].wait()

    buf[step % 2] = value
    for s in range(count):

        @pl.when(step == s)
        def _(s=s):
            copies[s].start()
            if s == count - 1:
                for k in range(max(0, count - 2), count):
                    copies[k].wait()


def cut_kernel(nz, c_ref, q_ref, k_ref, v_ref, *refs):
    up_refs, (down_ref, dense_ref, small_ref, first_ref, second_ref) = refs[:nz], refs[nz:]
    rows, w = q_ref.shape
    fb, half = down_ref.shape[0], rows // 2
    for i, ref in enumerate((q_ref, k_ref, v_ref)):
        first_ref[:rows, i * w : (i + 1) * w] = ref[...]
    for k in range(small_ref.shape[0]):
        first_ref[rows + k // 3 : rows + k // 3 + 1, (k % 3) * LANES : (k % 3 + 1) * LANES] = small_ref[k : k + 1, :]
    second_ref[:fb, :] = down_ref[...]
    for i, ref in enumerate(up_refs):
        for side in range(2):
            at = side * nz * fb + i * fb
            second_ref[fb : fb + half, at : at + fb] = ref[side * half : (side + 1) * half, :]
    second_ref[fb + half :, :] = dense_ref[...]


def cut_weights(c, w_qkv, w_up, w_down, w_dense, small, n, nz):
    shard, dim = w_dense.shape
    w = dim // n
    fb = w_down.shape[0] // n
    column = lambda size, at: pl.BlockSpec((shard, size), lambda i, c, at=at: (0, at + c[0]))
    rows = lambda size: pl.BlockSpec((size, dim), lambda i, c: (c[0], 0))
    whole = lambda shape: pl.BlockSpec(shape, lambda i, c: (0, 0))
    first = (shard + small.shape[0] // 3, 3 * w)
    second = (fb + shard // 2 + shard // n, dim)
    return pl.pallas_call(
        functools.partial(cut_kernel, nz),
        name="cut_weights",
        grid_spec=pltpu.PrefetchScalarGridSpec(
            num_scalar_prefetch=1,
            grid=(1,),
            in_specs=[column(w, i * n) for i in range(3)]
            + [column(fb, i * n) for i in range(nz)]
            + [rows(fb), rows(shard // n), whole(small.shape)],
            out_specs=[whole(first), whole(second)],
        ),
        out_shape=[jax.ShapeDtypeStruct(first, bf16), jax.ShapeDtypeStruct(second, bf16)],
        compiler_params=params(),
        cost_estimate=cost(0, 4 * MIB),
    )(c, *[w_qkv] * 3, *[w_up] * nz, w_down, w_dense, small)


def for_each_shard(nz, z, pieces, put):
    put(z, pieces[0])
    for k in range(1, nz):

        @pl.when(z >= k)
        def _(k=k):
            put(z - k, pieces[k])

        @pl.when(z + k < nz)
        def _(k=k):
            put(z + k, pieces[nz - 1 + k])


def join_first_kernel(nz, z_ref, *refs):
    pieces, (w_ref, v_ref) = refs[: 2 * nz - 1], refs[2 * nz - 1 :]
    z = z_ref[0]
    shard = w_ref.shape[0] // nz
    per = shard // LANES

    def put(t, ref):
        w_ref[pl.ds(pl.multiple_of(t * shard, shard), shard), :] = ref[:shard, :]
        for k in range((ref.shape[0] - shard) * 3):
            row = shard + k // 3
            value = ref[row : row + 1, (k % 3) * LANES : (k % 3 + 1) * LANES].astype(f32)
            at = pl.multiple_of(t * shard + (k % per) * LANES, LANES)
            v_ref[k // per : k // per + 1, pl.ds(at, LANES)] = value

    for_each_shard(nz, z, pieces, put)


def join_first(z, pieces, nz, shard):
    width = pieces[0].shape[1]
    small = (pieces[0].shape[0] - shard) * 3 * LANES // shard
    return pl.pallas_call(
        functools.partial(join_first_kernel, nz),
        name="join_first",
        in_specs=[SMEM] + [pl.BlockSpec(memory_space=pltpu.VMEM)] * len(pieces),
        out_shape=[
            jax.ShapeDtypeStruct((nz * shard, width), bf16),
            jax.ShapeDtypeStruct((small, nz * shard), f32),
        ],
        compiler_params=params(),
        cost_estimate=cost(0, 2 * MIB),
    )(z, *pieces)


def join_second_kernel(nz, z_ref, *refs):
    pieces, (up_ref, down_ref, dense_ref) = refs[: 2 * nz - 1], refs[2 * nz - 1 :]
    z = z_ref[0]
    shard = up_ref.shape[0] // nz
    fl = up_ref.shape[1]
    fb, half = fl // nz, shard // 2
    rest = dense_ref.shape[0] // nz

    def put(t, ref):
        down_ref[pl.ds(pl.multiple_of(t * fb, fb), fb), :] = ref[:fb, :]
        for side in range(2):
            at = pl.multiple_of(t * shard + side * half, half)
            up_ref[pl.ds(at, half), :] = ref[fb : fb + half, side * fl : (side + 1) * fl]
        dense_ref[pl.ds(pl.multiple_of(t * rest, rest), rest), :] = ref[fb + half :, :]

    for_each_shard(nz, z, pieces, put)


def join_second(z, pieces, nz, shard, fl, rest):
    dim = pieces[0].shape[1]
    return pl.pallas_call(
        functools.partial(join_second_kernel, nz),
        name="join_second",
        in_specs=[SMEM] + [pl.BlockSpec(memory_space=pltpu.VMEM)] * len(pieces),
        out_shape=[
            jax.ShapeDtypeStruct((nz * shard, fl), bf16),
            jax.ShapeDtypeStruct((fl, dim), bf16),
            jax.ShapeDtypeStruct((nz * rest, dim), bf16),
        ],
        compiler_params=params(),
        cost_estimate=cost(0, 6 * MIB),
    )(z, *pieces)


def join_dense_kernel(n, nz, c_ref, slots_ref, out_ref):
    c = c_ref[0]
    rows = slots_ref.shape[0] // n
    rest = rows // nz
    for k in range(n):
        for t in range(nz):
            at = pl.multiple_of(t * n * rest + (c ^ EVEN_FIRST[k]) * rest, rest)
            out_ref[pl.ds(at, rest), :] = slots_ref[k * rows + t * rest : k * rows + (t + 1) * rest, :]


def join_dense(c, slots, n, nz):
    return pl.pallas_call(
        functools.partial(join_dense_kernel, n, nz),
        name="join_dense",
        in_specs=[SMEM, pl.BlockSpec(memory_space=pltpu.VMEM)],
        out_shape=jax.ShapeDtypeStruct(slots.shape, bf16),
        compiler_params=params(),
        cost_estimate=cost(0, 4 * MIB),
    )(c, slots)


def ln_qkv_kernel(where, count, *refs):
    slots, (g_ref, s_ref, w_ref, b_ref, h_ref, q_ref, k_ref, v_ref, buf, sem) = refs[:count], refs[count:]
    step = pl.program_id(0)
    take_slot(step, slots, where, buf, sem)
    width = q_ref.shape[1]
    normed, _ = normalize(buf[step % 2].astype(f32))
    h = (normed * g_ref[...] + s_ref[...]).astype(bf16)
    h_ref[...] = h
    p = dot(h, w_ref[...])
    q_ref[...] = (p[:, :width] + b_ref[0:1, :]).astype(bf16)
    k_ref[...] = p[:, width : 2 * width].astype(bf16)
    v_ref[...] = (p[:, 2 * width :] + b_ref[1:2, :]).astype(bf16)


def ln_qkv(slots, gain, shift, weight, bias, blk):
    flat, where = pieces_of(slots)
    n = len(slots)
    rows, dim = n * blk, weight.shape[0]
    width = weight.shape[1] // 3
    full = lambda a: pl.BlockSpec(a.shape, lambda i: (0, 0))
    tok = lambda cols: pl.BlockSpec((blk, cols), lambda i: (i, 0))
    out = lambda cols: jax.ShapeDtypeStruct((rows, cols), bf16)
    return pl.pallas_call(
        functools.partial(ln_qkv_kernel, where, len(flat)),
        name="ln_qkv",
        grid=(n,),
        in_specs=[ANY] * len(flat) + [full(gain), full(shift), full(weight), full(bias)],
        out_specs=[tok(dim), tok(width), tok(width), tok(width)],
        out_shape=[out(dim), out(width), out(width), out(width)],
        scratch_shapes=[pltpu.VMEM((2, blk, dim), bf16), pltpu.SemaphoreType.DMA((2, 2))],
        compiler_params=params(),
        cost_estimate=cost(6 * rows * dim * width, 4 * rows * dim),
    )(*flat, gain, shift, weight, bias)


def attn_fwd_kernel(hp, blk, sc_ref, sl_ref, q_ref, k_ref, v_ref, o_ref, lse_ref):
    i = pl.program_id(0)
    c, b = sc_ref[0], sc_ref[1]
    w = q_ref.shape[1]
    masks = head_masks(hp, w)
    q = q_ref[...] * jnp.asarray(0.125, bf16)
    zero = jnp.zeros_like(q)
    q2 = jnp.concatenate([jnp.where(m, q, zero) for m in masks], axis=0)
    rows = hp * blk

    def tile(j, carry, masked):
        m, l, acc = carry
        at = pl.multiple_of((j ^ c) * blk, blk)
        k = k_ref[pl.ds(at, blk), :]
        v = v_ref[pl.ds(at, blk), :]
        s = lax.dot_general(q2, k, NT, preferred_element_type=f32)
        kpos = j * blk + lax.broadcasted_iota(jnp.int32, (1, blk), 1)
        kf = kpos.astype(f32)
        parts = []
        if masked:
            qpos = i * blk + lax.broadcasted_iota(jnp.int32, (blk, 1), 0)
            allowed = (kpos <= qpos) & ((kpos >= b) | (qpos < b))
        for h in range(hp):
            t = s[h * blk:(h + 1) * blk] + sl_ref[h] * kf
            if masked:
                t = jnp.where(allowed, t, MASKED_SCORE)
            parts.append(t)
        s = jnp.concatenate(parts, axis=0)
        mn = jnp.maximum(m, jnp.max(s, axis=1, keepdims=True))
        p = jnp.exp(s - mn)
        alpha = jnp.exp(m - mn)
        l = l * alpha + jnp.sum(p, axis=1, keepdims=True)
        acc = acc * alpha + jnp.dot(p.astype(bf16), v, preferred_element_type=f32)
        return mn, l, acc

    init = (jnp.full((rows, 1), MASKED_SCORE, f32), jnp.zeros((rows, 1), f32), jnp.zeros((rows, w), f32))
    carry = tile(i, init, True)
    own_first = i * blk < b
    lo = jnp.where(own_first, 0, b // blk)
    mixed = (i + 1) * blk > b
    split = jnp.where(mixed, jnp.minimum((b + blk - 1) // blk, i), lo)
    split = jnp.maximum(split, lo)
    carry = lax.fori_loop(lo, split, lambda j, cy: tile(j, cy, True), carry)
    m, l, acc = lax.fori_loop(split, i, lambda j, cy: tile(j, cy, False), carry)
    out = acc / l
    o = out[:blk]
    for h in range(1, hp):
        o = jnp.where(masks[h], out[h * blk:(h + 1) * blk], o)
    o_ref[...] = o.astype(bf16)
    lse = m + jnp.log(l)
    lse_ref[0] = jnp.transpose(jnp.broadcast_to(lse, (rows, 128)))[0:1, :]

def attn_fwd(sc, sl, q, k, v, blk, hp):
    S, w = q.shape
    nb = S // blk
    return pl.pallas_call(
        functools.partial(attn_fwd_kernel, hp, blk),
        name="attn_fwd",
        grid_spec=pltpu.PrefetchScalarGridSpec(
            num_scalar_prefetch=2, grid=(nb,),
            in_specs=[pl.BlockSpec((blk, w), lambda i, sc, sl: (i ^ sc[0], 0)),
                      pl.BlockSpec((S, w), lambda i, sc, sl: (0, 0)),
                      pl.BlockSpec((S, w), lambda i, sc, sl: (0, 0))],
            out_specs=[pl.BlockSpec((blk, w), lambda i, sc, sl: (i, 0)),
                       pl.BlockSpec((1, 1, hp * blk), lambda i, sc, sl: (i, 0, 0))]),
        out_shape=[jax.ShapeDtypeStruct((S, w), bf16), jax.ShapeDtypeStruct((nb, 1, hp * blk), f32)],
        compiler_params=pltpu.CompilerParams(vmem_limit_bytes=48 * MIB),
        cost_estimate=pl.CostEstimate(flops=4 * S * S * w, bytes_accessed=8 * S * w, transcendentals=S * S * hp // 2),
    )(sc, sl, q, k, v)

def attn_bwd_kernel(hp, blk, sc_ref, sl_ref, q_ref, k_ref, v_ref, do_ref, o_ref, lse_ref, g_ref, gb_ref,
                    q2_ref, do2_ref, delta_ref, dq_ref, bias_ref, dk_ref, dv_ref):
    j = pl.program_id(0)
    nb = pl.num_programs(0)
    c, b = sc_ref[0], sc_ref[1]
    w = k_ref.shape[1]
    rows = hp * blk
    masks = head_masks(hp, w)

    @pl.when(j == 0)
    def _():
        pick = (lax.broadcasted_iota(jnp.int32, (8, w), 1) // HEAD == lax.broadcasted_iota(jnp.int32, (8, w), 0)).astype(f32)
        gb_ref[...] = jnp.zeros_like(gb_ref)
        def prep(i, _):
            at = pl.multiple_of((i ^ c) * blk, blk)
            ai = pl.multiple_of(i * blk, blk)
            q = q_ref[pl.ds(at, blk), :] * jnp.asarray(0.125, bf16)
            do = do_ref[pl.ds(ai, blk), :]
            o = o_ref[pl.ds(ai, blk), :]
            zero = jnp.zeros_like(q)
            for h in range(hp):
                q2_ref[i, h * blk:(h + 1) * blk, :] = jnp.where(masks[h], q, zero)
                do2_ref[i, h * blk:(h + 1) * blk, :] = jnp.where(masks[h], do, zero)
            prod = do.astype(f32) * o.astype(f32)
            d = lax.dot_general(pick, prod, NT, preferred_element_type=f32, precision=lax.Precision.HIGHEST)
            for h in range(hp):
                delta_ref[i, :, h * blk:(h + 1) * blk] = d[h:h + 1, :]
            dq_ref[i] = jnp.zeros((blk, w), f32)
            return 0
        lax.fori_loop(0, nb, prep, 0)

    k = k_ref[...]
    v = v_ref[...]
    kcol = j * blk + lax.broadcasted_iota(jnp.int32, (blk, 1), 0)
    kf = kcol.astype(f32)
    for h in range(hp):
        bias_ref[:, h * blk:(h + 1) * blk] = jnp.broadcast_to(kf * sl_ref[h], (blk, blk))
    dk_ref[...] = jnp.zeros_like(dk_ref)
    dv_ref[...] = jnp.zeros_like(dv_ref)

    def tile(i, masked):
        q2 = q2_ref[i]
        do2 = do2_ref[i]
        s = lax.dot_general(k, q2, NT, preferred_element_type=f32)
        p = jnp.exp(s + bias_ref[...] - lse_ref[i])
        if masked:
            r = lax.broadcasted_iota(jnp.int32, (1, rows), 1)
            qpos = i * blk + (r & (blk - 1))
            allowed = (kcol <= qpos) & ((kcol >= b) | (qpos < b))
            p = jnp.where(allowed, p, 0.0)
        dp = lax.dot_general(v, do2, NT, preferred_element_type=f32)
        ds = (p * (dp - delta_ref[i])).astype(bf16)
        dv_ref[...] += jnp.dot(p.astype(bf16), do2, preferred_element_type=f32)
        dk_ref[...] += jnp.dot(ds, q2, preferred_element_type=f32)
        dq2 = lax.dot_general(ds, k, TN, preferred_element_type=f32)
        d = dq2[:blk]
        for h in range(1, hp):
            d = jnp.where(masks[h], dq2[h * blk:(h + 1) * blk], d)
        dq_ref[i] += d

    tile(j, True)
    hi = jnp.where((j + 1) * blk <= b, (b + blk - 1) // blk, nb)
    split = jnp.where(j * blk < b, jnp.maximum(b // blk, j + 1), hi)
    split = jnp.minimum(split, hi)
    lax.fori_loop(j + 1, split, lambda i, _: (tile(i, False), 0)[1], 0)
    lax.fori_loop(jnp.maximum(split, j + 1), hi, lambda i, _: (tile(i, True), 0)[1], 0)
    dq = dq_ref[j] * 0.125
    dv = dv_ref[...]
    g_ref[:, 0:w] = dq.astype(bf16)
    g_ref[:, w:2 * w] = dk_ref[...].astype(bf16)
    g_ref[:, 2 * w:3 * w] = dv.astype(bf16)
    gb_ref[0:1, :] += jnp.sum(dq, axis=0, keepdims=True)
    gb_ref[1:2, :] += jnp.sum(dv, axis=0, keepdims=True)

def attn_bwd(sc, sl, q, k, v, do, o, lse, blk, hp):
    S, w = q.shape
    nb = S // blk
    full = lambda shape: pl.BlockSpec(shape, lambda j, sc, sl: (0,) * len(shape))
    slot = lambda width: pl.BlockSpec((blk, width), lambda j, sc, sl: (j ^ sc[0], 0))
    return pl.pallas_call(
        functools.partial(attn_bwd_kernel, hp, blk),
        name="attn_bwd",
        grid_spec=pltpu.PrefetchScalarGridSpec(
            num_scalar_prefetch=2, grid=(nb,),
            in_specs=[full((S, w)), slot(w), slot(w), full((S, w)), full((S, w)), full((nb, 1, hp * blk))],
            out_specs=[slot(3 * w), full((8, w))],
            scratch_shapes=[pltpu.VMEM((nb, hp * blk, w), bf16), pltpu.VMEM((nb, hp * blk, w), bf16),
                            pltpu.VMEM((nb, 1, hp * blk), f32), pltpu.VMEM((nb, blk, w), f32),
                            pltpu.VMEM((blk, hp * blk), f32), pltpu.VMEM((blk, w), f32), pltpu.VMEM((blk, w), f32)]),
        out_shape=[jax.ShapeDtypeStruct((S, 3 * w), bf16), jax.ShapeDtypeStruct((8, w), f32)],
        compiler_params=pltpu.CompilerParams(vmem_limit_bytes=48 * MIB),
        cost_estimate=pl.CostEstimate(flops=10 * S * S * w, bytes_accessed=16 * S * w, transcendentals=S * S * hp // 2),
    )(sc, sl, q, k, v, do, o, lse)


def dense_ln_kernel(x_ref, o_ref, w_ref, v_ref, y_ref, h_ref):
    y = x_ref[...].astype(f32) + (dot(o_ref[...], w_ref[...]) + v_ref[2:3, :])
    y_ref[...] = y
    normed, _ = normalize(y)
    h_ref[...] = (normed * v_ref[3:4, :] + v_ref[4:5, :]).astype(bf16)


def dense_ln(x, o, weight, vectors):
    rows, dim = x.shape
    return pl.pallas_call(
        dense_ln_kernel,
        name="dense_ln",
        out_shape=[jax.ShapeDtypeStruct((rows, dim), f32), jax.ShapeDtypeStruct((rows, dim), bf16)],
        compiler_params=params(),
        cost_estimate=cost(2 * rows * dim * dim, 2 * dim * dim + 12 * rows * dim),
    )(x, o, weight, vectors)


def mlp_kernel(where, count, outs, extra, *refs):
    h_slots, cot_slots = refs[:count], refs[count : 2 * count]
    u_ref, d_ref, b_ref = refs[2 * count : 2 * count + 3]
    refs = refs[2 * count + 3 + extra :]
    hall_ref, call_ref, z_ref, du_ref, gb_ref = refs[:5]
    dh_slots = refs[5 : 5 + outs]
    hbuf, hsem, cbuf, csem, dbuf, dsem = refs[5 + outs :]
    step = pl.program_id(0)
    take_slot(step, h_slots, where, hbuf, hsem)
    take_slot(step, cot_slots, where, cbuf, csem)
    h, cot = hbuf[step % 2], cbuf[step % 2]
    hall_ref[...] = h
    call_ref[...] = cot
    value, deriv = gelu_pair(dot(h, u_ref[...]) + b_ref[...])
    z_ref[...] = value.astype(bf16)
    du = dot_nt(cot, d_ref[...]) * deriv

    @pl.when(step == 0)
    def _():
        gb_ref[...] = jnp.zeros_like(gb_ref)

    gb_ref[...] += rowsum(du)
    du = du.astype(bf16)
    du_ref[...] = du
    give_slot(step, dot_nt(du, u_ref[...]).astype(bf16), dh_slots, dbuf, dsem)


def mlp(h_slots, cot_slots, up, down, bias, blk, n, first, so_far=None):
    flat, where = pieces_of(h_slots)
    cot_flat, _ = pieces_of(cot_slots)
    count = len(h_slots)
    dim, width = up.shape
    full = lambda a: pl.BlockSpec(a.shape, lambda i: (0, 0))
    tok = lambda cols: pl.BlockSpec((blk, cols), lambda i: (first + i, 0))
    out = lambda rows, cols: jax.ShapeDtypeStruct((rows, cols), bf16)
    so_far = list(so_far or ())
    at = 2 * len(flat) + 3
    res = pl.pallas_call(
        functools.partial(mlp_kernel, where, len(flat), count, len(so_far)),
        name=f"mlp_{first}",
        grid=(count,),
        in_specs=[ANY] * (2 * len(flat)) + [full(up), full(down), full(bias)] + [ANY] * len(so_far),
        out_specs=[tok(dim), tok(dim), tok(width), tok(width), pl.BlockSpec((1, width), lambda i: (0, 0))] + [ANY] * count,
        out_shape=[out(n * blk, dim), out(n * blk, dim), out(n * blk, width), out(n * blk, width), jax.ShapeDtypeStruct((1, width), f32)]
        + [out(blk, dim)] * count,
        scratch_shapes=[
            pltpu.VMEM((2, blk, dim), bf16),
            pltpu.SemaphoreType.DMA((2, 2)),
            pltpu.VMEM((2, blk, dim), bf16),
            pltpu.SemaphoreType.DMA((2, 2)),
            pltpu.VMEM((2, blk, dim), bf16),
            pltpu.SemaphoreType.DMA((2,)),
        ],
        input_output_aliases={at + k: k for k in range(len(so_far))},
        compiler_params=params(),
        cost_estimate=cost(6 * count * blk * dim * width, count * blk * dim * 16, count * blk * width),
    )(*flat, *cot_flat, up, down, bias, *so_far)
    return res[:4], res[4], res[5:]


def to_slots_kernel(count, transposed, a_ref, w_ref, *refs):
    slots, (buf, sem) = refs[:count], refs[count:]
    product = (dot_nt if transposed else dot)(a_ref[...], w_ref[...])
    give_slot(pl.program_id(0), product.astype(bf16), slots, buf, sem)


def to_slots(a, weight, blk, transposed=False):
    count, dim = a.shape[0] // blk, weight.shape[0 if transposed else 1]
    return pl.pallas_call(
        functools.partial(to_slots_kernel, count, transposed),
        name="to_slots",
        grid=(count,),
        in_specs=[pl.BlockSpec((blk, a.shape[1]), lambda i: (i, 0)), pl.BlockSpec(weight.shape, lambda i: (0, 0))],
        out_specs=[ANY] * count,
        out_shape=[jax.ShapeDtypeStruct((blk, dim), bf16)] * count,
        scratch_shapes=[pltpu.VMEM((2, blk, dim), bf16), pltpu.SemaphoreType.DMA((2,))],
        compiler_params=params(),
        cost_estimate=cost(2 * a.shape[0] * a.shape[1] * dim, 2 * a.shape[0] * (a.shape[1] + dim)),
    )(a, weight)


def summed(parts):
    total = parts[0][...].astype(f32)
    if len(parts) == 1:
        return total
    near2, last2, near4, last4 = [ref[...].astype(f32) for ref in parts[1:]]
    return total + jnp.concatenate([last2 + near4, near2 + last4], axis=0)


def ln2_back_kernel(count, *refs):
    parts, (y_ref, cot_ref, w_ref, v_ref, dy_ref, dyb_ref, do_ref, gs_ref) = refs[:count], refs[count:]
    normed, inv_std = normalize(y_ref[...])
    dh = summed(parts)
    dy = cot_ref[...].astype(f32) + norm_backward(dh, normed, inv_std, v_ref[3:4, :])
    dy_ref[...] = dy
    dyb = dy.astype(bf16)
    dyb_ref[...] = dyb
    do_ref[...] = dot_nt(dyb, w_ref[...]).astype(bf16)
    gs_ref[0:1, :] = rowsum(dy)
    gs_ref[1:2, :] = rowsum(dh * normed)
    gs_ref[2:3, :] = rowsum(dh)
    gs_ref[3:4, :] = rowsum(cot_ref[...].astype(f32))


def ln2_back(parts, y, cot, weight, vectors):
    rows, dim = y.shape
    return pl.pallas_call(
        functools.partial(ln2_back_kernel, len(parts)),
        name="ln2_back",
        out_shape=[
            jax.ShapeDtypeStruct((rows, dim), f32),
            jax.ShapeDtypeStruct((rows, dim), bf16),
            jax.ShapeDtypeStruct((rows, dim), bf16),
            jax.ShapeDtypeStruct((4, dim), f32),
        ],
        compiler_params=params(),
        cost_estimate=cost(2 * rows * dim * dim, 2 * dim * dim + 20 * rows * dim),
    )(*parts, y, cot, weight, vectors)


def finish_kernel(count, *refs):
    parts, (y_ref, v_ref, out_ref) = refs[:count], refs[count:]
    out_ref[...] = y_ref[...] + (summed(parts) + v_ref[5:6, :])


def finish_out(parts, y, vectors):
    return pl.pallas_call(
        functools.partial(finish_kernel, len(parts)),
        name="finish_out",
        out_shape=jax.ShapeDtypeStruct(y.shape, f32),
        compiler_params=params(),
        cost_estimate=cost(y.size, 10 * y.size),
    )(*parts, y, vectors)


def ln1_back_kernel(count, *refs):
    parts, (x_ref, dy_ref, v_ref, out_ref) = refs[:count], refs[count:]
    normed, inv_std = normalize(x_ref[...].astype(f32))
    out_ref[...] = dy_ref[...] + norm_backward(summed(parts), normed, inv_std, v_ref[0:1, :])


def ln1_back(parts, x, dy, vectors):
    return pl.pallas_call(
        functools.partial(ln1_back_kernel, len(parts)),
        name="ln1_back",
        out_shape=jax.ShapeDtypeStruct(dy.shape, f32),
        compiler_params=params(),
        cost_estimate=cost(20 * dy.size, 14 * dy.size),
    )(*parts, x, dy, vectors)


def dh1_kernel(where, count, outs, *refs):
    x_slots, (g_ref, w_ref, gs_ref) = refs[:count], refs[count : count + 3]
    slots, (xbuf, xsem, buf, sem) = refs[count + 3 : count + 3 + outs], refs[count + 3 + outs :]
    step = pl.program_id(0)
    take_slot(step, x_slots, where, xbuf, xsem)
    dh = dot_nt(g_ref[...], w_ref[...])
    normed, _ = normalize(xbuf[step % 2].astype(f32))

    @pl.when(step == 0)
    def _():
        gs_ref[...] = jnp.zeros_like(gs_ref)

    gs_ref[0:1, :] += rowsum(dh * normed)
    gs_ref[1:2, :] += rowsum(dh)
    give_slot(step, dh.astype(bf16), slots, buf, sem)


def dh1_part(g, weight, x_slots, blk):
    flat, where = pieces_of(x_slots)
    n, dim = len(x_slots), weight.shape[0]
    res = pl.pallas_call(
        functools.partial(dh1_kernel, where, len(flat), n),
        name="dh1_part",
        grid=(n,),
        in_specs=[ANY] * len(flat)
        + [pl.BlockSpec((blk, g.shape[1]), lambda i: (i, 0)), pl.BlockSpec(weight.shape, lambda i: (0, 0))],
        out_specs=[pl.BlockSpec((2, dim), lambda i: (0, 0))] + [ANY] * n,
        out_shape=[jax.ShapeDtypeStruct((2, dim), f32)] + [jax.ShapeDtypeStruct((blk, dim), bf16)] * n,
        scratch_shapes=[
            pltpu.VMEM((2, blk, dim), bf16),
            pltpu.SemaphoreType.DMA((2, 2)),
            pltpu.VMEM((2, blk, dim), bf16),
            pltpu.SemaphoreType.DMA((2,)),
        ],
        compiler_params=params(),
        cost_estimate=cost(2 * n * blk * dim * g.shape[1], 4 * n * blk * dim),
    )(*flat, g, weight)
    return res[0], res[1:]


def shard_order(i):
    return (i % 2) * 2 + i // 2


def grad_ff_kernel(z_ref, act_ref, cot_ref, h_ref, du_ref, out_ref):
    fb, half = act_ref.shape[1], h_ref.shape[1] // 2
    fl = du_ref.shape[1]
    out_ref[0, :fb, :] = dot_tn(act_ref[...], cot_ref[...]).astype(bf16)
    up = dot_tn(h_ref[...], du_ref[...]).astype(bf16)
    for side in range(2):
        out_ref[0, fb:, side * fl : (side + 1) * fl] = up[side * half : (side + 1) * half, :]


def grad_ff(z, act, cot, h, du, nz):
    rows, dim = cot.shape
    fl = act.shape[1]
    fb, shard = fl // nz, dim // nz
    full = lambda a: pl.BlockSpec(a.shape, lambda i, z: (0, 0))
    pick = lambda size: pl.BlockSpec((rows, size), lambda i, z: (0, z[0] ^ shard_order(i)))
    height = fb + shard // 2
    return pl.pallas_call(
        grad_ff_kernel,
        name="grad_ff",
        grid_spec=pltpu.PrefetchScalarGridSpec(
            num_scalar_prefetch=1,
            grid=(nz,),
            in_specs=[pick(fb), full(cot), pick(shard), full(du)],
            out_specs=pl.BlockSpec((1, height, dim), lambda i, z: (i, 0, 0)),
        ),
        out_shape=jax.ShapeDtypeStruct((nz, height, dim), bf16),
        compiler_params=params(),
        cost_estimate=cost(4 * rows * dim * fl, 2 * rows * (2 * dim + 2 * fl)),
    )(z, act, cot, h, du)


def grad_qkv_kernel(z_ref, h_ref, g_ref, s_ref, out_ref):
    w = g_ref.shape[1] // 3
    shard = h_ref.shape[1]
    grad = dot_tn(h_ref[...], g_ref[...]).astype(bf16)
    for i in range(3):
        out_ref[0, i * shard : (i + 1) * shard, :] = grad[:, i * w : (i + 1) * w]
    out_ref[0, 3 * shard :, :] = s_ref[0].astype(bf16)


def grad_qkv(z, h, g, small, nz):
    rows, dim = h.shape
    shard, w = dim // nz, g.shape[1] // 3
    height = 3 * shard + small.shape[1]
    return pl.pallas_call(
        grad_qkv_kernel,
        name="grad_qkv",
        grid_spec=pltpu.PrefetchScalarGridSpec(
            num_scalar_prefetch=1,
            grid=(nz,),
            in_specs=[
                pl.BlockSpec((rows, shard), lambda i, z: (0, z[0] ^ shard_order(i))),
                pl.BlockSpec(g.shape, lambda i, z: (0, 0)),
                pl.BlockSpec((1,) + small.shape[1:], lambda i, z: (z[0] ^ shard_order(i), 0, 0)),
            ],
            out_specs=pl.BlockSpec((1, height, w), lambda i, z: (i, 0, 0)),
        ),
        out_shape=jax.ShapeDtypeStruct((nz, height, w), bf16),
        compiler_params=params(),
        cost_estimate=cost(6 * rows * dim * w, 2 * rows * (dim + 3 * w)),
    )(z, h, g, small)


def grad_dense_kernel(n, nz, at_ref, o_ref, d_ref, out_ref, acc_ref):
    c, z = at_ref[0], at_ref[1]
    acc_ref[...] = dot_tn(o_ref[...], d_ref[...])
    rest = acc_ref.shape[0] // (n * nz)
    for k in range(n):
        for i in range(nz):
            at = (z ^ shard_order(i)) * n * rest + (c ^ EVEN_FIRST[k]) * rest
            out_ref[(k * nz + i) * rest : (k * nz + i + 1) * rest, :] = acc_ref[
                pl.ds(pl.multiple_of(at, rest), rest), :
            ].astype(bf16)


def grad_dense(at, o, dyb, n, nz):
    dim = o.shape[1]
    return pl.pallas_call(
        functools.partial(grad_dense_kernel, n, nz),
        name="grad_dense",
        in_specs=[SMEM] + [pl.BlockSpec(memory_space=pltpu.VMEM)] * 2,
        out_shape=jax.ShapeDtypeStruct((dim, dim), bf16),
        scratch_shapes=[pltpu.VMEM((dim, dim), f32)],
        compiler_params=params(),
        cost_estimate=cost(2 * o.shape[0] * dim * dim, 2 * dim * dim),
    )(at, o, dyb)


def small_kernel(n, nz, c_ref, s1_ref, s2_ref, qv_ref, up_ref, out_ref):
    c = c_ref[0]
    out_ref[...] = jnp.zeros_like(out_ref)
    shard = s1_ref.shape[1] // nz
    per = shard // LANES
    for t in range(nz):
        for v in range(6):
            ref, row = (s1_ref, v) if v < 2 else (s2_ref, v - 2)
            for e in range(per):
                at = t * shard + e * LANES
                out_ref[t, v * per + e : v * per + e + 1, :] = ref[row : row + 1, at : at + LANES]
        out_ref[t, pl.ds(8 * per + c, 1), :] = up_ref[:, t * LANES : (t + 1) * LANES]
    row = 6 * per + c % (2 * per)
    out_ref[c // (2 * per), pl.ds(row, 1), :] = qv_ref[0:1, :]
    out_ref[nz // 2 + c // (2 * per), pl.ds(row, 1), :] = qv_ref[1:2, :]


def small_grads(c, sums1, sums2, qv, up, n, nz):
    dim = sums1.shape[1]
    return pl.pallas_call(
        functools.partial(small_kernel, n, nz),
        name="small_grads",
        in_specs=[SMEM] + [pl.BlockSpec(memory_space=pltpu.VMEM)] * 4,
        out_shape=jax.ShapeDtypeStruct((nz, 12 * dim // nz // LANES, LANES), f32),
        compiler_params=params(),
        cost_estimate=cost(0, 1 << 16),
    )(c, sums1, sums2, qv, up)


def spread_kernel(where, count, outs, c_ref, *refs):
    slots, refs = refs[:count], refs[count:]
    out_refs, (buf, sem, wide, osem) = refs[: len(outs)], refs[len(outs) :]
    c = c_ref[0]
    step = pl.program_id(0)
    last = pl.num_programs(0) - 1
    take_slot(step, slots, where, buf, sem)
    mine = c ^ step

    def copies(slot, block_of):
        done = []
        for ref, blocks in zip(out_refs, outs, strict=True):
            for row, col, height, width, trow, tcol, by_row in blocks:
                if by_row:
                    target = ref.at[pl.ds(pl.multiple_of(trow + block_of * height, 8), height), pl.ds(tcol, width)]
                else:
                    target = ref.at[pl.ds(trow, height), pl.ds(pl.multiple_of(tcol + block_of * width, LANES), width)]
                source = wide.at[slot, pl.ds(row, height), pl.ds(col, width)]
                done.append(pltpu.make_async_copy(source, target, osem.at[slot, len(done)]))
        return done

    @pl.when(step >= 2)
    def _():
        for copy in copies(step % 2, mine):
            copy.wait()

    wide[step % 2] = buf[step % 2].astype(f32)
    for copy in copies(step % 2, mine):
        copy.start()

    @pl.when(step == last)
    def _():
        for slot in range(2):
            for copy in copies(slot, mine):
                copy.wait()


def spread(c, slots, outs, shapes, name):
    flat, where = pieces_of(slots)
    n = len(slots)
    height = sum(where[0][1])
    width = flat[0].shape[1]
    return pl.pallas_call(
        functools.partial(spread_kernel, where, len(flat), outs),
        name=name,
        grid=(n,),
        in_specs=[SMEM] + [ANY] * len(flat),
        out_specs=[ANY] * len(shapes),
        out_shape=[jax.ShapeDtypeStruct(shape, f32) for shape in shapes],
        scratch_shapes=[
            pltpu.VMEM((2, height, width), bf16),
            pltpu.SemaphoreType.DMA((2, 2)),
            pltpu.VMEM((2, height, width), f32),
            pltpu.SemaphoreType.DMA((2, sum(len(blocks) for blocks in outs))),
        ],
        compiler_params=params(),
        cost_estimate=cost(0, 6 * n * height * width),
    )(c, *flat)


def swap(x, n, bit, axis="ctx"):
    return lax.ppermute(x, axis, [(i, i ^ bit) for i in range(n)])


def gather_slots(x, n):
    if n != 8:
        slots = {0: x}
        bit = n >> 1
        while bit:
            for s in list(slots):
                slots[s ^ bit] = swap(slots[s], n, bit)
            bit >>= 1
        return [slots[s] for s in range(n)]
    half = x.shape[0] // 32 * 16
    a, b = swap(x, n, 2), swap(x, n, 4)
    far = (swap(a[:half], n, 4), swap(b[half:], n, 2))
    slots = [x, None, a, None, b, None, far, None]
    for s in range(0, 6, 2):
        slots[s + 1] = swap(slots[s], n, 1)
    slots[7] = tuple(swap(part, n, 1) for part in far)
    return slots


def add16(a, b):
    return (a.astype(f32) + b.astype(f32)).astype(bf16)


def scatter_slots(parts, n):
    if n != 8:
        parts = dict(enumerate(parts))
        bit = 1
        while bit < n:
            for s in [s for s in parts if not s & bit]:
                parts[s] = add16(parts[s], swap(parts.pop(s | bit), n, bit))
            bit <<= 1
        return [parts[0]]
    half = parts[0].shape[0] // 2
    q6, q2, q4, q0 = [add16(parts[s], swap(parts[s + 1], n, 1)) for s in (6, 2, 4, 0)]
    far2, far4 = swap(q6[:half], n, 4), swap(q6[half:], n, 2)
    near2 = swap(q2[half:], n, 2)
    near4 = swap(q4[:half], n, 4)
    last2 = swap(add16(q2[:half], far2), n, 2)
    last4 = swap(add16(q4[half:], far4), n, 4)
    return [q0, near2, last2, near4, last4]


def chain(x, nz, gate=None):
    up = [(i, i + 1) for i in range(nz - 1)]
    down = [(i + 1, i) for i in range(nz - 1)]
    below, above = [x], [x]
    for _ in range(nz - 1):
        below.append(lax.ppermute(below[-1], "fsdp", up))
        above.append(lax.ppermute(above[-1], "fsdp", down))
    return below + above[1:]


def over_shards(x, nz):
    kept = add16(x[:2], swap(x[2:], nz, 1, "fsdp"))
    return add16(kept[0], swap(kept[1], nz, 2, "fsdp"))


def after(x, *others):
    return lax.optimization_barrier((x, *others))[0]


def weights_fast(c, z, w_qkv, b_qv, w_dense, w_up, b_up, w_down, small, n, nz):
    shard, dim = w_dense.shape
    fl = w_down.shape[0] // n * nz
    w = dim // n
    first, second = cut_weights(c, w_qkv, w_up, w_down, w_dense, small.reshape(-1, LANES), n, nz)
    pieces = chain(first, nz)
    wq, vectors = join_first(z, pieces, nz, shard)
    second = after(second, pieces[nz - 2], pieces[2 * nz - 3])
    pieces = chain(second, nz)
    wu, wn, dense = join_second(z, pieces, nz, shard, fl, shard // n)
    per = 2 * shard // w
    at = lambda first: (6 + (first + c[0]) % per * w // shard, (first + c[0]) // per * shard + (first + c[0]) % per * w % shard)
    bias_qv = jnp.concatenate([lax.dynamic_slice(vectors, at(k * n), (1, w)) for k in range(2)], axis=0)
    bias_up = lax.dynamic_slice(vectors.reshape(-1, nz, shard // LANES, LANES), (8 + c[0] // 2, 0, c[0] % 2, 0), (1, nz, 1, LANES)).reshape(1, fl)
    return wq, wu, wn, dense, vectors, bias_qv, bias_up


def on_device(
    hidden_in,
    seq_ids,
    ln1_gain,
    ln1_bias,
    w_qkv,
    b_qv,
    w_dense,
    b_dense,
    ln2_gain,
    ln2_bias,
    w_up,
    b_up,
    w_down,
    b_down,
    cotangent,
    n,
    nz,
):
    fast = n == 8 and nz == 4 and w_down.shape[0] // n == LANES
    c = lax.axis_index("ctx").astype(jnp.int32)
    z = lax.axis_index("fsdp").astype(jnp.int32)
    c1, z1 = c.reshape(1), z.reshape(1)
    rows, dim = hidden_in.shape
    seq_len = seq_ids.shape[1]
    shard = dim // nz
    hp = HEADS // n
    w = hp * HEAD
    fb = w_down.shape[0] // n
    fl = nz * fb
    ff = fl * n
    both = ("fsdp", "ctx")

    small = jnp.concatenate([ln1_gain, ln1_bias, b_dense, ln2_gain, ln2_bias, b_down, b_qv, b_up])
    if fast:
        wq, wu, wn, dense, vectors, bias_qv, bias_up = weights_fast(
            c1, z1, w_qkv, b_qv, w_dense, w_up, b_up, w_down, small, n, nz
        )
    else:
        small = lax.all_gather(small, "fsdp", axis=0, tiled=False).astype(f32)
        vectors = small[:, : 6 * shard].reshape(nz, 6, shard).transpose(1, 0, 2).reshape(6, dim)
        bias_qv = small[:, 6 * shard : 8 * shard].reshape(2, n, w)
        bias_qv = lax.dynamic_index_in_dim(bias_qv, c, 1, keepdims=False)
        bias_up = small[:, 8 * shard :].reshape(nz, n, fb)
        bias_up = lax.dynamic_index_in_dim(bias_up, c, 1, keepdims=False).reshape(1, fl)
        wq = lax.dynamic_index_in_dim(w_qkv.reshape(shard, 3, n, w), c, 2, keepdims=False).reshape(shard, 3 * w)
        wq = lax.all_gather(wq, "fsdp", axis=0, tiled=True)
        wu = lax.dynamic_index_in_dim(w_up.reshape(shard, nz, n, fb), c, 2, keepdims=False).reshape(shard, fl)
        wu = lax.all_gather(wu, "fsdp", axis=0, tiled=True)
        wn = lax.all_gather(lax.dynamic_slice_in_dim(w_down, c * fb, fb, 0), "fsdp", axis=0, tiled=True)
        wd = lax.all_gather(w_dense, "fsdp", axis=0, tiled=True)

    seg = seq_ids[0]
    boundary = jnp.sum((seg == seg[0]).astype(jnp.int32))
    sc = jnp.stack([c, boundary])
    head = (c * hp + 1 + jnp.arange(hp)).astype(f32)
    slopes = jnp.exp2(-8.0 * head / HEADS) * (8.0 / seq_len)

    x_slots = gather_slots(hidden_in, n)
    tail = lambda slots: slots[n - 2][0] if n == 8 else slots[n - 1]
    if fast:
        dense = after(dense, tail(x_slots))
        for bit in (2, 4, 1):
            dense = jnp.concatenate([dense, swap(dense, n, bit)], axis=0)
        wd = join_dense(c1, dense, n, nz)
    cot_slots = gather_slots(after(cotangent, tail(x_slots)), n)

    h1, q, k, v = ln_qkv(x_slots, vectors[0:1], vectors[1:2], wq, bias_qv, rows)
    o, lse = attn_fwd(sc, slopes, q, k, v, rows, hp)
    o_own = lax.all_to_all(o, "ctx", split_axis=0, concat_axis=1, tiled=True)
    y1, h2 = dense_ln(hidden_in, o_own, wd, vectors)

    h2_slots = gather_slots(h2, n)
    early = n - 2
    alls, gb_a, dh_a = mlp(h2_slots[:early], cot_slots[:early], wu, wn, bias_up, rows, n, 0)
    alls, gb_b, dh_b = mlp(h2_slots[early:], cot_slots[early:], wu, wn, bias_up, rows, n, early, alls)
    h2_all, cot_all, act, du = alls
    dh2_parts = scatter_slots(list(dh_a) + list(dh_b), n)
    dy, dyb, do, sums2 = ln2_back(dh2_parts, y1, cotangent, wd, vectors)
    do_heads = lax.all_to_all(do, "ctx", split_axis=1, concat_axis=0, tiled=True)

    g, gb_qv = attn_bwd(sc, slopes, q, k, v, do_heads, o, lse, rows, hp)
    sums1, dh1_slots = dh1_part(g, wq, x_slots, rows)
    dh1_parts = scatter_slots(dh1_slots, n)
    grad_input = ln1_back(dh1_parts, hidden_in, dy, vectors)

    out_slots = to_slots(after(act, do_heads), wn, rows)
    block_out = finish_out(scatter_slots(out_slots, n), y1, vectors)

    if fast:
        g_ff = over_shards(grad_ff(z1, act, cot_all, h2_all, du, nz), nz)
        g_dense = grad_dense(jnp.stack([c, z]), o_own, after(dyb, do_heads), n, nz)
        for bit in (1, 4, 2):
            size = g_dense.shape[0] // 2
            g_dense = add16(g_dense[:size], swap(g_dense[size:], n, bit))
        g_dense = over_shards(g_dense.reshape(nz, shard // n, dim), nz)
        small = small_grads(c1, sums1, sums2, gb_qv, gb_a + gb_b, n, nz)
        g_qkv = over_shards(grad_qkv(z1, h1, g, small, nz), nz)
        bundle = after(jnp.concatenate([g_ff, g_dense], axis=0), dh1_slots[0])
        half = shard // 2
        g_down, g_up, g_dense = spread(
            c1,
            gather_slots(bundle, n),
            [
                [(0, 0, fb, dim, 0, 0, True)],
                [
                    (fb, side * fl + t * fb, half, fb, side * half, t * n * fb, False)
                    for side in range(2)
                    for t in range(nz)
                ],
                [(fb + half, 0, shard // n, dim, 0, 0, True)],
            ],
            [(n * fb, dim), (shard, ff), (shard, dim)],
            "spread_ff",
        )
        qkv_slots = gather_slots(g_qkv, n)
        (g_qkv,) = spread(
            c1,
            qkv_slots,
            [[(i * shard, 0, shard, w, 0, i * dim, False) for i in range(3)]],
            [(shard, 3 * dim)],
            "spread_qkv",
        )
        join = lambda slot: slot if not isinstance(slot, tuple) else jnp.concatenate(slot, axis=0)
        total = sum(join(slot)[3 * shard :].astype(f32) for slot in qkv_slots).reshape(-1)
    else:
        reduce = lambda a: lax.psum(
            lax.psum_scatter(a.astype(bf16), "fsdp", scatter_dimension=0, tiled=True), "ctx"
        ).astype(f32)
        every = lambda a, axis: lax.all_gather(
            lax.psum_scatter(a.astype(bf16), "fsdp", scatter_dimension=0, tiled=True), "ctx", axis=axis, tiled=True
        ).astype(f32)
        g_down = every(dot_tn(act, cot_all), 0)
        g_up = dot_tn(h2_all, du).reshape(dim, nz, fb)
        g_up = every(g_up, 2).reshape(shard, ff)
        g_dense = reduce(dot_tn(o_own, dyb))
        g_qkv = every(dot_tn(h1, g).reshape(dim, 3, w), 2).reshape(shard, 3 * dim)
        own = lambda a, lead: lax.dynamic_update_index_in_dim(jnp.zeros((lead, n, a.shape[-1]), f32), a, c, 1)
        by_shard = lambda a: a.reshape(-1, nz, shard).transpose(1, 0, 2).reshape(nz, -1)
        flat = jnp.concatenate(
            [
                by_shard(sums1),
                by_shard(sums2),
                own(gb_qv[:2], 2).reshape(nz, 2 * shard),
                own((gb_a + gb_b).reshape(nz, fb), nz).reshape(nz, n * fb),
            ],
            axis=1,
        )
        total = lax.dynamic_index_in_dim(lax.psum(flat, both), z, 0, keepdims=False)
    piece = lambda i, k=1: total[i * shard : (i + k) * shard]
    return (
        block_out,
        grad_input,
        piece(0),
        piece(1),
        g_qkv,
        piece(6, 2),
        g_dense,
        piece(2),
        piece(3),
        piece(4),
        g_up,
        total[8 * shard :],
        g_down,
        piece(5),
    )


def solution(mesh):
    n, nz = mesh.shape["ctx"], mesh.shape["fsdp"]
    shard = P("fsdp")
    mat = P("fsdp", None)
    tokens = P(("fsdp", "ctx"), None)
    return jax.shard_map(
        functools.partial(on_device, n=n, nz=nz),
        mesh=mesh,
        in_specs=(tokens, mat, shard, shard, mat, shard, mat, shard, shard, shard, mat, shard, mat, shard, tokens),
        out_specs=(tokens, tokens, shard, shard, mat, shard, mat, shard, shard, shard, mat, shard, mat, shard),
        check_vma=False,
    )
```

```python
import functools
import math

import jax
import jax.numpy as jnp
from jax import lax
from jax.experimental import pallas as pl
from jax.experimental.pallas import tpu as pltpu
from jax.sharding import PartitionSpec as P


HEADS = 16
HEAD = 64
LANES = 128
NORM_EPSILON = 1e-05
MASKED_SCORE = -1e30
GELU_SCALE = math.sqrt(2.0 / math.pi)
NT = (((1,), (1,)), ((), ()))
TN = (((0,), (0,)), ((), ()))
f32 = jnp.float32
bf16 = jnp.bfloat16
MIB = 1 << 20
ROW, SHARDS = "ctx", "fsdp"
ANY = pl.BlockSpec(memory_space=pl.ANY)
SMEM = pl.BlockSpec(memory_space=pltpu.SMEM)
VMEM = pl.BlockSpec(memory_space=pltpu.VMEM)


def params(limit=20):
    return pltpu.CompilerParams(vmem_limit_bytes=limit * MIB)


def cost(flops, moved, hard=0):
    return pl.CostEstimate(flops=flops, bytes_accessed=moved, transcendentals=hard)


def head_masks(hp, w):
    lane = lax.broadcasted_iota(jnp.int32, (1, w), 1)
    return [(lane // HEAD) == h for h in range(hp)]


def normalize(x):
    centre = x - jnp.mean(x, axis=-1, keepdims=True)
    inv_std = lax.rsqrt(jnp.mean(centre * centre, axis=-1, keepdims=True) + NORM_EPSILON)
    return centre * inv_std, inv_std


def norm_backward(grad_out, normed, inv_std, gain):
    scaled = grad_out * gain
    return inv_std * (
        scaled
        - jnp.mean(scaled, axis=-1, keepdims=True)
        - normed * jnp.mean(scaled * normed, axis=-1, keepdims=True)
    )


def gelu_pair(u):
    square = u * u
    share = 0.5 + 0.5 * jnp.tanh(u * (GELU_SCALE + (GELU_SCALE * 0.044715) * square))
    value = u * share
    slope = 2.0 * GELU_SCALE + (2.0 * GELU_SCALE * 3.0 * 0.044715) * square
    return value, share + value * (1.0 - share) * slope


def dot(a, b):
    return jnp.dot(a, b, preferred_element_type=f32)


def dot_nt(a, b):
    return lax.dot_general(a, b, NT, preferred_element_type=f32)


def dot_tn(a, b):
    return lax.dot_general(a, b, TN, preferred_element_type=f32)


def by_rows(rows, body, step=64):
    def one(i, _):
        body(pl.ds(pl.multiple_of(i * step, step), step))
        return 0

    lax.fori_loop(0, rows // step, one, 0)


def rowsum(x):
    return jnp.sum(x, axis=0, keepdims=True)


def take_slot(step, refs, buf, sem):
    blk = refs[0].shape[0]
    group = buf.shape[1] // blk
    copies = [
        pltpu.make_async_copy(ref, buf.at[s // group % 2, pl.ds(s % group * blk, blk), :], sem.at[s // group % 2, s % group])
        for s, ref in enumerate(refs)
    ]
    groups = [copies[s : s + group] for s in range(0, len(refs), group)]

    @pl.when(step == 0)
    def _():
        for copy in groups[0]:
            copy.start()

    for s, mine in enumerate(groups):

        @pl.when(step == s)
        def _(s=s, mine=mine):
            if s + 1 < len(groups):
                for copy in groups[s + 1]:
                    copy.start()
            for copy in mine:
                copy.wait()


def give_slot(step, value, refs, buf, sem):
    blk = refs[0].shape[0]
    group = buf.shape[1] // blk
    copies = [
        pltpu.make_async_copy(buf.at[s // group % 2, pl.ds(s % group * blk, blk), :], ref, sem.at[s // group % 2, s % group])
        for s, ref in enumerate(refs)
    ]
    groups = [copies[s : s + group] for s in range(0, len(refs), group)]
    count = len(groups)
    for s in range(2, count):

        @pl.when(step == s)
        def _(s=s):
            for copy in groups[s - 2]:
                copy.wait()

    buf[step % 2] = value
    for s in range(count):

        @pl.when(step == s)
        def _(s=s):
            for copy in groups[s]:
                copy.start()
            if s == count - 1:
                for k in range(max(0, count - 2), count):
                    for copy in groups[k]:
                        copy.wait()


def staging(group, blk, dim):
    return [pltpu.VMEM((2, group * blk, dim), bf16), pltpu.SemaphoreType.DMA((2, group))]


def group_of(count):
    return 2 - count % 2


def run_copies(moves, sem):
    copies = [pltpu.make_async_copy(source, target, sem.at[k]) for k, (source, target) in enumerate(moves)]
    for copy in copies:
        copy.start()
    return copies


def cut_first_kernel(n, count, c_ref, qkv_ref, *refs):
    small_refs, first_ref, vectors, sem = refs[:count], refs[count], refs[count + 1 : -1], refs[-1]
    rows, dim = qkv_ref.shape[0], qkv_ref.shape[1] // 3
    w = dim // n
    moves = list(zip(small_refs, vectors, strict=True))
    for i in range(3):
        at = pl.multiple_of(i * dim + c_ref[0] * w, w)
        moves.append((qkv_ref.at[:, pl.ds(at, w)], first_ref.at[pl.ds(0, rows), pl.ds(i * w, w)]))
    copies = run_copies(moves, sem)
    for copy in copies[:count]:
        copy.wait()
    k = 0
    for vector in vectors:
        for at in range(0, vector.shape[0], LANES):
            value = vector[at : at + LANES].reshape(1, LANES)
            first_ref[rows + k // 3 : rows + k // 3 + 1, (k % 3) * LANES : (k % 3 + 1) * LANES] = value
            k += 1
    for copy in copies[count:]:
        copy.wait()


def cut_first(c, w_qkv, small, n):
    rows, dim = w_qkv.shape[0], w_qkv.shape[1] // 3
    return pl.pallas_call(
        functools.partial(cut_first_kernel, n, len(small)),
        in_specs=[SMEM] + [ANY] * (1 + len(small)),
        out_specs=VMEM,
        out_shape=jax.ShapeDtypeStruct((rows + sum(a.shape[0] for a in small) // LANES // 3, 3 * dim // n), bf16),
        scratch_shapes=[pltpu.VMEM(a.shape, bf16) for a in small] + [pltpu.SemaphoreType.DMA((3 + len(small),))],
        compiler_params=params(63),
        cost_estimate=cost(0, MIB),
    )(c, w_qkv, *small)


def cut_second_kernel(n, nz, c_ref, up_ref, down_ref, out_ref, sem):
    c = c_ref[0]
    fb, half = down_ref.shape[0] // n, up_ref.shape[0] // 2
    moves = [(down_ref.at[pl.ds(pl.multiple_of(c * fb, fb), fb), :], out_ref.at[pl.ds(0, fb), :])]
    for i in range(nz):
        at = pl.multiple_of((i * n + c) * fb, fb)
        for side in range(2):
            target = out_ref.at[pl.ds(fb, half), pl.ds((side * nz + i) * fb, fb)]
            moves.append((up_ref.at[pl.ds(side * half, half), pl.ds(at, fb)], target))
    for copy in run_copies(moves, sem):
        copy.wait()


def cut_second(c, w_up, w_down, n, nz):
    out = (w_down.shape[0] // n + w_up.shape[0] // 2, w_down.shape[1])
    return pl.pallas_call(
        functools.partial(cut_second_kernel, n, nz),
        in_specs=[SMEM, ANY, ANY],
        out_specs=VMEM,
        out_shape=jax.ShapeDtypeStruct(out, bf16),
        scratch_shapes=[pltpu.SemaphoreType.DMA((1 + 2 * nz,))],
        compiler_params=params(),
        cost_estimate=cost(0, 2 * MIB),
    )(c, w_up, w_down)


def shard_of(z, k, nz):
    return jnp.where(z >= k, z - k, z - k + nz)


def pick_row(rows, which):
    picked = rows[0:1]
    for r in range(1, rows.shape[0]):
        picked = jnp.where(which == r, rows[r : r + 1], picked)
    return picked


def join_first_kernel(nz, n, at_ref, sc_ref, sl_ref, *refs):
    pieces, (w_ref, v_ref, qv_ref, up_ref) = refs[:nz], refs[nz:]
    c, z = at_ref[0], at_ref[1]
    shard = w_ref.shape[0] // nz
    per = shard // LANES
    for i, ref in enumerate(pieces):
        t = shard_of(z, i, nz)
        w_ref[pl.ds(pl.multiple_of(t * shard, shard), shard), :] = ref[:shard, :]
        for k in range((ref.shape[0] - shard) * 3):
            row = shard + k // 3
            value = ref[row : row + 1, (k % 3) * LANES : (k % 3 + 1) * LANES].astype(f32)
            at = pl.multiple_of(t * shard + (k % per) * LANES, LANES)
            v_ref[k // per : k // per + 1, pl.ds(at, LANES)] = value
    group = 2 * per
    for i in range(2):
        d = c + i * n
        at = pl.multiple_of((d // group) * shard + (d % per) * LANES, LANES)
        qv_ref[i : i + 1, :] = pick_row(v_ref[6:8, pl.ds(at, LANES)], d % group // per)
    for t in range(nz):
        at = pl.multiple_of(t * shard + (c % per) * LANES, LANES)
        up_ref[:, t * LANES : (t + 1) * LANES] = pick_row(v_ref[8:12, pl.ds(at, LANES)], c // per)


def join_first(at, sc, slopes, pieces, n, nz, shard):
    width = pieces[0].shape[1]
    small = (pieces[0].shape[0] - shard) * 3 * LANES // shard
    return pl.pallas_call(
        functools.partial(join_first_kernel, nz, n),
        in_specs=[SMEM] * 3 + [VMEM] * nz,
        out_shape=[
            jax.ShapeDtypeStruct((nz * shard, width), bf16),
            jax.ShapeDtypeStruct((small, nz * shard), f32),
            jax.ShapeDtypeStruct((2, LANES), f32),
            jax.ShapeDtypeStruct((1, nz * LANES), f32),
        ],
        compiler_params=params(),
        cost_estimate=cost(0, 2 * MIB),
    )(at, sc, slopes, *pieces)


def join_second_kernel(nz, at_ref, *refs):
    pieces, (up_ref, down_ref) = refs[:nz], refs[nz:]
    z = at_ref[1]
    shard = up_ref.shape[0] // nz
    fl = up_ref.shape[1]
    fb, half = fl // nz, shard // 2
    for i, ref in enumerate(pieces):
        t = shard_of(z, i, nz)
        down_ref[pl.ds(pl.multiple_of(t * fb, fb), fb), :] = ref[:fb, :]
        for side in range(2):
            at = pl.multiple_of(t * shard + side * half, half)
            up_ref[pl.ds(at, half), :] = ref[fb:, side * fl : (side + 1) * fl]


def join_second(at, pieces, nz, shard, fl):
    dim = pieces[0].shape[1]
    return pl.pallas_call(
        functools.partial(join_second_kernel, nz),
        in_specs=[SMEM] + [VMEM] * nz,
        out_shape=[jax.ShapeDtypeStruct((nz * shard, fl), bf16), jax.ShapeDtypeStruct((fl, dim), bf16)],
        compiler_params=params(),
        cost_estimate=cost(0, 6 * MIB),
    )(at, *pieces)


def stack_kernel(nz, at_ref, *refs):
    pieces, out_ref = refs[:nz], refs[nz]
    rows = pieces[0].shape[0]
    for i, ref in enumerate(pieces):
        at = pl.multiple_of(shard_of(at_ref[1], i, nz) * rows, rows)
        out_ref[pl.ds(at, rows), :] = ref[...]


def stack_shards(at, pieces, nz):
    rows, dim = pieces[0].shape
    return pl.pallas_call(
        functools.partial(stack_kernel, nz),
        in_specs=[SMEM] + [VMEM] * nz,
        out_shape=jax.ShapeDtypeStruct((nz * rows, dim), bf16),
        compiler_params=params(),
        cost_estimate=cost(0, MIB // 2),
    )(at, *pieces)


def join_dense_kernel(n, nz, sc_ref, *refs):
    slots, out_ref = refs[:n], refs[n]
    rest = slots[0].shape[0] // nz
    for p, ref in enumerate(slots):
        for t in range(nz):
            at = pl.multiple_of(t * n * rest + sc_ref[1 + n + p] * rest, rest)
            out_ref[pl.ds(at, rest), :] = ref[t * rest : (t + 1) * rest, :]


def join_dense(sc, slots, n, nz):
    rows, dim = slots[0].shape
    return pl.pallas_call(
        functools.partial(join_dense_kernel, n, nz),
        in_specs=[SMEM] + [VMEM] * n,
        out_shape=jax.ShapeDtypeStruct((n * rows, dim), bf16),
        compiler_params=params(),
        cost_estimate=cost(0, 4 * MIB),
    )(sc, *slots)


def ln_qkv_kernel(count, *refs):
    slots, (g_ref, s_ref, w_ref, b_ref, h_ref, q_ref, k_ref, v_ref, buf, sem) = refs[:count], refs[count:]
    step = pl.program_id(0)
    take_slot(step, slots, buf, sem)
    width = q_ref.shape[1]

    def norm(at):
        normed, _ = normalize(buf[step % 2, at, :].astype(f32))
        h_ref[at, :] = (normed * g_ref[...] + s_ref[...]).astype(bf16)

    by_rows(h_ref.shape[0], norm, 256)
    p = dot(h_ref[...], w_ref[...])
    q_ref[...] = (p[:, :width] + b_ref[0:1, :]).astype(bf16)
    k_ref[...] = p[:, width : 2 * width].astype(bf16)
    v_ref[...] = (p[:, 2 * width :] + b_ref[1:2, :]).astype(bf16)


def ln_qkv(slots, gain, shift, weight, bias, blk):
    n = len(slots)
    rows, dim = n * blk, weight.shape[0]
    width = weight.shape[1] // 3
    full = lambda a: pl.BlockSpec(a.shape, lambda i: (0, 0))
    group = group_of(n)
    tok = lambda cols: pl.BlockSpec((group * blk, cols), lambda i: (i, 0))
    out = lambda cols: jax.ShapeDtypeStruct((rows, cols), bf16)
    return pl.pallas_call(
        functools.partial(ln_qkv_kernel, n),
        grid=(n // group,),
        in_specs=[ANY] * n + [full(gain), full(shift), full(weight), full(bias)],
        out_specs=[tok(dim), tok(width), tok(width), tok(width)],
        out_shape=[out(dim), out(width), out(width), out(width)],
        scratch_shapes=staging(group, blk, dim),
        compiler_params=params(),
        cost_estimate=cost(6 * rows * dim * width, 4 * rows * dim),
    )(*slots, gain, shift, weight, bias)


def stacked(x, masks):
    zero = jnp.zeros_like(x)
    return jnp.concatenate([jnp.where(m, x, zero) for m in masks], axis=0)


def slope_lanes(sl_ref, hp, blk, w, first_query, b):
    lane = lax.broadcasted_iota(jnp.int32, (blk, w), 1)
    row = first_query + lax.broadcasted_iota(jnp.int32, (blk, w), 0)
    out = []
    for h in range(hp):
        slope = jnp.full((blk, w), sl_ref[h])
        high = slope.astype(bf16).astype(f32)
        mid = (slope - high).astype(bf16).astype(f32)
        low = slope - high - mid
        part = lane % 4
        value = jnp.where(part == 0, high, jnp.where(part == 1, mid, low))
        value = jnp.where(lane >= 4, value * blk, value)
        value = jnp.where((part == 3) | (lane >= 8), 0.0, value)
        value = jnp.where((lane == 3) & (row >= b), MASKED_SCORE, value)
        out.append(value.astype(bf16))
    return out


def key_lanes(blk, w, block, b):
    lane = lax.broadcasted_iota(jnp.int32, (blk, w), 1)
    row = lax.broadcasted_iota(jnp.int32, (blk, w), 0)
    value = jnp.where(lane < 4, row, block)
    value = jnp.where(lane == 3, jnp.where(block * blk + row < b, 1, 0), value)
    return jnp.where(lane < 8, value, 0).astype(f32).astype(bf16)


def causal(blk, cols):
    row = lax.broadcasted_iota(jnp.int32, (blk, cols), 0)
    col = lax.broadcasted_iota(jnp.int32, (blk, cols), 1) & (blk - 1)
    return jnp.where(row <= col, 0.0, MASKED_SCORE).astype(f32)


def attn_fwd_kernel(hp, blk, first, sc_ref, sl_ref, q_ref, k_ref, v_ref, *refs):
    o_ref, lse_ref, kx_ref, vt_ref, late_ref = refs[-5:]
    i = pl.program_id(0) + first
    b = sc_ref[0]
    nb, w = k_ref.shape[0] // blk, q_ref.shape[1]
    cols = hp * blk

    @pl.when(pl.program_id(0) == 0)
    def _():
        late_ref[...] = causal(blk, cols)
        for h in range(hp):
            vt_ref[h, HEAD:, :] = jnp.ones((16, nb * blk), bf16)
        for s in range(nb):
            at = pl.ds(pl.multiple_of(sc_ref[1 + s] * blk, blk), blk)
            rows = slice(s * blk, (s + 1) * blk)
            kx_ref[rows, :w] = k_ref[at, :]
            kx_ref[rows, w:] = key_lanes(blk, w, s, b)
            turned = jnp.transpose(v_ref[at, :].astype(f32)).astype(bf16)
            for h in range(hp):
                vt_ref[h, :HEAD, rows] = turned[h * HEAD : (h + 1) * HEAD, :]

    q2 = stacked(q_ref[...] * jnp.asarray(0.125, bf16), head_masks(hp, w))
    q2 = jnp.concatenate([q2, jnp.concatenate(slope_lanes(sl_ref, hp, blk, w, i * blk, b), axis=0)], axis=1)

    def chunk(j, carry, count, diagonal=False):
        m, accs = carry
        keys = pl.ds(pl.multiple_of(j * blk, blk), count * blk)
        s = dot_nt(kx_ref[keys, :], q2)
        if diagonal:
            last = s[(count - 1) * blk :] + late_ref[...]
            s = last if count == 1 else jnp.concatenate([s[: (count - 1) * blk], last], axis=0)
        mn = jnp.maximum(m, jnp.max(s, axis=0, keepdims=True))
        p = jnp.exp(s - mn).astype(bf16)
        alpha = jnp.exp(m - mn)
        out = []
        for h in range(hp):
            part = slice(h * blk, (h + 1) * blk)
            out.append(accs[h] * alpha[:, part] + dot(vt_ref[h, :, keys], p[:, part]))
        return mn, tuple(out)

    carry = (jnp.full((1, cols), MASKED_SCORE, f32), tuple(jnp.zeros((HEAD + 16, blk), f32) for _ in range(hp)))
    lo = jnp.where(i * blk < b, 0, b // blk)
    count = i - lo
    odd = count % 2
    carry = lax.switch(odd, [lambda cy, k=k: chunk(i - k, cy, k + 1, True) for k in range(2)], carry)
    m, accs = lax.fori_loop(0, count // 2, lambda t, cy: chunk(lo + 2 * t, cy, 2), carry)
    turned = jnp.concatenate([acc[:HEAD] / acc[HEAD : HEAD + 1] for acc in accs], axis=0)
    o_ref[...] = jnp.transpose(turned).astype(bf16)
    lse_ref[...] = m + jnp.log(jnp.concatenate([acc[HEAD : HEAD + 1] for acc in accs], axis=1))


def attn_fwd(sc, sl, q, k, v, blk, hp, first, count, so_far=()):
    S, w = q.shape
    so_far = list(so_far)
    return pl.pallas_call(
        functools.partial(attn_fwd_kernel, hp, blk, first),
        grid_spec=pltpu.PrefetchScalarGridSpec(
            num_scalar_prefetch=2,
            grid=(count,),
            in_specs=[
                pl.BlockSpec((blk, w), lambda i, sc, sl: (sc[1 + first + i], 0)),
                pl.BlockSpec((S, w), lambda i, sc, sl: (0, 0)),
                pl.BlockSpec((S, w), lambda i, sc, sl: (0, 0)),
            ]
            + [ANY] * len(so_far),
            out_specs=[
                pl.BlockSpec((blk, w), lambda i, sc, sl: (first + i, 0)),
                pl.BlockSpec((1, hp * blk), lambda i, sc, sl: (0, first + i)),
            ],
            scratch_shapes=[pltpu.VMEM((S, 2 * w), bf16), pltpu.VMEM((hp, HEAD + 16, S), bf16), pltpu.VMEM((blk, hp * blk), f32)],
        ),
        out_shape=[jax.ShapeDtypeStruct((S, w), bf16), jax.ShapeDtypeStruct((1, S * hp), f32)],
        input_output_aliases={5 + k: k for k in range(len(so_far))},
        compiler_params=params(),
        cost_estimate=cost(4 * S * count * blk * w, 8 * S * w, S * count * blk * hp // 2),
    )(sc, sl, q, k, v, *so_far)


def attn_bwd_kernel(hp, blk, sc_ref, sl_ref, q_ref, k_ref, v_ref, do_ref, o_ref, lse_ref, g_ref, gb_ref, q2_ref, do2_ref, delta_ref, dq_ref, late_ref, dk_ref, dv_ref):
    j = pl.program_id(0)
    nb = pl.num_programs(0)
    b = sc_ref[0]
    w = k_ref.shape[1]
    cols = hp * blk
    masks = head_masks(hp, w)

    @pl.when(j == 0)
    def _():
        pick = (lax.broadcasted_iota(jnp.int32, (8, w), 1) // HEAD == lax.broadcasted_iota(jnp.int32, (8, w), 0)).astype(bf16)
        gb_ref[...] = jnp.zeros_like(gb_ref)
        late_ref[...] = causal(blk, cols)

        def prepare(i, _):
            at = pl.multiple_of(sc_ref[1 + i] * blk, blk)
            rows = pl.ds(pl.multiple_of(i * cols, cols), cols)
            do = do_ref[pl.ds(pl.multiple_of(i * blk, blk), blk), :]
            q2_ref[rows, :w] = stacked(q_ref[pl.ds(at, blk), :] * jnp.asarray(0.125, bf16), masks)
            q2_ref[rows, w:] = jnp.concatenate(slope_lanes(sl_ref, hp, blk, w, i * blk, b), axis=0)
            do2_ref[rows, :] = stacked(do, masks)
            prod = do.astype(f32) * o_ref[pl.ds(pl.multiple_of(i * blk, blk), blk), :].astype(f32)
            high = prod.astype(bf16)
            d = dot_nt(pick, high) + dot_nt(pick, (prod - high.astype(f32)).astype(bf16))
            for h in range(hp):
                delta_ref[:, pl.ds(pl.multiple_of(i * cols + h * blk, blk), blk)] = d[h : h + 1, :]
            dq_ref[i] = jnp.zeros((w, blk), f32)
            return 0

        lax.fori_loop(0, nb, prepare, 0)

    k = k_ref[...]
    v = v_ref[...]
    kx = jnp.concatenate([k, key_lanes(blk, w, j, b)], axis=1)
    kt = jnp.transpose(k.astype(f32)).astype(bf16)

    def chunk(i, count, diagonal=False):
        at = pl.ds(pl.multiple_of(i * cols, cols), count * cols)
        s = dot_nt(kx, q2_ref[at, :])
        if diagonal:
            s = s + late_ref[...]
        p = jnp.exp(s - lse_ref[:, at])
        ds = (p * (dot_nt(v, do2_ref[at, :]) - delta_ref[:, at])).astype(bf16)
        dv = dot(p.astype(bf16), do2_ref[at, :])
        dk = dot(ds, q2_ref[at, :w])
        if diagonal:
            dv_ref[...] = dv
            dk_ref[...] = dk
        else:
            dv_ref[...] += dv
            dk_ref[...] += dk
        for t in range(count):
            for h in range(hp):
                rows = slice(h * HEAD, (h + 1) * HEAD)
                first = t * cols + h * blk
                dq_ref[i + t, rows, :] += dot(kt[rows, :], ds[:, first : first + blk])

    chunk(j, 1, True)
    hi = jnp.where((j + 1) * blk <= b, (b + blk - 1) // blk, nb)
    count = hi - j - 1
    lax.fori_loop(0, count // 2, lambda t, _: (chunk(j + 1 + 2 * t, 2), 0)[1], 0)
    for k in range(1, 2):

        @pl.when(count % 2 == k)
        def _(k=k):
            chunk(hi - k, k)

    dq = jnp.transpose(dq_ref[j]) * 0.125
    dv = dv_ref[...]
    g_ref[:, 0:w] = dq.astype(bf16)
    g_ref[:, w : 2 * w] = dk_ref[...].astype(bf16)
    g_ref[:, 2 * w : 3 * w] = dv.astype(bf16)
    gb_ref[0:1, :] += jnp.sum(dq, axis=0, keepdims=True)
    gb_ref[1:2, :] += jnp.sum(dv, axis=0, keepdims=True)


def attn_bwd(sc, sl, q, k, v, do, o, lse, blk, hp):
    S, w = q.shape
    nb = S // blk
    full = lambda shape: pl.BlockSpec(shape, lambda j, sc, sl: (0,) * len(shape))
    slot = lambda width: pl.BlockSpec((blk, width), lambda j, sc, sl: (sc[1 + j], 0))
    return pl.pallas_call(
        functools.partial(attn_bwd_kernel, hp, blk),
        grid_spec=pltpu.PrefetchScalarGridSpec(
            num_scalar_prefetch=2, grid=(nb,),
            in_specs=[full((S, w)), slot(w), slot(w), full((S, w)), full((S, w)), full((1, S * hp))],
            out_specs=[slot(3 * w), full((8, w))],
            scratch_shapes=[
                pltpu.VMEM((S * hp, 2 * w), bf16),
                pltpu.VMEM((S * hp, w), bf16),
                pltpu.VMEM((1, S * hp), f32),
                pltpu.VMEM((nb, w, blk), f32),
                pltpu.VMEM((blk, hp * blk), f32),
                pltpu.VMEM((blk, w), f32),
                pltpu.VMEM((blk, w), f32),
            ],
        ),
        out_shape=[jax.ShapeDtypeStruct((S, 3 * w), bf16), jax.ShapeDtypeStruct((8, w), f32)],
        compiler_params=params(),
        cost_estimate=cost(10 * S * S * w, 16 * S * w, S * S * hp // 2),
    )(sc, sl, q, k, v, do, o, lse)


def side_by_side(ref):
    return jnp.concatenate([ref[p] for p in range(ref.shape[0])], axis=1)


def dense_ln_kernel(x_ref, o_ref, w_ref, v_ref, y_ref, h_ref):
    y_ref[...] = dot(side_by_side(o_ref), w_ref[...])

    def norm(at):
        y = x_ref[at, :].astype(f32) + (y_ref[at, :] + v_ref[2:3, :])
        y_ref[at, :] = y
        normed, _ = normalize(y)
        h_ref[at, :] = (normed * v_ref[3:4, :] + v_ref[4:5, :]).astype(bf16)

    by_rows(x_ref.shape[0], norm, 128)


def dense_ln(x, o, weight, vectors):
    rows, dim = x.shape
    return pl.pallas_call(
        dense_ln_kernel,
        out_shape=[jax.ShapeDtypeStruct((rows, dim), f32), jax.ShapeDtypeStruct((rows, dim), bf16)],
        compiler_params=params(),
        cost_estimate=cost(2 * rows * dim * dim, 2 * dim * dim + 12 * rows * dim),
    )(x, o, weight, vectors)


def dz_kernel(count, *refs):
    slots, (w_ref, all_ref, dz_ref, buf, sem) = refs[:count], refs[count:]
    step = pl.program_id(0)
    take_slot(step, slots, buf, sem)
    cot = buf[step % 2]
    all_ref[...] = cot
    dz_ref[...] = dot_nt(cot, w_ref[...]).astype(bf16)


def dz_blocks(slots, down, blk):
    n, (width, dim) = len(slots), down.shape
    group = group_of(n)
    tok = lambda cols: pl.BlockSpec((group * blk, cols), lambda i: (i, 0))
    return pl.pallas_call(
        functools.partial(dz_kernel, n),
        grid=(n // group,),
        in_specs=[ANY] * n + [pl.BlockSpec(down.shape, lambda i: (0, 0))],
        out_specs=[tok(dim), tok(width)],
        out_shape=[jax.ShapeDtypeStruct((n * blk, dim), bf16), jax.ShapeDtypeStruct((n * blk, width), bf16)],
        scratch_shapes=staging(group, blk, dim),
        compiler_params=params(),
        cost_estimate=cost(2 * n * blk * dim * width, 4 * n * blk * (dim + width)),
    )(*slots, down)


def mlp_kernel(count, extra, *refs):
    h_slots, (dz_ref, u_ref, b_ref) = refs[:count], refs[count : count + 3]
    refs = refs[count + 3 + extra :]
    hall_ref, z_ref, du_ref, gb_ref = refs[:4]
    dh_slots, (hbuf, hsem, dbuf, dsem) = refs[4 : 4 + count], refs[4 + count :]
    step = pl.program_id(0)
    take_slot(step, h_slots, hbuf, hsem)
    h = hbuf[step % 2]
    hall_ref[...] = h
    value, deriv = gelu_pair(dot(h, u_ref[...]) + b_ref[...])
    z_ref[...] = value.astype(bf16)
    du = dz_ref[...].astype(f32) * deriv

    @pl.when(step == 0)
    def _():
        gb_ref[...] = jnp.zeros_like(gb_ref)

    gb_ref[...] += rowsum(du)
    du = du.astype(bf16)
    du_ref[...] = du
    give_slot(step, dot_nt(du, u_ref[...]).astype(bf16), dh_slots, dbuf, dsem)


def mlp(h_slots, dz, up, bias, blk, n, first, so_far=()):
    count = len(h_slots)
    dim, width = up.shape
    full = lambda a: pl.BlockSpec(a.shape, lambda i: (0, 0))
    group = group_of(count)
    tok = lambda cols: pl.BlockSpec((group * blk, cols), lambda i: (first // group + i, 0))
    out = lambda rows, cols: jax.ShapeDtypeStruct((rows, cols), bf16)
    so_far = list(so_far)
    res = pl.pallas_call(
        functools.partial(mlp_kernel, count, len(so_far)),
        grid=(count // group,),
        in_specs=[ANY] * count + [tok(width), full(up), full(bias)] + [ANY] * len(so_far),
        out_specs=[tok(dim), tok(width), tok(width), pl.BlockSpec((1, width), lambda i: (0, 0))] + [ANY] * count,
        out_shape=[out(n * blk, dim), out(n * blk, width), out(n * blk, width), jax.ShapeDtypeStruct((1, width), f32)]
        + [out(blk, dim)] * count,
        scratch_shapes=staging(group, blk, dim) + staging(group, blk, dim),
        input_output_aliases={count + 3 + k: k for k in range(len(so_far))},
        compiler_params=params(),
        cost_estimate=cost(4 * count * blk * dim * width, count * blk * dim * 10, count * blk * width),
    )(*h_slots, dz, up, bias, *so_far)
    return res[:3], res[3], res[4:]


def to_slots_kernel(count, extra, blk, transposed, a_ref, w_ref, *refs):
    slots, (buf, sem) = refs[extra : extra + count], refs[extra + count :]
    product = (dot_nt if transposed else dot)(a_ref[...], w_ref[...])
    targets = [ref.at[pl.ds(0, blk), :] for ref in slots]
    give_slot(pl.program_id(0), product.astype(bf16), targets, buf, sem)


def to_slots(a, weight, blk, first, count, transposed=False, onto=()):
    dim = weight.shape[0 if transposed else 1]
    onto = list(onto)
    group = group_of(count)
    return pl.pallas_call(
        functools.partial(to_slots_kernel, count, len(onto), blk, transposed),
        grid=(count // group,),
        in_specs=[pl.BlockSpec((group * blk, a.shape[1]), lambda i: (first // group + i, 0)), pl.BlockSpec(weight.shape, lambda i: (0, 0))]
        + [ANY] * len(onto),
        out_specs=[ANY] * count,
        out_shape=[jax.ShapeDtypeStruct(onto[k].shape if onto else (blk, dim), bf16) for k in range(count)],
        scratch_shapes=staging(group, blk, dim),
        input_output_aliases={2 + k: k for k in range(len(onto))},
        compiler_params=params(),
        cost_estimate=cost(2 * count * blk * a.shape[1] * dim, 2 * count * blk * (a.shape[1] + dim)),
    )(a, weight, *onto)


def summed(parts, at):
    return sum(ref[at, :].astype(f32) for ref in parts)


def ln2_back_kernel(count, *refs):
    parts, (y_ref, cot_ref, w_ref, v_ref, dy_ref, dyb_ref, do_ref, gs_ref) = refs[:count], refs[count:]
    gs_ref[...] = jnp.zeros_like(gs_ref)

    def norm(at):
        normed, inv_std = normalize(y_ref[at, :])
        dh = summed(parts, at)
        cot = cot_ref[at, :].astype(f32)
        dy = cot + norm_backward(dh, normed, inv_std, v_ref[3:4, :])
        dy_ref[at, :] = dy
        dyb_ref[at, :] = dy.astype(bf16)
        for row, value in enumerate((dy, dh * normed, dh, cot)):
            gs_ref[row : row + 1, :] += rowsum(value)

    by_rows(y_ref.shape[0], norm, 128)
    do = dot_nt(dyb_ref[...], w_ref[...]).astype(bf16)
    width = do_ref.shape[2]
    for p in range(do_ref.shape[0]):
        do_ref[p] = do[:, p * width : (p + 1) * width]


def ln2_back(parts, y, cot, weight, vectors, n):
    rows, dim = y.shape
    return pl.pallas_call(
        functools.partial(ln2_back_kernel, len(parts)),
        out_shape=[
            jax.ShapeDtypeStruct((rows, dim), f32),
            jax.ShapeDtypeStruct((rows, dim), bf16),
            jax.ShapeDtypeStruct((n, rows, dim // n), bf16),
            jax.ShapeDtypeStruct((4, dim), f32),
        ],
        compiler_params=params(),
        cost_estimate=cost(2 * rows * dim * dim, 2 * dim * dim + 20 * rows * dim),
    )(*parts, y, cot, weight, vectors)


def finish_kernel(count, *refs):
    parts, (y_ref, v_ref, out_ref) = refs[:count], refs[count:]

    def add(at):
        out_ref[at, :] = y_ref[at, :] + (summed(parts, at) + v_ref[5:6, :])

    by_rows(y_ref.shape[0], add)


def finish_out(parts, y, vectors):
    return pl.pallas_call(
        functools.partial(finish_kernel, len(parts)),
        out_shape=jax.ShapeDtypeStruct(y.shape, f32),
        compiler_params=params(),
        cost_estimate=cost(y.size, 10 * y.size),
    )(*parts, y, vectors)


def ln1_back_kernel(count, *refs):
    parts, (x_ref, dy_ref, v_ref, out_ref) = refs[:count], refs[count:]

    def norm(at):
        normed, inv_std = normalize(x_ref[at, :].astype(f32))
        out_ref[at, :] = dy_ref[at, :] + norm_backward(summed(parts, at), normed, inv_std, v_ref[0:1, :])

    by_rows(x_ref.shape[0], norm, 128)


def ln1_back(parts, x, dy, vectors):
    return pl.pallas_call(
        functools.partial(ln1_back_kernel, len(parts)),
        out_shape=jax.ShapeDtypeStruct(dy.shape, f32),
        compiler_params=params(),
        cost_estimate=cost(20 * dy.size, 14 * dy.size),
    )(*parts, x, dy, vectors)


def shard_at(z, i, nz):
    return lax.rem(z + i, nz)


def grad_kernel(nz, fold, z_ref, a_ref, b_ref, *refs):
    outs, acc_ref = refs[-nz - 1 : -1], refs[-1]
    acc_ref[...] = dot_tn(a_ref[...], b_ref[...])
    cols = acc_ref.shape[1]
    for i, ref in enumerate(outs):
        rows = ref.shape[0]
        base = shard_at(z_ref[0], i, nz) * rows * fold
        for side in range(fold):
            at = pl.ds(pl.multiple_of(base + side * rows, rows), rows)
            ref[:, side * cols : (side + 1) * cols] = acc_ref[at, :].astype(bf16)


def grad_blocks(z, a, b, nz, fold, part, so_far=()):
    rows, cols = a.shape[1] // nz // fold, fold * b.shape[1]
    so_far = list(so_far)
    return pl.pallas_call(
        functools.partial(grad_kernel, nz, fold),
        grid=(1,),
        in_specs=[SMEM, VMEM, VMEM] + [ANY] * len(so_far),
        out_specs=[pl.BlockSpec((rows, cols), lambda i: (part, 0))] * nz,
        out_shape=[jax.ShapeDtypeStruct((2 * rows, cols), bf16)] * nz,
        scratch_shapes=[pltpu.VMEM((a.shape[1], b.shape[1]), f32)],
        input_output_aliases={3 + k: k for k in range(len(so_far))},
        compiler_params=params(),
        cost_estimate=cost(2 * a.size * b.shape[1], 2 * (a.size + b.size)),
    )(z, a, b, *so_far)


def split_nt(wide, narrow, swapped=False):
    high = wide.astype(bf16)
    terms = (high, (wide - high.astype(f32)).astype(bf16))
    return sum(dot_nt(narrow, t) if swapped else dot_nt(t, narrow) for t in terms)


def grad_qkv_kernel(nz, z_ref, h_ref, g_ref, s_ref, w_ref, v_ref, *refs):
    outs, (acc_ref, row_ref) = refs[:nz], refs[nz:]
    w = g_ref.shape[1] // 3
    shard = h_ref.shape[1] // nz
    acc_ref[...] = dot_tn(h_ref[...], g_ref[...])
    column = dot(jnp.ones((8, g_ref.shape[0]), bf16), g_ref[...])

    def sums(at):
        weight = w_ref[at, :]
        shift = split_nt(column, weight)[0:1]
        gain = split_nt(acc_ref[at, :] * weight.astype(f32), jnp.ones((8, 3 * w), bf16), True)[0:1]
        row_ref[0:1, at] = (gain - v_ref[1:2, at] * shift) / v_ref[0:1, at]
        row_ref[1:2, at] = shift

    by_rows(acc_ref.shape[0], sums, shard)
    per = shard // LANES
    base = 3 * shard
    for k, ref in enumerate(outs):
        t = shard_at(z_ref[0], k, nz)
        grad = acc_ref[pl.ds(pl.multiple_of(t * shard, shard), shard), :].astype(bf16)
        for i in range(3):
            ref[i * shard : (i + 1) * shard, :] = grad[:, i * w : (i + 1) * w]
        ref[base:, :] = s_ref[t].astype(bf16)
        for e in range(per):
            pair = row_ref[0:8, pl.ds(pl.multiple_of(t * shard + e * LANES, LANES), LANES)].astype(bf16)
            for v in range(2):
                row = base + v * per + e
                ref[row : row + 1, :] = pair[v : v + 1]


def grad_qkv(z, h, g, small, weight, vectors, nz):
    rows, dim = h.shape
    shard, w = dim // nz, g.shape[1] // 3
    out = (3 * shard + small.shape[1], w)
    return pl.pallas_call(
        functools.partial(grad_qkv_kernel, nz),
        in_specs=[SMEM] + [VMEM] * 5,
        out_shape=[jax.ShapeDtypeStruct(out, bf16)] * nz,
        scratch_shapes=[pltpu.VMEM((dim, 3 * w), f32), pltpu.VMEM((8, dim), f32)],
        compiler_params=params(),
        cost_estimate=cost(6 * rows * dim * w, 2 * rows * (dim + 3 * w)),
    )(z, h, g, small, weight, vectors)


def grad_dense_kernel(n, nz, at_ref, sc_ref, o_ref, d_ref, *refs):
    outs, acc_ref = refs[:n], refs[n]
    z = at_ref[1]
    acc_ref[...] = dot_tn(side_by_side(o_ref), d_ref[...])
    rest = acc_ref.shape[0] // (n * nz)
    for p, ref in enumerate(outs):
        for i in range(nz):
            at = shard_at(z, i, nz) * n * rest + sc_ref[1 + n + p] * rest
            ref[i * rest : (i + 1) * rest, :] = acc_ref[pl.ds(pl.multiple_of(at, rest), rest), :].astype(bf16)


def grad_dense(at, sc, o, dyb, n, nz):
    rows, dim = dyb.shape
    rest = dim // n
    return pl.pallas_call(
        functools.partial(grad_dense_kernel, n, nz),
        grid=(1,),
        in_specs=[SMEM, SMEM, VMEM, VMEM],
        out_specs=[pl.BlockSpec((rest, dim), lambda i: (rows // rest, 0))] * n,
        out_shape=[jax.ShapeDtypeStruct((rows + rest, dim), bf16)] * n,
        scratch_shapes=[pltpu.VMEM((dim, dim), f32)],
        compiler_params=params(),
        cost_estimate=cost(2 * rows * dim * dim, 2 * dim * dim),
    )(at, sc, o, dyb)


def small_kernel(n, nz, c_ref, s_ref, qv_ref, *refs):
    out_ref = refs[-1]
    c = c_ref[0]
    out_ref[...] = jnp.zeros_like(out_ref)
    shard = s_ref.shape[1] // nz
    per = shard // LANES
    up = sum(ref[...] for ref in refs[:-1])
    for t in range(nz):
        for v in range(4):
            for e in range(per):
                at = t * shard + e * LANES
                row = (v + 2) * per + e
                out_ref[t, row : row + 1, :] = s_ref[v : v + 1, at : at + LANES]
        out_ref[t, pl.ds(8 * per + c, 1), :] = up[:, t * LANES : (t + 1) * LANES]
    row = 6 * per + c % (2 * per)
    out_ref[c // (2 * per), pl.ds(row, 1), :] = qv_ref[0:1, :]
    out_ref[nz // 2 + c // (2 * per), pl.ds(row, 1), :] = qv_ref[1:2, :]


def small_grads(c, sums, qv, ups, n, nz):
    dim = sums.shape[1]
    return pl.pallas_call(
        functools.partial(small_kernel, n, nz),
        in_specs=[SMEM] + [VMEM] * (2 + len(ups)),
        out_shape=jax.ShapeDtypeStruct((nz, 12 * dim // nz // LANES, LANES), f32),
        compiler_params=params(),
        cost_estimate=cost(0, 1 << 16),
    )(c, sums, qv, *ups)


def spread_kernel(first, n, count, outs, small, small_row, others, extra, sc_ref, *refs):
    slots, more, refs = refs[:count], refs[count : count + others], refs[count + others + extra :]
    out_refs, refs = refs[: len(outs)], refs[len(outs) :]
    sums, (wide, osem) = refs[:-2], refs[-2:]
    started = []
    for s, slot in enumerate(slots):
        block_of = sc_ref[1 + n + first + s]
        wide[s] = slot[...].astype(f32)
        k = 0
        for ref, blocks in zip(out_refs, outs, strict=True):
            for row, col, height, width, trow, tcol, by_row in blocks:
                if by_row:
                    target = ref.at[pl.ds(pl.multiple_of(trow + block_of * height, 8), height), pl.ds(tcol, width)]
                else:
                    target = ref.at[pl.ds(trow, height), pl.ds(pl.multiple_of(tcol + block_of * width, LANES), width)]
                source = wide.at[s, pl.ds(row, height), pl.ds(col, width)]
                started.append(pltpu.make_async_copy(source, target, osem.at[s, k]))
                started[-1].start()
                k += 1
    if small:
        held = slice(small_row, small_row + sum(small) // LANES)
        total = wide[0, held, :]
        for s in range(1, count):
            total = total + wide[s, held, :]
        for ref in more:
            total = total + ref[held, :].astype(f32)
        row = 0
        for ref, size in zip(sums, small, strict=True):
            for at in range(0, size, LANES):
                ref[at : at + LANES] = total[row : row + 1, :].reshape(LANES)
                row += 1
    for copy in started:
        copy.wait()


def spread(sc, n, first, slots, outs, shapes, so_far=(), small=(), small_row=0, more=()):
    count = len(slots)
    height, width = slots[0].shape
    so_far, small, more = list(so_far), list(small), list(more)
    return pl.pallas_call(
        functools.partial(spread_kernel, first, n, count, outs, small, small_row, len(more), len(so_far)),
        in_specs=[SMEM] + [VMEM] * (count + len(more)) + [ANY] * len(so_far),
        out_specs=[ANY] * len(shapes) + [VMEM] * len(small),
        out_shape=[jax.ShapeDtypeStruct(shape, f32) for shape in shapes + [(size,) for size in small]],
        scratch_shapes=[
            pltpu.VMEM((count, height, width), f32),
            pltpu.SemaphoreType.DMA((count, sum(len(blocks) for blocks in outs))),
        ],
        input_output_aliases={1 + count + len(more) + k: k for k in range(len(so_far))},
        compiler_params=params(),
        cost_estimate=cost(0, 6 * count * height * width),
    )(sc, *slots, *more, *so_far)


def swap(x, n, bit, axis=ROW):
    return lax.ppermute(x, axis, [(i, i ^ bit) for i in range(n)])


def turn(n, first):
    return [(i, i ^ (2 if (i % 2 == 0) == first else 4)) for i in range(n)]


def places(c, n):
    slot = jnp.arange(n, dtype=jnp.int32)

    def moved(s):
        if n != 8:
            return s
        cross = jnp.where(c % 2 == 0, (s == 3) | (s == 5), (s == 2) | (s == 4))
        return jnp.where(cross, s ^ 6, s)

    return jnp.concatenate([moved(slot ^ c), c ^ moved(slot)])


def gather_slots(x, n):
    if n != 8:
        slots = {0: x}
        bit = n >> 1
        while bit:
            for s in list(slots):
                slots[s ^ bit] = swap(slots[s], n, bit)
            bit >>= 1
        return [slots[s] for s in range(n)]
    near = lax.ppermute(x, ROW, turn(n, True))
    side = lax.ppermute(x, ROW, turn(n, False))
    far = lax.ppermute(near, ROW, turn(n, False))
    slots = []
    for part in (x, near, side, far):
        slots += [part, swap(part, n, 1)]
    return slots


def add16(*terms):
    return sum(a.astype(f32) for a in terms).astype(bf16)


def scatter_slots(parts, n):
    if n != 8:
        parts = dict(enumerate(parts))
        bit = 1
        while bit < n:
            for s in [s for s in parts if not s & bit]:
                parts[s] = add16(parts[s], swap(parts.pop(s | bit), n, bit))
            bit <<= 1
        return [parts[0]]
    got = [swap(parts[2 * k + 1], n, 1) for k in range(4)]
    far = lax.ppermute(add16(parts[6], got[3]), ROW, turn(n, False))
    side = lax.ppermute(add16(parts[4], got[2]), ROW, turn(n, False))
    near = lax.ppermute(add16(parts[2], got[1], far), ROW, turn(n, True))
    return [parts[0], got[0], side, near]


def ring(x, nz):
    return [x] + [lax.ppermute(x, SHARDS, [(i, (i + k) % nz) for i in range(nz)]) for k in range(1, nz)]


def over_shards(parts, nz):
    got = [lax.ppermute(parts[k], SHARDS, [(i, (i + k) % nz) for i in range(nz)]) for k in range(1, nz)]
    return add16(parts[0], *got)


def layer(
    hidden_in,
    seq_ids,
    ln1_gain,
    ln1_bias,
    w_qkv,
    b_qv,
    w_dense,
    b_dense,
    ln2_gain,
    ln2_bias,
    w_up,
    b_up,
    w_down,
    b_down,
    cotangent,
    n,
    nz,
    fast,
):
    c = lax.axis_index(ROW).astype(jnp.int32)
    z = lax.axis_index(SHARDS).astype(jnp.int32)
    at = jnp.stack([c, z])
    rows, dim = hidden_in.shape
    seq_len = seq_ids.shape[1]
    shard = dim // nz
    hp = HEADS // n
    w = hp * HEAD
    fb = w_down.shape[0] // n
    fl = nz * fb
    ff = fl * n
    both = (SHARDS, ROW)

    seg = seq_ids[0]
    boundary = jnp.sum((seg == seg[0]).astype(jnp.int32))
    sc = jnp.concatenate([boundary.reshape(1), places(c, n)])
    head = (c * hp + 1 + jnp.arange(hp)).astype(f32)
    slopes = jnp.exp2(-8.0 * head / HEADS) * (8.0 / seq_len)

    x_slots = gather_slots(hidden_in, n)
    cot_slots = gather_slots(cotangent, n)
    small = (ln1_gain, ln1_bias, b_dense, ln2_gain, ln2_bias, b_down, b_qv, b_up)
    if fast:
        first = cut_first(c.reshape(1), w_qkv, small, n)
        second = cut_second(c.reshape(1), w_up, w_down, n, nz)
        wq, vectors, bias_qv, bias_up = join_first(at, sc, slopes, ring(first, nz), n, nz, shard)
        dense = lax.dynamic_slice_in_dim(w_dense, c * (shard // n), shard // n, 0)
        dense = stack_shards(at, ring(dense, nz), nz)
        wd = join_dense(sc, gather_slots(dense, n), n, nz)
        wu, wn = join_second(at, ring(second, nz), nz, shard, fl)
    else:
        small = lax.all_gather(jnp.concatenate(small), SHARDS, axis=0, tiled=False).astype(f32)
        vectors = small[:, : 6 * shard].reshape(nz, 6, shard).transpose(1, 0, 2).reshape(6, dim)
        bias_qv = small[:, 6 * shard : 8 * shard].reshape(2, n, w)
        bias_qv = lax.dynamic_index_in_dim(bias_qv, c, 1, keepdims=False)
        bias_up = small[:, 8 * shard :].reshape(nz, n, fb)
        bias_up = lax.dynamic_index_in_dim(bias_up, c, 1, keepdims=False).reshape(1, fl)
        wq = lax.dynamic_index_in_dim(w_qkv.reshape(shard, 3, n, w), c, 2, keepdims=False).reshape(shard, 3 * w)
        wq = lax.all_gather(wq, SHARDS, axis=0, tiled=True)
        wu = lax.dynamic_index_in_dim(w_up.reshape(shard, nz, n, fb), c, 2, keepdims=False).reshape(shard, fl)
        wu = lax.all_gather(wu, SHARDS, axis=0, tiled=True)
        wn = lax.all_gather(lax.dynamic_slice_in_dim(w_down, c * fb, fb, 0), SHARDS, axis=0, tiled=True)
        wd = lax.all_gather(w_dense, SHARDS, axis=0, tiled=True)

    h1, q, k, v = ln_qkv(x_slots, vectors[0:1], vectors[1:2], wq, bias_qv, rows)
    o, lse = attn_fwd(sc, slopes, q, k, v, rows, hp, 0, n)
    o_own = lax.all_to_all(o.reshape(n, rows, w), ROW, split_axis=0, concat_axis=0, tiled=True)
    y1, h2 = dense_ln(hidden_in, o_own, wd, vectors)

    h2_slots = gather_slots(h2, n)
    early = n - 2
    cot_all, dz = dz_blocks(cot_slots, wn, rows)
    alls, gb_up, dh2_slots = (), [], []
    for first, last in ((0, 2), (2, early), (early, n)):
        alls, gb, dh = mlp(h2_slots[first:last], dz, wu, bias_up, rows, n, first, alls)
        gb_up.append(gb)
        dh2_slots += dh
    h2_all, act, du = alls
    dh2_parts = scatter_slots(dh2_slots, n)
    dy, dyb, do, sums2 = ln2_back(dh2_parts, y1, cotangent, wd, vectors, n)
    do_heads = lax.all_to_all(do, ROW, split_axis=0, concat_axis=0, tiled=True).reshape(seq_len, w)

    g, gb_qv = attn_bwd(sc, slopes, q, k, v, do_heads, o, lse, rows, hp)
    dh1_far = to_slots(g, wq, rows, early, n - early, True)
    dh1_slots = [*to_slots(g, wq, rows, 0, early, True), *dh1_far]
    dh1_parts = scatter_slots(dh1_slots, n)
    grad_input = ln1_back(dh1_parts, hidden_in, dy, vectors)

    onto = grad_dense(at, sc, o_own, dyb, n, nz) if fast else ()
    out_parts = scatter_slots(to_slots(act, wn, rows, 0, n, False, onto), n)
    block_out = finish_out(out_parts, y1, vectors)

    if fast:
        parts = grad_blocks(z.reshape(1), act, cot_all, nz, 1, 0)
        parts = grad_blocks(z.reshape(1), h2_all, du, nz, 2, 1, parts)
        g_ff = over_shards(parts, nz)
        small = small_grads(c.reshape(1), sums2, gb_qv, gb_up, n, nz)
        g_qkv = over_shards(grad_qkv(z.reshape(1), h1, g, small, wq, vectors, nz), nz)
        rest = shard // n
        dense = [add16(*[part[rows + i * rest : rows + (i + 1) * rest] for part in out_parts]) for i in range(nz)]
        dense = over_shards(dense, nz).reshape(rest, n, w).transpose(1, 0, 2).reshape(n * rest, w)
        qkv_slots = gather_slots(jnp.concatenate([g_qkv, dense], axis=0), n)
        half = shard // 2
        ff_slots = gather_slots(g_ff, n)
        blocks_of = [
            [(0, 0, fb, dim, 0, 0, True)],
            [
                (fb, side * fl + t * fb, half, fb, side * half, t * n * fb, False)
                for side in range(2)
                for t in range(nz)
            ],
        ]
        shapes_of = [(n * fb, dim), (shard, ff)]
        so_far = spread(sc, n, 0, ff_slots[:6], blocks_of, shapes_of)
        g_down, g_up = spread(sc, n, 6, ff_slots[6:], blocks_of, shapes_of, so_far)
        lengths = [shard] * 6 + [2 * shard, 4 * shard]
        base = 3 * shard + sum(lengths) // LANES
        blocks_of = [
            [(i * shard, 0, shard, w, 0, i * dim, False) for i in range(3)],
            [(base + e * rest, 0, rest, w, 0, e * w, True) for e in range(n)],
        ]
        shapes_of = [(shard, 3 * dim), (shard, dim)]
        so_far = spread(sc, n, 0, qkv_slots[:6], blocks_of, shapes_of)
        g_qkv, g_dense, *total = spread(
            sc, n, 6, qkv_slots[6:], blocks_of, shapes_of, so_far, lengths, 3 * shard, qkv_slots[:6]
        )
    else:
        reduce = lambda a: lax.psum(
            lax.psum_scatter(a.astype(bf16), SHARDS, scatter_dimension=0, tiled=True), ROW
        ).astype(f32)
        every = lambda a, axis: lax.all_gather(
            lax.psum_scatter(a.astype(bf16), SHARDS, scatter_dimension=0, tiled=True), ROW, axis=axis, tiled=True
        ).astype(f32)
        g_down = every(dot_tn(act, cot_all), 0)
        g_up = dot_tn(h2_all, du).reshape(dim, nz, fb)
        g_up = every(g_up, 2).reshape(shard, ff)
        g_dense = reduce(dot_tn(o_own.transpose(1, 0, 2).reshape(rows, dim), dyb))
        g_qkv = every(dot_tn(h1, g).reshape(dim, 3, w), 2).reshape(shard, 3 * dim)
        dh1 = dot_nt(g, wq)
        normed = jnp.concatenate([normalize(x.astype(f32))[0] for x in x_slots], axis=0)
        sums1 = jnp.concatenate([rowsum(dh1 * normed), rowsum(dh1)], axis=0)
        own = lambda a, lead: lax.dynamic_update_index_in_dim(jnp.zeros((lead, n, a.shape[-1]), f32), a, c, 1)
        by_shard = lambda a: a.reshape(-1, nz, shard).transpose(1, 0, 2).reshape(nz, -1)
        flat = jnp.concatenate(
            [
                by_shard(sums1),
                by_shard(sums2),
                own(gb_qv[:2], 2).reshape(nz, 2 * shard),
                own(sum(gb_up).reshape(nz, fb), nz).reshape(nz, n * fb),
            ],
            axis=1,
        )
        total = lax.dynamic_index_in_dim(lax.psum(flat, both), z, 0, keepdims=False)
        total = [total[i * shard : (i + 1) * shard] for i in range(6)] + [total[6 * shard : 8 * shard], total[8 * shard :]]
    return (
        block_out,
        grad_input,
        total[0],
        total[1],
        g_qkv,
        total[6],
        g_dense,
        total[2],
        total[3],
        total[4],
        g_up,
        total[7],
        g_down,
        total[5],
    )


def solution(mesh):
    n, nz = mesh.shape[ROW], mesh.shape[SHARDS]
    fast = n == 8 and nz == 4
    shard = P(SHARDS)
    mat = P(SHARDS, None)
    tokens = P((SHARDS, ROW), None)
    return jax.shard_map(
        functools.partial(layer, n=n, nz=nz, fast=fast),
        mesh=mesh,
        in_specs=(tokens, mat, shard, shard, mat, shard, mat, shard, shard, shard, mat, shard, mat, shard, tokens),
        out_specs=(tokens, tokens, shard, shard, mat, shard, mat, shard, shard, shard, mat, shard, mat, shard),
        check_vma=False,
    )
```

```python
import functools
import math

import jax
import jax.numpy as jnp
from jax import lax
from jax.experimental import pallas as pl
from jax.experimental.pallas import tpu as pltpu
from jax.sharding import PartitionSpec as P


HEADS = 16
HEAD = 64
LANES = 128
NORM_EPSILON = 1e-05
MASKED_SCORE = -1e30
GELU_SCALE = math.sqrt(2.0 / math.pi)
NT = (((1,), (1,)), ((), ()))
TN = (((0,), (0,)), ((), ()))
f32 = jnp.float32
bf16 = jnp.bfloat16
MIB = 1 << 20
ROW, SHARDS = "ctx", "fsdp"
ANY = pl.BlockSpec(memory_space=pl.ANY)
SMEM = pl.BlockSpec(memory_space=pltpu.SMEM)
VMEM = pl.BlockSpec(memory_space=pltpu.VMEM)


def params(limit=20):
    return pltpu.CompilerParams(vmem_limit_bytes=limit * MIB)


def cost(flops, moved, hard=0):
    return pl.CostEstimate(flops=flops, bytes_accessed=moved, transcendentals=hard)


def head_masks(hp, w):
    lane = lax.broadcasted_iota(jnp.int32, (1, w), 1)
    return [(lane // HEAD) == h for h in range(hp)]


def normalize(x):
    centre = x - jnp.mean(x, axis=-1, keepdims=True)
    inv_std = lax.rsqrt(jnp.mean(centre * centre, axis=-1, keepdims=True) + NORM_EPSILON)
    return centre * inv_std, inv_std


def norm_backward(grad_out, normed, inv_std, gain):
    scaled = grad_out * gain
    return inv_std * (
        scaled
        - jnp.mean(scaled, axis=-1, keepdims=True)
        - normed * jnp.mean(scaled * normed, axis=-1, keepdims=True)
    )


def gelu_pair(u):
    square = u * u
    share = 0.5 + 0.5 * jnp.tanh(u * (GELU_SCALE + (GELU_SCALE * 0.044715) * square))
    value = u * share
    slope = 2.0 * GELU_SCALE + (2.0 * GELU_SCALE * 3.0 * 0.044715) * square
    return value, share + value * (1.0 - share) * slope


def dot(a, b):
    return jnp.dot(a, b, preferred_element_type=f32)


def dot_nt(a, b):
    return lax.dot_general(a, b, NT, preferred_element_type=f32)


def dot_tn(a, b):
    return lax.dot_general(a, b, TN, preferred_element_type=f32)


def by_rows(rows, body, step=64):
    def one(i, _):
        body(pl.ds(pl.multiple_of(i * step, step), step))
        return 0

    lax.fori_loop(0, rows // step, one, 0)


def rowsum(x):
    return jnp.sum(x, axis=0, keepdims=True)


def take_slot(step, refs, buf, sem):
    blk = refs[0].shape[0]
    group = buf.shape[1] // blk
    copies = [
        pltpu.make_async_copy(ref, buf.at[s // group % 2, pl.ds(s % group * blk, blk), :], sem.at[s // group % 2, s % group])
        for s, ref in enumerate(refs)
    ]
    groups = [copies[s : s + group] for s in range(0, len(refs), group)]

    @pl.when(step == 0)
    def _():
        for copy in groups[0]:
            copy.start()

    for s, mine in enumerate(groups):

        @pl.when(step == s)
        def _(s=s, mine=mine):
            if s + 1 < len(groups):
                for copy in groups[s + 1]:
                    copy.start()
            for copy in mine:
                copy.wait()


def give_slot(step, value, refs, buf, sem):
    blk = refs[0].shape[0]
    group = buf.shape[1] // blk
    copies = [
        pltpu.make_async_copy(buf.at[s // group % 2, pl.ds(s % group * blk, blk), :], ref, sem.at[s // group % 2, s % group])
        for s, ref in enumerate(refs)
    ]
    groups = [copies[s : s + group] for s in range(0, len(refs), group)]
    count = len(groups)
    for s in range(2, count):

        @pl.when(step == s)
        def _(s=s):
            for copy in groups[s - 2]:
                copy.wait()

    buf[step % 2] = value
    for s in range(count):

        @pl.when(step == s)
        def _(s=s):
            for copy in groups[s]:
                copy.start()
            if s == count - 1:
                for k in range(max(0, count - 2), count):
                    for copy in groups[k]:
                        copy.wait()


def staging(group, blk, dim):
    return [pltpu.VMEM((2, group * blk, dim), bf16), pltpu.SemaphoreType.DMA((2, group))]


def group_of(count):
    return 2 - count % 2


def run_copies(moves, sem):
    copies = [pltpu.make_async_copy(source, target, sem.at[k]) for k, (source, target) in enumerate(moves)]
    for copy in copies:
        copy.start()
    return copies


def cut_first_kernel(n, count, c_ref, qkv_ref, *refs):
    small_refs, first_ref, vectors, sem = refs[:count], refs[count], refs[count + 1 : -1], refs[-1]
    rows, dim = qkv_ref.shape[0], qkv_ref.shape[1] // 3
    w = dim // n
    moves = list(zip(small_refs, vectors, strict=True))
    for i in range(3):
        at = pl.multiple_of(i * dim + c_ref[0] * w, w)
        moves.append((qkv_ref.at[:, pl.ds(at, w)], first_ref.at[pl.ds(0, rows), pl.ds(i * w, w)]))
    copies = run_copies(moves, sem)
    for copy in copies[:count]:
        copy.wait()
    k = 0
    for vector in vectors:
        for at in range(0, vector.shape[0], LANES):
            value = vector[at : at + LANES].reshape(1, LANES)
            first_ref[rows + k // 3 : rows + k // 3 + 1, (k % 3) * LANES : (k % 3 + 1) * LANES] = value
            k += 1
    for copy in copies[count:]:
        copy.wait()


def cut_first(c, w_qkv, small, n):
    rows, dim = w_qkv.shape[0], w_qkv.shape[1] // 3
    return pl.pallas_call(
        functools.partial(cut_first_kernel, n, len(small)),
        in_specs=[SMEM] + [ANY] * (1 + len(small)),
        out_specs=VMEM,
        out_shape=jax.ShapeDtypeStruct((rows + sum(a.shape[0] for a in small) // LANES // 3, 3 * dim // n), bf16),
        scratch_shapes=[pltpu.VMEM(a.shape, bf16) for a in small] + [pltpu.SemaphoreType.DMA((3 + len(small),))],
        compiler_params=params(63),
        cost_estimate=cost(0, MIB),
    )(c, w_qkv, *small)


def cut_second_kernel(n, nz, c_ref, up_ref, down_ref, out_ref, sem):
    c = c_ref[0]
    fb, half = down_ref.shape[0] // n, up_ref.shape[0] // 2
    moves = [(down_ref.at[pl.ds(pl.multiple_of(c * fb, fb), fb), :], out_ref.at[pl.ds(0, fb), :])]
    for i in range(nz):
        at = pl.multiple_of((i * n + c) * fb, fb)
        for side in range(2):
            target = out_ref.at[pl.ds(fb, half), pl.ds((side * nz + i) * fb, fb)]
            moves.append((up_ref.at[pl.ds(side * half, half), pl.ds(at, fb)], target))
    for copy in run_copies(moves, sem):
        copy.wait()


def cut_second(c, w_up, w_down, n, nz):
    out = (w_down.shape[0] // n + w_up.shape[0] // 2, w_down.shape[1])
    return pl.pallas_call(
        functools.partial(cut_second_kernel, n, nz),
        in_specs=[SMEM, ANY, ANY],
        out_specs=VMEM,
        out_shape=jax.ShapeDtypeStruct(out, bf16),
        scratch_shapes=[pltpu.SemaphoreType.DMA((1 + 2 * nz,))],
        compiler_params=params(),
        cost_estimate=cost(0, 2 * MIB),
    )(c, w_up, w_down)


def shard_of(z, k, nz):
    return jnp.where(z >= k, z - k, z - k + nz)


def pick_row(rows, which):
    picked = rows[0:1]
    for r in range(1, rows.shape[0]):
        picked = jnp.where(which == r, rows[r : r + 1], picked)
    return picked


def join_first_kernel(nz, n, at_ref, sc_ref, sl_ref, *refs):
    pieces, (w_ref, v_ref, qv_ref, up_ref) = refs[:nz], refs[nz:]
    c, z = at_ref[0], at_ref[1]
    shard = w_ref.shape[0] // nz
    per = shard // LANES
    for i, ref in enumerate(pieces):
        t = shard_of(z, i, nz)
        w_ref[pl.ds(pl.multiple_of(t * shard, shard), shard), :] = ref[:shard, :]
        for k in range((ref.shape[0] - shard) * 3):
            row = shard + k // 3
            value = ref[row : row + 1, (k % 3) * LANES : (k % 3 + 1) * LANES].astype(f32)
            at = pl.multiple_of(t * shard + (k % per) * LANES, LANES)
            v_ref[k // per : k // per + 1, pl.ds(at, LANES)] = value
    group = 2 * per
    for i in range(2):
        d = c + i * n
        at = pl.multiple_of((d // group) * shard + (d % per) * LANES, LANES)
        qv_ref[i : i + 1, :] = pick_row(v_ref[6:8, pl.ds(at, LANES)], d % group // per)
    for t in range(nz):
        at = pl.multiple_of(t * shard + (c % per) * LANES, LANES)
        up_ref[:, t * LANES : (t + 1) * LANES] = pick_row(v_ref[8:12, pl.ds(at, LANES)], c // per)


def join_first(at, sc, slopes, pieces, n, nz, shard):
    width = pieces[0].shape[1]
    small = (pieces[0].shape[0] - shard) * 3 * LANES // shard
    return pl.pallas_call(
        functools.partial(join_first_kernel, nz, n),
        in_specs=[SMEM] * 3 + [VMEM] * nz,
        out_shape=[
            jax.ShapeDtypeStruct((nz * shard, width), bf16),
            jax.ShapeDtypeStruct((small, nz * shard), f32),
            jax.ShapeDtypeStruct((2, LANES), f32),
            jax.ShapeDtypeStruct((1, nz * LANES), f32),
        ],
        compiler_params=params(),
        cost_estimate=cost(0, 2 * MIB),
    )(at, sc, slopes, *pieces)


def join_second_kernel(nz, at_ref, *refs):
    pieces, (up_ref, down_ref) = refs[:nz], refs[nz:]
    z = at_ref[1]
    shard = up_ref.shape[0] // nz
    fl = up_ref.shape[1]
    fb, half = fl // nz, shard // 2
    for i, ref in enumerate(pieces):
        t = shard_of(z, i, nz)
        down_ref[pl.ds(pl.multiple_of(t * fb, fb), fb), :] = ref[:fb, :]
        for side in range(2):
            at = pl.multiple_of(t * shard + side * half, half)
            up_ref[pl.ds(at, half), :] = ref[fb:, side * fl : (side + 1) * fl]


def join_second(at, pieces, nz, shard, fl):
    dim = pieces[0].shape[1]
    return pl.pallas_call(
        functools.partial(join_second_kernel, nz),
        in_specs=[SMEM] + [VMEM] * nz,
        out_shape=[jax.ShapeDtypeStruct((nz * shard, fl), bf16), jax.ShapeDtypeStruct((fl, dim), bf16)],
        compiler_params=params(),
        cost_estimate=cost(0, 6 * MIB),
    )(at, *pieces)


def stack_kernel(nz, at_ref, *refs):
    pieces, out_ref = refs[:nz], refs[nz]
    rows = pieces[0].shape[0]
    for i, ref in enumerate(pieces):
        at = pl.multiple_of(shard_of(at_ref[1], i, nz) * rows, rows)
        out_ref[pl.ds(at, rows), :] = ref[...]


def stack_shards(at, pieces, nz):
    rows, dim = pieces[0].shape
    return pl.pallas_call(
        functools.partial(stack_kernel, nz),
        in_specs=[SMEM] + [VMEM] * nz,
        out_shape=jax.ShapeDtypeStruct((nz * rows, dim), bf16),
        compiler_params=params(),
        cost_estimate=cost(0, MIB // 2),
    )(at, *pieces)


def join_dense_kernel(n, nz, sc_ref, *refs):
    slots, out_ref = refs[:n], refs[n]
    rest = slots[0].shape[0] // nz
    for p, ref in enumerate(slots):
        for t in range(nz):
            at = pl.multiple_of(t * n * rest + sc_ref[1 + n + p] * rest, rest)
            out_ref[pl.ds(at, rest), :] = ref[t * rest : (t + 1) * rest, :]


def join_dense(sc, slots, n, nz):
    rows, dim = slots[0].shape
    return pl.pallas_call(
        functools.partial(join_dense_kernel, n, nz),
        in_specs=[SMEM] + [VMEM] * n,
        out_shape=jax.ShapeDtypeStruct((n * rows, dim), bf16),
        compiler_params=params(),
        cost_estimate=cost(0, 4 * MIB),
    )(sc, *slots)


def ln_qkv_kernel(count, *refs):
    slots, (g_ref, s_ref, w_ref, b_ref, h_ref, q_ref, k_ref, v_ref, buf, sem) = refs[:count], refs[count:]
    step = pl.program_id(0)
    take_slot(step, slots, buf, sem)
    width = q_ref.shape[1]

    def norm(at):
        normed, _ = normalize(buf[step % 2, at, :].astype(f32))
        h_ref[at, :] = (normed * g_ref[...] + s_ref[...]).astype(bf16)

    by_rows(h_ref.shape[0], norm, 256)
    p = dot(h_ref[...], w_ref[...])
    q_ref[...] = (p[:, :width] + b_ref[0:1, :]).astype(bf16)
    k_ref[...] = p[:, width : 2 * width].astype(bf16)
    v_ref[...] = (p[:, 2 * width :] + b_ref[1:2, :]).astype(bf16)


def ln_qkv(slots, gain, shift, weight, bias, blk):
    n = len(slots)
    rows, dim = n * blk, weight.shape[0]
    width = weight.shape[1] // 3
    full = lambda a: pl.BlockSpec(a.shape, lambda i: (0, 0))
    group = group_of(n)
    tok = lambda cols: pl.BlockSpec((group * blk, cols), lambda i: (i, 0))
    out = lambda cols: jax.ShapeDtypeStruct((rows, cols), bf16)
    return pl.pallas_call(
        functools.partial(ln_qkv_kernel, n),
        grid=(n // group,),
        in_specs=[ANY] * n + [full(gain), full(shift), full(weight), full(bias)],
        out_specs=[tok(dim), tok(width), tok(width), tok(width)],
        out_shape=[out(dim), out(width), out(width), out(width)],
        scratch_shapes=staging(group, blk, dim),
        compiler_params=params(),
        cost_estimate=cost(6 * rows * dim * width, 4 * rows * dim),
    )(*slots, gain, shift, weight, bias)


def stacked(x, masks):
    zero = jnp.zeros_like(x)
    return jnp.concatenate([jnp.where(m, x, zero) for m in masks], axis=0)


def slope_lanes(sl_ref, hp, blk, w, first_query, b):
    lane = lax.broadcasted_iota(jnp.int32, (blk, w), 1)
    row = first_query + lax.broadcasted_iota(jnp.int32, (blk, w), 0)
    out = []
    for h in range(hp):
        slope = jnp.full((blk, w), sl_ref[h])
        high = slope.astype(bf16).astype(f32)
        mid = (slope - high).astype(bf16).astype(f32)
        low = slope - high - mid
        part = lane % 4
        value = jnp.where(part == 0, high, jnp.where(part == 1, mid, low))
        value = jnp.where(lane >= 4, value * blk, value)
        value = jnp.where((part == 3) | (lane >= 8), 0.0, value)
        value = jnp.where((lane == 3) & (row >= b), MASKED_SCORE, value)
        out.append(value.astype(bf16))
    return out


def key_lanes(blk, w, block, b):
    lane = lax.broadcasted_iota(jnp.int32, (blk, w), 1)
    row = lax.broadcasted_iota(jnp.int32, (blk, w), 0)
    value = jnp.where(lane < 4, row, block)
    value = jnp.where(lane == 3, jnp.where(block * blk + row < b, 1, 0), value)
    return jnp.where(lane < 8, value, 0).astype(f32).astype(bf16)


def causal(blk, cols):
    row = lax.broadcasted_iota(jnp.int32, (blk, cols), 0)
    col = lax.broadcasted_iota(jnp.int32, (blk, cols), 1) & (blk - 1)
    return jnp.where(row <= col, 0.0, MASKED_SCORE).astype(f32)


def attn_fwd_kernel(hp, blk, first, sc_ref, sl_ref, q_ref, k_ref, v_ref, *refs):
    o_ref, lse_ref, kx_ref, vt_ref, late_ref = refs[-5:]
    i = pl.program_id(0) + first
    b = sc_ref[0]
    nb, w = k_ref.shape[0] // blk, q_ref.shape[1]
    cols = hp * blk

    @pl.when(pl.program_id(0) == 0)
    def _():
        late_ref[...] = causal(blk, cols)
        for h in range(hp):
            vt_ref[h, HEAD:, :] = jnp.ones((16, nb * blk), bf16)
        for s in range(nb):
            at = pl.ds(pl.multiple_of(sc_ref[1 + s] * blk, blk), blk)
            rows = slice(s * blk, (s + 1) * blk)
            kx_ref[rows, :w] = k_ref[at, :]
            kx_ref[rows, w:] = key_lanes(blk, w, s, b)
            turned = jnp.transpose(v_ref[at, :].astype(f32)).astype(bf16)
            for h in range(hp):
                vt_ref[h, :HEAD, rows] = turned[h * HEAD : (h + 1) * HEAD, :]

    q2 = stacked(q_ref[...] * jnp.asarray(0.125, bf16), head_masks(hp, w))
    q2 = jnp.concatenate([q2, jnp.concatenate(slope_lanes(sl_ref, hp, blk, w, i * blk, b), axis=0)], axis=1)

    def chunk(j, carry, count, diagonal=False):
        m, accs = carry
        keys = pl.ds(pl.multiple_of(j * blk, blk), count * blk)
        s = dot_nt(kx_ref[keys, :], q2)
        if diagonal:
            last = s[(count - 1) * blk :] + late_ref[...]
            s = last if count == 1 else jnp.concatenate([s[: (count - 1) * blk], last], axis=0)
        mn = jnp.maximum(m, jnp.max(s, axis=0, keepdims=True))
        p = jnp.exp(s - mn).astype(bf16)
        alpha = jnp.exp(m - mn)
        out = []
        for h in range(hp):
            part = slice(h * blk, (h + 1) * blk)
            out.append(accs[h] * alpha[:, part] + dot(vt_ref[h, :, keys], p[:, part]))
        return mn, tuple(out)

    carry = (jnp.full((1, cols), MASKED_SCORE, f32), tuple(jnp.zeros((HEAD + 16, blk), f32) for _ in range(hp)))
    lo = jnp.where(i * blk < b, 0, b // blk)
    count = i - lo
    odd = count % 3
    carry = lax.switch(odd, [lambda cy, k=k: chunk(i - k, cy, k + 1, True) for k in range(3)], carry)
    m, accs = lax.fori_loop(0, count // 3, lambda t, cy: chunk(lo + 3 * t, cy, 3), carry)
    turned = jnp.concatenate([acc[:HEAD] / acc[HEAD : HEAD + 1] for acc in accs], axis=0)
    o_ref[...] = jnp.transpose(turned).astype(bf16)
    lse_ref[...] = m + jnp.log(jnp.concatenate([acc[HEAD : HEAD + 1] for acc in accs], axis=1))


def attn_fwd(sc, sl, q, k, v, blk, hp, first, count, so_far=()):
    S, w = q.shape
    so_far = list(so_far)
    return pl.pallas_call(
        functools.partial(attn_fwd_kernel, hp, blk, first),
        grid_spec=pltpu.PrefetchScalarGridSpec(
            num_scalar_prefetch=2,
            grid=(count,),
            in_specs=[
                pl.BlockSpec((blk, w), lambda i, sc, sl: (sc[1 + first + i], 0)),
                pl.BlockSpec((S, w), lambda i, sc, sl: (0, 0)),
                pl.BlockSpec((S, w), lambda i, sc, sl: (0, 0)),
            ]
            + [ANY] * len(so_far),
            out_specs=[
                pl.BlockSpec((blk, w), lambda i, sc, sl: (first + i, 0)),
                pl.BlockSpec((1, hp * blk), lambda i, sc, sl: (0, first + i)),
            ],
            scratch_shapes=[pltpu.VMEM((S, 2 * w), bf16), pltpu.VMEM((hp, HEAD + 16, S), bf16), pltpu.VMEM((blk, hp * blk), f32)],
        ),
        out_shape=[jax.ShapeDtypeStruct((S, w), bf16), jax.ShapeDtypeStruct((1, S * hp), f32)],
        input_output_aliases={5 + k: k for k in range(len(so_far))},
        compiler_params=params(),
        cost_estimate=cost(4 * S * count * blk * w, 8 * S * w, S * count * blk * hp // 2),
    )(sc, sl, q, k, v, *so_far)


def attn_bwd_kernel(hp, blk, sc_ref, sl_ref, q_ref, k_ref, v_ref, do_ref, o_ref, lse_ref, g_ref, gb_ref, q2_ref, do2_ref, delta_ref, dq_ref, late_ref, dk_ref, dv_ref):
    j = pl.program_id(0)
    nb = pl.num_programs(0)
    b = sc_ref[0]
    w = k_ref.shape[1]
    cols = hp * blk
    masks = head_masks(hp, w)

    @pl.when(j == 0)
    def _():
        pick = (lax.broadcasted_iota(jnp.int32, (8, w), 1) // HEAD == lax.broadcasted_iota(jnp.int32, (8, w), 0)).astype(bf16)
        gb_ref[...] = jnp.zeros_like(gb_ref)
        late_ref[...] = causal(blk, cols)

        def prepare(i, _):
            at = pl.multiple_of(sc_ref[1 + i] * blk, blk)
            rows = pl.ds(pl.multiple_of(i * cols, cols), cols)
            do = do_ref[pl.ds(pl.multiple_of(i * blk, blk), blk), :]
            q2_ref[rows, :w] = stacked(q_ref[pl.ds(at, blk), :] * jnp.asarray(0.125, bf16), masks)
            q2_ref[rows, w:] = jnp.concatenate(slope_lanes(sl_ref, hp, blk, w, i * blk, b), axis=0)
            do2_ref[rows, :] = stacked(do, masks)
            prod = do.astype(f32) * o_ref[pl.ds(pl.multiple_of(i * blk, blk), blk), :].astype(f32)
            high = prod.astype(bf16)
            d = dot_nt(pick, high) + dot_nt(pick, (prod - high.astype(f32)).astype(bf16))
            for h in range(hp):
                delta_ref[:, pl.ds(pl.multiple_of(i * cols + h * blk, blk), blk)] = d[h : h + 1, :]
            dq_ref[i] = jnp.zeros((w, blk), f32)
            return 0

        lax.fori_loop(0, nb, prepare, 0)

    k = k_ref[...]
    v = v_ref[...]
    kx = jnp.concatenate([k, key_lanes(blk, w, j, b)], axis=1)
    kt = jnp.transpose(k.astype(f32)).astype(bf16)

    def chunk(i, count, diagonal=False):
        at = pl.ds(pl.multiple_of(i * cols, cols), count * cols)
        s = dot_nt(kx, q2_ref[at, :])
        if diagonal:
            s = s + late_ref[...]
        p = jnp.exp(s - lse_ref[:, at])
        ds = (p * (dot_nt(v, do2_ref[at, :]) - delta_ref[:, at])).astype(bf16)
        dv = dot(p.astype(bf16), do2_ref[at, :])
        dk = dot(ds, q2_ref[at, :w])
        if diagonal:
            dv_ref[...] = dv
            dk_ref[...] = dk
        else:
            dv_ref[...] += dv
            dk_ref[...] += dk
        for t in range(count):
            for h in range(hp):
                rows = slice(h * HEAD, (h + 1) * HEAD)
                first = t * cols + h * blk
                dq_ref[i + t, rows, :] += dot(kt[rows, :], ds[:, first : first + blk])

    chunk(j, 1, True)
    hi = jnp.where((j + 1) * blk <= b, (b + blk - 1) // blk, nb)
    count = hi - j - 1
    lax.fori_loop(0, count // 2, lambda t, _: (chunk(j + 1 + 2 * t, 2), 0)[1], 0)
    for k in range(1, 2):

        @pl.when(count % 2 == k)
        def _(k=k):
            chunk(hi - k, k)

    dq = jnp.transpose(dq_ref[j]) * 0.125
    dv = dv_ref[...]
    g_ref[:, 0:w] = dq.astype(bf16)
    g_ref[:, w : 2 * w] = dk_ref[...].astype(bf16)
    g_ref[:, 2 * w : 3 * w] = dv.astype(bf16)
    gb_ref[0:1, :] += jnp.sum(dq, axis=0, keepdims=True)
    gb_ref[1:2, :] += jnp.sum(dv, axis=0, keepdims=True)


def attn_bwd(sc, sl, q, k, v, do, o, lse, blk, hp):
    S, w = q.shape
    nb = S // blk
    full = lambda shape: pl.BlockSpec(shape, lambda j, sc, sl: (0,) * len(shape))
    slot = lambda width: pl.BlockSpec((blk, width), lambda j, sc, sl: (sc[1 + j], 0))
    return pl.pallas_call(
        functools.partial(attn_bwd_kernel, hp, blk),
        grid_spec=pltpu.PrefetchScalarGridSpec(
            num_scalar_prefetch=2, grid=(nb,),
            in_specs=[full((S, w)), slot(w), slot(w), full((S, w)), full((S, w)), full((1, S * hp))],
            out_specs=[slot(3 * w), full((8, w))],
            scratch_shapes=[
                pltpu.VMEM((S * hp, 2 * w), bf16),
                pltpu.VMEM((S * hp, w), bf16),
                pltpu.VMEM((1, S * hp), f32),
                pltpu.VMEM((nb, w, blk), f32),
                pltpu.VMEM((blk, hp * blk), f32),
                pltpu.VMEM((blk, w), f32),
                pltpu.VMEM((blk, w), f32),
            ],
        ),
        out_shape=[jax.ShapeDtypeStruct((S, 3 * w), bf16), jax.ShapeDtypeStruct((8, w), f32)],
        compiler_params=params(),
        cost_estimate=cost(10 * S * S * w, 16 * S * w, S * S * hp // 2),
    )(sc, sl, q, k, v, do, o, lse)


def side_by_side(ref):
    return jnp.concatenate([ref[p] for p in range(ref.shape[0])], axis=1)


def dense_ln_kernel(x_ref, o_ref, w_ref, v_ref, y_ref, h_ref):
    y_ref[...] = dot(side_by_side(o_ref), w_ref[...])

    def norm(at):
        y = x_ref[at, :].astype(f32) + (y_ref[at, :] + v_ref[2:3, :])
        y_ref[at, :] = y
        normed, _ = normalize(y)
        h_ref[at, :] = (normed * v_ref[3:4, :] + v_ref[4:5, :]).astype(bf16)

    by_rows(x_ref.shape[0], norm, 128)


def dense_ln(x, o, weight, vectors):
    rows, dim = x.shape
    return pl.pallas_call(
        dense_ln_kernel,
        out_shape=[jax.ShapeDtypeStruct((rows, dim), f32), jax.ShapeDtypeStruct((rows, dim), bf16)],
        compiler_params=params(),
        cost_estimate=cost(2 * rows * dim * dim, 2 * dim * dim + 12 * rows * dim),
    )(x, o, weight, vectors)


def dz_kernel(count, *refs):
    slots, (w_ref, all_ref, dz_ref, buf, sem) = refs[:count], refs[count:]
    step = pl.program_id(0)
    take_slot(step, slots, buf, sem)
    cot = buf[step % 2]
    all_ref[...] = cot
    dz_ref[...] = dot_nt(cot, w_ref[...]).astype(bf16)


def dz_blocks(slots, down, blk):
    n, (width, dim) = len(slots), down.shape
    group = group_of(n)
    tok = lambda cols: pl.BlockSpec((group * blk, cols), lambda i: (i, 0))
    return pl.pallas_call(
        functools.partial(dz_kernel, n),
        grid=(n // group,),
        in_specs=[ANY] * n + [pl.BlockSpec(down.shape, lambda i: (0, 0))],
        out_specs=[tok(dim), tok(width)],
        out_shape=[jax.ShapeDtypeStruct((n * blk, dim), bf16), jax.ShapeDtypeStruct((n * blk, width), bf16)],
        scratch_shapes=staging(group, blk, dim),
        compiler_params=params(),
        cost_estimate=cost(2 * n * blk * dim * width, 4 * n * blk * (dim + width)),
    )(*slots, down)


def mlp_kernel(count, extra, *refs):
    h_slots, (dz_ref, u_ref, b_ref) = refs[:count], refs[count : count + 3]
    refs = refs[count + 3 + extra :]
    hall_ref, z_ref, du_ref, gb_ref = refs[:4]
    dh_slots, (hbuf, hsem, dbuf, dsem) = refs[4 : 4 + count], refs[4 + count :]
    step = pl.program_id(0)
    take_slot(step, h_slots, hbuf, hsem)
    h = hbuf[step % 2]
    hall_ref[...] = h
    value, deriv = gelu_pair(dot(h, u_ref[...]) + b_ref[...])
    z_ref[...] = value.astype(bf16)
    du = dz_ref[...].astype(f32) * deriv

    @pl.when(step == 0)
    def _():
        gb_ref[...] = jnp.zeros_like(gb_ref)

    gb_ref[...] += rowsum(du)
    du = du.astype(bf16)
    du_ref[...] = du
    give_slot(step, dot_nt(du, u_ref[...]).astype(bf16), dh_slots, dbuf, dsem)


def mlp(h_slots, dz, up, bias, blk, n, first, so_far=()):
    count = len(h_slots)
    dim, width = up.shape
    full = lambda a: pl.BlockSpec(a.shape, lambda i: (0, 0))
    group = group_of(count)
    tok = lambda cols: pl.BlockSpec((group * blk, cols), lambda i: (first // group + i, 0))
    out = lambda rows, cols: jax.ShapeDtypeStruct((rows, cols), bf16)
    so_far = list(so_far)
    res = pl.pallas_call(
        functools.partial(mlp_kernel, count, len(so_far)),
        grid=(count // group,),
        in_specs=[ANY] * count + [tok(width), full(up), full(bias)] + [ANY] * len(so_far),
        out_specs=[tok(dim), tok(width), tok(width), pl.BlockSpec((1, width), lambda i: (0, 0))] + [ANY] * count,
        out_shape=[out(n * blk, dim), out(n * blk, width), out(n * blk, width), jax.ShapeDtypeStruct((1, width), f32)]
        + [out(blk, dim)] * count,
        scratch_shapes=staging(group, blk, dim) + staging(group, blk, dim),
        input_output_aliases={count + 3 + k: k for k in range(len(so_far))},
        compiler_params=params(),
        cost_estimate=cost(4 * count * blk * dim * width, count * blk * dim * 10, count * blk * width),
    )(*h_slots, dz, up, bias, *so_far)
    return res[:3], res[3], res[4:]


def to_slots_kernel(count, extra, blk, transposed, a_ref, w_ref, *refs):
    slots, (buf, sem) = refs[extra : extra + count], refs[extra + count :]
    product = (dot_nt if transposed else dot)(a_ref[...], w_ref[...])
    targets = [ref.at[pl.ds(0, blk), :] for ref in slots]
    give_slot(pl.program_id(0), product.astype(bf16), targets, buf, sem)


def to_slots(a, weight, blk, first, count, transposed=False, onto=()):
    dim = weight.shape[0 if transposed else 1]
    onto = list(onto)
    group = group_of(count)
    return pl.pallas_call(
        functools.partial(to_slots_kernel, count, len(onto), blk, transposed),
        grid=(count // group,),
        in_specs=[pl.BlockSpec((group * blk, a.shape[1]), lambda i: (first // group + i, 0)), pl.BlockSpec(weight.shape, lambda i: (0, 0))]
        + [ANY] * len(onto),
        out_specs=[ANY] * count,
        out_shape=[jax.ShapeDtypeStruct(onto[k].shape if onto else (blk, dim), bf16) for k in range(count)],
        scratch_shapes=staging(group, blk, dim),
        input_output_aliases={2 + k: k for k in range(len(onto))},
        compiler_params=params(),
        cost_estimate=cost(2 * count * blk * a.shape[1] * dim, 2 * count * blk * (a.shape[1] + dim)),
    )(a, weight, *onto)


def summed(parts, at):
    return sum(ref[at, :].astype(f32) for ref in parts)


def ln2_back_kernel(count, *refs):
    parts, (y_ref, cot_ref, w_ref, v_ref, dy_ref, dyb_ref, do_ref, gs_ref) = refs[:count], refs[count:]
    gs_ref[...] = jnp.zeros_like(gs_ref)

    def norm(at):
        normed, inv_std = normalize(y_ref[at, :])
        dh = summed(parts, at)
        cot = cot_ref[at, :].astype(f32)
        dy = cot + norm_backward(dh, normed, inv_std, v_ref[3:4, :])
        dy_ref[at, :] = dy
        dyb_ref[at, :] = dy.astype(bf16)
        for row, value in enumerate((dy, dh * normed, dh, cot)):
            gs_ref[row : row + 1, :] += rowsum(value)

    by_rows(y_ref.shape[0], norm, 128)
    do = dot_nt(dyb_ref[...], w_ref[...]).astype(bf16)
    width = do_ref.shape[2]
    for p in range(do_ref.shape[0]):
        do_ref[p] = do[:, p * width : (p + 1) * width]


def ln2_back(parts, y, cot, weight, vectors, n):
    rows, dim = y.shape
    return pl.pallas_call(
        functools.partial(ln2_back_kernel, len(parts)),
        out_shape=[
            jax.ShapeDtypeStruct((rows, dim), f32),
            jax.ShapeDtypeStruct((rows, dim), bf16),
            jax.ShapeDtypeStruct((n, rows, dim // n), bf16),
            jax.ShapeDtypeStruct((4, dim), f32),
        ],
        compiler_params=params(),
        cost_estimate=cost(2 * rows * dim * dim, 2 * dim * dim + 20 * rows * dim),
    )(*parts, y, cot, weight, vectors)


def finish_kernel(count, *refs):
    parts, (y_ref, v_ref, out_ref) = refs[:count], refs[count:]

    def add(at):
        out_ref[at, :] = y_ref[at, :] + (summed(parts, at) + v_ref[5:6, :])

    by_rows(y_ref.shape[0], add)


def finish_out(parts, y, vectors):
    return pl.pallas_call(
        functools.partial(finish_kernel, len(parts)),
        out_shape=jax.ShapeDtypeStruct(y.shape, f32),
        compiler_params=params(),
        cost_estimate=cost(y.size, 10 * y.size),
    )(*parts, y, vectors)


def ln1_back_kernel(count, *refs):
    parts, (x_ref, dy_ref, v_ref, out_ref) = refs[:count], refs[count:]

    def norm(at):
        normed, inv_std = normalize(x_ref[at, :].astype(f32))
        out_ref[at, :] = dy_ref[at, :] + norm_backward(summed(parts, at), normed, inv_std, v_ref[0:1, :])

    by_rows(x_ref.shape[0], norm, 128)


def ln1_back(parts, x, dy, vectors):
    return pl.pallas_call(
        functools.partial(ln1_back_kernel, len(parts)),
        out_shape=jax.ShapeDtypeStruct(dy.shape, f32),
        compiler_params=params(),
        cost_estimate=cost(20 * dy.size, 14 * dy.size),
    )(*parts, x, dy, vectors)


def shard_at(z, i, nz):
    return lax.rem(z + i, nz)


def grad_kernel(nz, fold, z_ref, a_ref, b_ref, *refs):
    outs, acc_ref = refs[-nz - 1 : -1], refs[-1]
    acc_ref[...] = dot_tn(a_ref[...], b_ref[...])
    cols = acc_ref.shape[1]
    for i, ref in enumerate(outs):
        rows = ref.shape[0]
        base = shard_at(z_ref[0], i, nz) * rows * fold
        for side in range(fold):
            at = pl.ds(pl.multiple_of(base + side * rows, rows), rows)
            ref[:, side * cols : (side + 1) * cols] = acc_ref[at, :].astype(bf16)


def grad_blocks(z, a, b, nz, fold, part, so_far=()):
    rows, cols = a.shape[1] // nz // fold, fold * b.shape[1]
    so_far = list(so_far)
    return pl.pallas_call(
        functools.partial(grad_kernel, nz, fold),
        grid=(1,),
        in_specs=[SMEM, VMEM, VMEM] + [ANY] * len(so_far),
        out_specs=[pl.BlockSpec((rows, cols), lambda i: (part, 0))] * nz,
        out_shape=[jax.ShapeDtypeStruct((2 * rows, cols), bf16)] * nz,
        scratch_shapes=[pltpu.VMEM((a.shape[1], b.shape[1]), f32)],
        input_output_aliases={3 + k: k for k in range(len(so_far))},
        compiler_params=params(),
        cost_estimate=cost(2 * a.size * b.shape[1], 2 * (a.size + b.size)),
    )(z, a, b, *so_far)


def split_nt(wide, narrow, swapped=False):
    high = wide.astype(bf16)
    terms = (high, (wide - high.astype(f32)).astype(bf16))
    return sum(dot_nt(narrow, t) if swapped else dot_nt(t, narrow) for t in terms)


def grad_qkv_kernel(nz, z_ref, h_ref, g_ref, s_ref, w_ref, v_ref, *refs):
    outs, (acc_ref, row_ref) = refs[:nz], refs[nz:]
    w = g_ref.shape[1] // 3
    shard = h_ref.shape[1] // nz
    acc_ref[...] = dot_tn(h_ref[...], g_ref[...])
    column = dot(jnp.ones((8, g_ref.shape[0]), bf16), g_ref[...])

    def sums(at):
        weight = w_ref[at, :]
        shift = split_nt(column, weight)[0:1]
        gain = split_nt(acc_ref[at, :] * weight.astype(f32), jnp.ones((8, 3 * w), bf16), True)[0:1]
        row_ref[0:1, at] = (gain - v_ref[1:2, at] * shift) / v_ref[0:1, at]
        row_ref[1:2, at] = shift

    by_rows(acc_ref.shape[0], sums, shard)
    per = shard // LANES
    base = 3 * shard
    for k, ref in enumerate(outs):
        t = shard_at(z_ref[0], k, nz)
        grad = acc_ref[pl.ds(pl.multiple_of(t * shard, shard), shard), :].astype(bf16)
        for i in range(3):
            ref[i * shard : (i + 1) * shard, :] = grad[:, i * w : (i + 1) * w]
        ref[base:, :] = s_ref[t].astype(bf16)
        for e in range(per):
            pair = row_ref[0:8, pl.ds(pl.multiple_of(t * shard + e * LANES, LANES), LANES)].astype(bf16)
            for v in range(2):
                row = base + v * per + e
                ref[row : row + 1, :] = pair[v : v + 1]


def grad_qkv(z, h, g, small, weight, vectors, nz):
    rows, dim = h.shape
    shard, w = dim // nz, g.shape[1] // 3
    out = (3 * shard + small.shape[1], w)
    return pl.pallas_call(
        functools.partial(grad_qkv_kernel, nz),
        in_specs=[SMEM] + [VMEM] * 5,
        out_shape=[jax.ShapeDtypeStruct(out, bf16)] * nz,
        scratch_shapes=[pltpu.VMEM((dim, 3 * w), f32), pltpu.VMEM((8, dim), f32)],
        compiler_params=params(),
        cost_estimate=cost(6 * rows * dim * w, 2 * rows * (dim + 3 * w)),
    )(z, h, g, small, weight, vectors)


def grad_dense_kernel(n, nz, at_ref, sc_ref, o_ref, d_ref, *refs):
    outs, acc_ref = refs[:n], refs[n]
    z = at_ref[1]
    acc_ref[...] = dot_tn(side_by_side(o_ref), d_ref[...])
    rest = acc_ref.shape[0] // (n * nz)
    for p, ref in enumerate(outs):
        for i in range(nz):
            at = shard_at(z, i, nz) * n * rest + sc_ref[1 + n + p] * rest
            ref[i * rest : (i + 1) * rest, :] = acc_ref[pl.ds(pl.multiple_of(at, rest), rest), :].astype(bf16)


def grad_dense(at, sc, o, dyb, n, nz):
    rows, dim = dyb.shape
    rest = dim // n
    return pl.pallas_call(
        functools.partial(grad_dense_kernel, n, nz),
        grid=(1,),
        in_specs=[SMEM, SMEM, VMEM, VMEM],
        out_specs=[pl.BlockSpec((rest, dim), lambda i: (rows // rest, 0))] * n,
        out_shape=[jax.ShapeDtypeStruct((rows + rest, dim), bf16)] * n,
        scratch_shapes=[pltpu.VMEM((dim, dim), f32)],
        compiler_params=params(),
        cost_estimate=cost(2 * rows * dim * dim, 2 * dim * dim),
    )(at, sc, o, dyb)


def small_kernel(n, nz, c_ref, s_ref, qv_ref, *refs):
    out_ref = refs[-1]
    c = c_ref[0]
    out_ref[...] = jnp.zeros_like(out_ref)
    shard = s_ref.shape[1] // nz
    per = shard // LANES
    up = sum(ref[...] for ref in refs[:-1])
    for t in range(nz):
        for v in range(4):
            for e in range(per):
                at = t * shard + e * LANES
                row = (v + 2) * per + e
                out_ref[t, row : row + 1, :] = s_ref[v : v + 1, at : at + LANES]
        out_ref[t, pl.ds(8 * per + c, 1), :] = up[:, t * LANES : (t + 1) * LANES]
    row = 6 * per + c % (2 * per)
    out_ref[c // (2 * per), pl.ds(row, 1), :] = qv_ref[0:1, :]
    out_ref[nz // 2 + c // (2 * per), pl.ds(row, 1), :] = qv_ref[1:2, :]


def small_grads(c, sums, qv, ups, n, nz):
    dim = sums.shape[1]
    return pl.pallas_call(
        functools.partial(small_kernel, n, nz),
        in_specs=[SMEM] + [VMEM] * (2 + len(ups)),
        out_shape=jax.ShapeDtypeStruct((nz, 12 * dim // nz // LANES, LANES), f32),
        compiler_params=params(),
        cost_estimate=cost(0, 1 << 16),
    )(c, sums, qv, *ups)


def spread_kernel(first, n, count, outs, small, small_row, others, extra, sc_ref, *refs):
    slots, more, refs = refs[:count], refs[count : count + others], refs[count + others + extra :]
    out_refs, refs = refs[: len(outs)], refs[len(outs) :]
    sums, (wide, osem) = refs[:-2], refs[-2:]
    started = []
    for s, slot in enumerate(slots):
        block_of = sc_ref[1 + n + first + s]
        wide[s] = slot[...].astype(f32)
        k = 0
        for ref, blocks in zip(out_refs, outs, strict=True):
            for row, col, height, width, trow, tcol, by_row in blocks:
                if by_row:
                    target = ref.at[pl.ds(pl.multiple_of(trow + block_of * height, 8), height), pl.ds(tcol, width)]
                else:
                    target = ref.at[pl.ds(trow, height), pl.ds(pl.multiple_of(tcol + block_of * width, LANES), width)]
                source = wide.at[s, pl.ds(row, height), pl.ds(col, width)]
                started.append(pltpu.make_async_copy(source, target, osem.at[s, k]))
                started[-1].start()
                k += 1
    if small:
        held = slice(small_row, small_row + sum(small) // LANES)
        total = wide[0, held, :]
        for s in range(1, count):
            total = total + wide[s, held, :]
        for ref in more:
            total = total + ref[held, :].astype(f32)
        row = 0
        for ref, size in zip(sums, small, strict=True):
            for at in range(0, size, LANES):
                ref[at : at + LANES] = total[row : row + 1, :].reshape(LANES)
                row += 1
    for copy in started:
        copy.wait()


def spread(sc, n, first, slots, outs, shapes, so_far=(), small=(), small_row=0, more=()):
    count = len(slots)
    height, width = slots[0].shape
    so_far, small, more = list(so_far), list(small), list(more)
    return pl.pallas_call(
        functools.partial(spread_kernel, first, n, count, outs, small, small_row, len(more), len(so_far)),
        in_specs=[SMEM] + [VMEM] * (count + len(more)) + [ANY] * len(so_far),
        out_specs=[ANY] * len(shapes) + [VMEM] * len(small),
        out_shape=[jax.ShapeDtypeStruct(shape, f32) for shape in shapes + [(size,) for size in small]],
        scratch_shapes=[
            pltpu.VMEM((count, height, width), f32),
            pltpu.SemaphoreType.DMA((count, sum(len(blocks) for blocks in outs))),
        ],
        input_output_aliases={1 + count + len(more) + k: k for k in range(len(so_far))},
        compiler_params=params(),
        cost_estimate=cost(0, 6 * count * height * width),
    )(sc, *slots, *more, *so_far)


def swap(x, n, bit, axis=ROW):
    return lax.ppermute(x, axis, [(i, i ^ bit) for i in range(n)])


def turn(n, first):
    return [(i, i ^ (2 if (i % 2 == 0) == first else 4)) for i in range(n)]


def places(c, n):
    slot = jnp.arange(n, dtype=jnp.int32)

    def moved(s):
        if n != 8:
            return s
        cross = jnp.where(c % 2 == 0, (s == 3) | (s == 5), (s == 2) | (s == 4))
        return jnp.where(cross, s ^ 6, s)

    return jnp.concatenate([moved(slot ^ c), c ^ moved(slot)])


def gather_slots(x, n):
    if n != 8:
        slots = {0: x}
        bit = n >> 1
        while bit:
            for s in list(slots):
                slots[s ^ bit] = swap(slots[s], n, bit)
            bit >>= 1
        return [slots[s] for s in range(n)]
    near = lax.ppermute(x, ROW, turn(n, True))
    side = lax.ppermute(x, ROW, turn(n, False))
    far = lax.ppermute(near, ROW, turn(n, False))
    slots = []
    for part in (x, near, side, far):
        slots += [part, swap(part, n, 1)]
    return slots


def add16(*terms):
    return sum(a.astype(f32) for a in terms).astype(bf16)


def scatter_slots(parts, n):
    if n != 8:
        parts = dict(enumerate(parts))
        bit = 1
        while bit < n:
            for s in [s for s in parts if not s & bit]:
                parts[s] = add16(parts[s], swap(parts.pop(s | bit), n, bit))
            bit <<= 1
        return [parts[0]]
    got = [swap(parts[2 * k + 1], n, 1) for k in range(4)]
    far = lax.ppermute(add16(parts[6], got[3]), ROW, turn(n, False))
    side = lax.ppermute(add16(parts[4], got[2]), ROW, turn(n, False))
    near = lax.ppermute(add16(parts[2], got[1], far), ROW, turn(n, True))
    return [parts[0], got[0], side, near]


def ring(x, nz):
    return [x] + [lax.ppermute(x, SHARDS, [(i, (i + k) % nz) for i in range(nz)]) for k in range(1, nz)]


def over_shards(parts, nz):
    got = [lax.ppermute(parts[k], SHARDS, [(i, (i + k) % nz) for i in range(nz)]) for k in range(1, nz)]
    return add16(parts[0], *got)


def layer(
    hidden_in,
    seq_ids,
    ln1_gain,
    ln1_bias,
    w_qkv,
    b_qv,
    w_dense,
    b_dense,
    ln2_gain,
    ln2_bias,
    w_up,
    b_up,
    w_down,
    b_down,
    cotangent,
    n,
    nz,
    fast,
):
    c = lax.axis_index(ROW).astype(jnp.int32)
    z = lax.axis_index(SHARDS).astype(jnp.int32)
    at = jnp.stack([c, z])
    rows, dim = hidden_in.shape
    seq_len = seq_ids.shape[1]
    shard = dim // nz
    hp = HEADS // n
    w = hp * HEAD
    fb = w_down.shape[0] // n
    fl = nz * fb
    ff = fl * n
    both = (SHARDS, ROW)

    seg = seq_ids[0]
    boundary = jnp.sum((seg == seg[0]).astype(jnp.int32))
    sc = jnp.concatenate([boundary.reshape(1), places(c, n)])
    head = (c * hp + 1 + jnp.arange(hp)).astype(f32)
    slopes = jnp.exp2(-8.0 * head / HEADS) * (8.0 / seq_len)

    x_slots = gather_slots(hidden_in, n)
    cot_slots = gather_slots(cotangent, n)
    small = (ln1_gain, ln1_bias, b_dense, ln2_gain, ln2_bias, b_down, b_qv, b_up)
    if fast:
        first = cut_first(c.reshape(1), w_qkv, small, n)
        second = cut_second(c.reshape(1), w_up, w_down, n, nz)
        wq, vectors, bias_qv, bias_up = join_first(at, sc, slopes, ring(first, nz), n, nz, shard)
        dense = lax.dynamic_slice_in_dim(w_dense, c * (shard // n), shard // n, 0)
        dense = stack_shards(at, ring(dense, nz), nz)
        wd = join_dense(sc, gather_slots(dense, n), n, nz)
        wu, wn = join_second(at, ring(second, nz), nz, shard, fl)
    else:
        small = lax.all_gather(jnp.concatenate(small), SHARDS, axis=0, tiled=False).astype(f32)
        vectors = small[:, : 6 * shard].reshape(nz, 6, shard).transpose(1, 0, 2).reshape(6, dim)
        bias_qv = small[:, 6 * shard : 8 * shard].reshape(2, n, w)
        bias_qv = lax.dynamic_index_in_dim(bias_qv, c, 1, keepdims=False)
        bias_up = small[:, 8 * shard :].reshape(nz, n, fb)
        bias_up = lax.dynamic_index_in_dim(bias_up, c, 1, keepdims=False).reshape(1, fl)
        wq = lax.dynamic_index_in_dim(w_qkv.reshape(shard, 3, n, w), c, 2, keepdims=False).reshape(shard, 3 * w)
        wq = lax.all_gather(wq, SHARDS, axis=0, tiled=True)
        wu = lax.dynamic_index_in_dim(w_up.reshape(shard, nz, n, fb), c, 2, keepdims=False).reshape(shard, fl)
        wu = lax.all_gather(wu, SHARDS, axis=0, tiled=True)
        wn = lax.all_gather(lax.dynamic_slice_in_dim(w_down, c * fb, fb, 0), SHARDS, axis=0, tiled=True)
        wd = lax.all_gather(w_dense, SHARDS, axis=0, tiled=True)

    h1, q, k, v = ln_qkv(x_slots, vectors[0:1], vectors[1:2], wq, bias_qv, rows)
    o, lse = attn_fwd(sc, slopes, q, k, v, rows, hp, 0, n)
    o_own = lax.all_to_all(o.reshape(n, rows, w), ROW, split_axis=0, concat_axis=0, tiled=True)
    y1, h2 = dense_ln(hidden_in, o_own, wd, vectors)

    h2_slots = gather_slots(h2, n)
    early = n - 2
    cot_all, dz = dz_blocks(cot_slots, wn, rows)
    alls, gb_up, dh2_slots = (), [], []
    for first, last in ((0, 2), (2, early), (early, n)):
        alls, gb, dh = mlp(h2_slots[first:last], dz, wu, bias_up, rows, n, first, alls)
        gb_up.append(gb)
        dh2_slots += dh
    h2_all, act, du = alls
    dh2_parts = scatter_slots(dh2_slots, n)
    dy, dyb, do, sums2 = ln2_back(dh2_parts, y1, cotangent, wd, vectors, n)
    do_heads = lax.all_to_all(do, ROW, split_axis=0, concat_axis=0, tiled=True).reshape(seq_len, w)

    g, gb_qv = attn_bwd(sc, slopes, q, k, v, do_heads, o, lse, rows, hp)
    dh1_far = to_slots(g, wq, rows, early, n - early, True)
    dh1_slots = [*to_slots(g, wq, rows, 0, early, True), *dh1_far]
    dh1_parts = scatter_slots(dh1_slots, n)
    grad_input = ln1_back(dh1_parts, hidden_in, dy, vectors)

    onto = grad_dense(at, sc, o_own, dyb, n, nz) if fast else ()
    out_parts = scatter_slots(to_slots(act, wn, rows, 0, n, False, onto), n)
    block_out = finish_out(out_parts, y1, vectors)

    if fast:
        parts = grad_blocks(z.reshape(1), act, cot_all, nz, 1, 0)
        parts = grad_blocks(z.reshape(1), h2_all, du, nz, 2, 1, parts)
        g_ff = over_shards(parts, nz)
        small = small_grads(c.reshape(1), sums2, gb_qv, gb_up, n, nz)
        g_qkv = over_shards(grad_qkv(z.reshape(1), h1, g, small, wq, vectors, nz), nz)
        rest = shard // n
        dense = [add16(*[part[rows + i * rest : rows + (i + 1) * rest] for part in out_parts]) for i in range(nz)]
        dense = over_shards(dense, nz).reshape(rest, n, w).transpose(1, 0, 2).reshape(n * rest, w)
        qkv_slots = gather_slots(jnp.concatenate([g_qkv, dense], axis=0), n)
        half = shard // 2
        ff_slots = gather_slots(g_ff, n)
        blocks_of = [
            [(0, 0, fb, dim, 0, 0, True)],
            [
                (fb, side * fl + t * fb, half, fb, side * half, t * n * fb, False)
                for side in range(2)
                for t in range(nz)
            ],
        ]
        shapes_of = [(n * fb, dim), (shard, ff)]
        so_far = spread(sc, n, 0, ff_slots[:6], blocks_of, shapes_of)
        g_down, g_up = spread(sc, n, 6, ff_slots[6:], blocks_of, shapes_of, so_far)
        lengths = [shard] * 6 + [2 * shard, 4 * shard]
        base = 3 * shard + sum(lengths) // LANES
        blocks_of = [
            [(i * shard, 0, shard, w, 0, i * dim, False) for i in range(3)],
            [(base + e * rest, 0, rest, w, 0, e * w, True) for e in range(n)],
        ]
        shapes_of = [(shard, 3 * dim), (shard, dim)]
        so_far = spread(sc, n, 0, qkv_slots[:6], blocks_of, shapes_of)
        g_qkv, g_dense, *total = spread(
            sc, n, 6, qkv_slots[6:], blocks_of, shapes_of, so_far, lengths, 3 * shard, qkv_slots[:6]
        )
    else:
        reduce = lambda a: lax.psum(
            lax.psum_scatter(a.astype(bf16), SHARDS, scatter_dimension=0, tiled=True), ROW
        ).astype(f32)
        every = lambda a, axis: lax.all_gather(
            lax.psum_scatter(a.astype(bf16), SHARDS, scatter_dimension=0, tiled=True), ROW, axis=axis, tiled=True
        ).astype(f32)
        g_down = every(dot_tn(act, cot_all), 0)
        g_up = dot_tn(h2_all, du).reshape(dim, nz, fb)
        g_up = every(g_up, 2).reshape(shard, ff)
        g_dense = reduce(dot_tn(o_own.transpose(1, 0, 2).reshape(rows, dim), dyb))
        g_qkv = every(dot_tn(h1, g).reshape(dim, 3, w), 2).reshape(shard, 3 * dim)
        dh1 = dot_nt(g, wq)
        normed = jnp.concatenate([normalize(x.astype(f32))[0] for x in x_slots], axis=0)
        sums1 = jnp.concatenate([rowsum(dh1 * normed), rowsum(dh1)], axis=0)
        own = lambda a, lead: lax.dynamic_update_index_in_dim(jnp.zeros((lead, n, a.shape[-1]), f32), a, c, 1)
        by_shard = lambda a: a.reshape(-1, nz, shard).transpose(1, 0, 2).reshape(nz, -1)
        flat = jnp.concatenate(
            [
                by_shard(sums1),
                by_shard(sums2),
                own(gb_qv[:2], 2).reshape(nz, 2 * shard),
                own(sum(gb_up).reshape(nz, fb), nz).reshape(nz, n * fb),
            ],
            axis=1,
        )
        total = lax.dynamic_index_in_dim(lax.psum(flat, both), z, 0, keepdims=False)
        total = [total[i * shard : (i + 1) * shard] for i in range(6)] + [total[6 * shard : 8 * shard], total[8 * shard :]]
    return (
        block_out,
        grad_input,
        total[0],
        total[1],
        g_qkv,
        total[6],
        g_dense,
        total[2],
        total[3],
        total[4],
        g_up,
        total[7],
        g_down,
        total[5],
    )


def solution(mesh):
    n, nz = mesh.shape[ROW], mesh.shape[SHARDS]
    fast = n == 8 and nz == 4
    shard = P(SHARDS)
    mat = P(SHARDS, None)
    tokens = P((SHARDS, ROW), None)
    return jax.shard_map(
        functools.partial(layer, n=n, nz=nz, fast=fast),
        mesh=mesh,
        in_specs=(tokens, mat, shard, shard, mat, shard, mat, shard, shard, shard, mat, shard, mat, shard, tokens),
        out_specs=(tokens, tokens, shard, shard, mat, shard, mat, shard, shard, shard, mat, shard, mat, shard),
        check_vma=False,
    )
```
